32 devices in a mesh: fsdp: 8 (over z, x), tensor: 4 (over y, core).
Axes of the slice: x: 2, y: 2, z: 4, core: 2. Of those that a mesh axis runs over, the one named last changes fastest.
Arguments:
- frames_in: bfloat16 [16, 1500, 768], P('fsdp'), may hold values from -6 to 6
- cotangent: bfloat16 [16, 1500, 768], P('fsdp'), may hold values from -6 to 6
- ln_first: bfloat16 [2, 768], P(None, 'fsdp'), may hold values from 0.25 to 1.75
- w_qkv: bfloat16 [768, 3, 768], P('fsdp', None, 'tensor'), may hold values from -0.21875 to 0.21875
- b_qv: bfloat16 [2, 768], P(None, ('tensor', 'fsdp')), may hold values from -3 to 3
- w_out: bfloat16 [768, 768], P('tensor', 'fsdp'), may hold values from -0.875 to 0.875
- b_out: bfloat16 [768], P('fsdp'), may hold values from -3 to 3
- ln_second: bfloat16 [2, 768], P(None, 'fsdp'), may hold values from 0.25 to 1.75
- w_fc1: bfloat16 [768, 3072], P('fsdp', 'tensor'), may hold values from -0.21875 to 0.21875
- b_fc1: bfloat16 [3072], P(('tensor', 'fsdp')), may hold values from -3 to 3
- w_fc2: bfloat16 [3072, 768], P('tensor', 'fsdp'), may hold values from -0.109375 to 0.109375
- b_fc2: bfloat16 [768], P('fsdp'), may hold values from -3 to 3
Outputs:
- frames_out: bfloat16 [16, 1500, 768], P('fsdp')
- grad_frames: float32 [16, 1500, 768], P('fsdp')
- grad_ln_first: float32 [2, 768], P(None, 'fsdp')
- grad_w_qkv: float32 [768, 3, 768], P('fsdp', None, 'tensor')
- grad_b_qv: float32 [2, 768], P(None, ('tensor', 'fsdp'))
- grad_w_out: float32 [768, 768], P('tensor', 'fsdp')
- grad_b_out: float32 [768], P('fsdp')
- grad_ln_second: float32 [2, 768], P(None, 'fsdp')
- grad_w_fc1: float32 [768, 3072], P('fsdp', 'tensor')
- grad_b_fc1: float32 [3072], P(('tensor', 'fsdp'))
- grad_w_fc2: float32 [3072, 768], P('tensor', 'fsdp')
- grad_b_fc2: float32 [768], P('fsdp')
The draws below stay inside these ranges and needn't reach their ends.
All inputs are finite; a program needn't handle non-finite values.
Results may differ from the reference program's by a relative error of at most 0.022.
Values may be sent and summed in bfloat16 or wider, within the bound.
No kernel may reach another device: no remote copies, remote signals or barrier semaphores. Data moves between devices by JAX's collectives and lax.ppermute only.
A program may use at most 320 MiB of HBM per device.

```python
import jax
import jax.numpy as jnp
from jax import lax

D = 768
HEADS = 12
HEAD_DIM = 64
FF = 3072
FRAMES = 1500
ALL_CLIPS = 16
N_TENSOR = 4


def block_levels(rng, dims, cuts, smallest, high):
    loudness = 1.0
    for dim, shards_of in cuts:
        heights = jax.random.uniform(jax.random.fold_in(jax.random.fold_in(rng, 6), dim), (shards_of,), jnp.float32, smallest / len(cuts), high / len(cuts))
        loudness = loudness * jnp.repeat(jnp.exp(heights), dims[dim] // shards_of).reshape((-1,) + (1,) * (len(dims) - 1 - dim))
    return loudness


def bell_draw(key, dims, deviation, bound, cuts=(), dtype=jnp.bfloat16):
    entries = deviation * jax.random.normal(key, dims, jnp.float32)
    if cuts:
        entries = entries * block_levels(key, dims, cuts, -0.22, 0.18)
    return jnp.clip(entries, -bound, bound).astype(dtype)


def setup_inputs(seed: int = 0) -> dict:
    keys = jax.random.split(jax.random.key(seed), 13)
    frames_in = bell_draw(keys[0], (ALL_CLIPS, FRAMES, D), 1.0, 6.0, ((0, 8),))
    cotangent = bell_draw(keys[1], (ALL_CLIPS, FRAMES, D), 1.0, 6.0, ((0, 8),))
    ln_first = jnp.clip(1.0 + 0.15 * jax.random.normal(keys[2], (2, D), jnp.float32), 0.25, 1.75).astype(jnp.bfloat16)
    w_qkv = bell_draw(keys[3], (D, 3, D), D ** -0.5, 0.21875, ((0, 8), (2, 4)))
    b_qv = bell_draw(keys[4], (2, D), 0.5, 3.0, ((1, 32),))
    w_out = bell_draw(keys[5], (D, D), (D // 16) ** -0.5, 0.875, ((0, 4), (1, 8)))
    b_out = bell_draw(keys[6], (D,), 0.5, 3.0, ((0, 8),))
    ln_second = jnp.clip(1.0 + 0.15 * jax.random.normal(keys[7], (2, D), jnp.float32), 0.25, 1.75).astype(jnp.bfloat16)
    w_fc1 = bell_draw(keys[8], (D, FF), D ** -0.5, 0.21875, ((0, 8), (1, 4)))
    b_fc1 = bell_draw(keys[9], (FF,), 0.5, 3.0, ((0, 32),))
    w_fc2 = bell_draw(keys[10], (FF, D), FF ** -0.5, 0.109375, ((0, 4), (1, 8)))
    b_fc2 = bell_draw(keys[11], (D,), 0.5, 3.0, ((0, 8),))
    return dict(frames_in=frames_in, cotangent=cotangent, ln_first=ln_first, w_qkv=w_qkv, b_qv=b_qv, w_out=w_out, b_out=b_out, ln_second=ln_second, w_fc1=w_fc1, b_fc1=b_fc1, w_fc2=w_fc2, b_fc2=b_fc2)


EPSILON = 1e-05

def layer_norm(values, norm_gain, norm_shift):
    centre = lax.optimization_barrier(jnp.mean(values, axis=-1, keepdims=True))
    centred = values - centre
    inverse = lax.rsqrt(lax.optimization_barrier(jnp.mean(centred * centred, axis=-1, keepdims=True)) + EPSILON)
    normed = centred * inverse
    return (normed * norm_gain + norm_shift, normed, inverse)

def norm_back(grad_out, normed, inverse, norm_gain):
    scaled = grad_out * norm_gain
    return inverse * (scaled - lax.optimization_barrier(jnp.mean(scaled, axis=-1, keepdims=True)) - normed * lax.optimization_barrier(jnp.mean(scaled * normed, axis=-1, keepdims=True)))

def gelu_value(pre_act):
    return 0.5 * pre_act * (1.0 + lax.erf(pre_act * 0.7071067811865476))

def gelu_slope(pre_act):
    return 0.5 * (1.0 + lax.erf(pre_act * 0.7071067811865476)) + pre_act * jnp.exp(-0.5 * pre_act * pre_act) * 0.3989422804014327

def grouped_sum(terms):
    rounded = lax.optimization_barrier(terms.astype(jnp.bfloat16))
    return lax.optimization_barrier(jnp.sum(rounded.astype(jnp.float32), axis=0))

def attend(queries, keys_in, values_in):
    scores = jnp.einsum('qhe,khe->hqk', queries.astype(jnp.float32), keys_in.astype(jnp.float32)) * HEAD_DIM ** (-0.5)
    highest = lax.optimization_barrier(jnp.max(scores, axis=-1, keepdims=True))
    log_total = highest + jnp.log(lax.optimization_barrier(jnp.sum(jnp.exp(scores - highest), axis=-1, keepdims=True)))
    weights = jnp.exp(scores - log_total).astype(jnp.bfloat16)
    blended = jnp.einsum('hqk,khe->qhe', weights.astype(jnp.float32), values_in.astype(jnp.float32))
    return (blended, log_total)

def attend_back(queries, keys_in, values_in, log_total, grad_out):
    score_scale = HEAD_DIM ** (-0.5)
    scores = jnp.einsum('qhe,khe->hqk', queries.astype(jnp.float32), keys_in.astype(jnp.float32)) * score_scale
    chances = jnp.exp(scores - log_total)
    grad_weights = jnp.einsum('qhe,khe->hqk', grad_out.astype(jnp.float32), values_in.astype(jnp.float32))
    centre = lax.optimization_barrier(jnp.sum(chances * grad_weights, axis=-1, keepdims=True))
    grad_scores = (chances * (grad_weights - centre) * score_scale).astype(jnp.bfloat16).astype(jnp.float32)
    grad_query = jnp.einsum('hqk,khe->qhe', grad_scores, keys_in.astype(jnp.float32))
    grad_keys = jnp.einsum('hqk,qhe->khe', grad_scores, queries.astype(jnp.float32))
    grad_values = jnp.einsum('hqk,qhe->khe', chances.astype(jnp.bfloat16).astype(jnp.float32), grad_out.astype(jnp.float32))
    return (grad_query, grad_keys, grad_values)

def reference(frames_in, cotangent, ln_first, w_qkv, b_qv, w_out, b_out, ln_second, w_fc1, b_fc1, w_fc2, b_fc2):
    head_group = D // N_TENSOR
    unit_group = FF // N_TENSOR
    norm_one = ln_first.astype(jnp.float32)
    norm_two = ln_second.astype(jnp.float32)
    qkv_wide = w_qkv.astype(jnp.float32)
    qkv_bias = b_qv.astype(jnp.float32)
    out_wide = w_out.astype(jnp.float32)
    out_bias = b_out.astype(jnp.float32)
    up_wide = w_fc1.astype(jnp.float32)
    up_bias = b_fc1.astype(jnp.float32)
    down_wide = w_fc2.astype(jnp.float32)
    down_bias = b_fc2.astype(jnp.float32)

    def clip_step(totals, inputs):
        frames, grad_in = inputs
        token_rows = frames.astype(jnp.float32)
        first_out, first_normed, first_inverse = layer_norm(token_rows, norm_one[0], norm_one[1])
        first_low = first_out.astype(jnp.bfloat16)
        projected = jnp.einsum('sd,dcf->csf', first_low.astype(jnp.float32), qkv_wide)
        queries = (projected[0] + qkv_bias[0]).astype(jnp.bfloat16).reshape(FRAMES, HEADS, HEAD_DIM)
        keys_low = projected[1].astype(jnp.bfloat16).reshape(FRAMES, HEADS, HEAD_DIM)
        values_low = (projected[2] + qkv_bias[1]).astype(jnp.bfloat16).reshape(FRAMES, HEADS, HEAD_DIM)
        blended, log_total = attend(queries, keys_low, values_low)
        attn_low = blended.reshape(FRAMES, D).astype(jnp.bfloat16)
        attn_terms = jnp.einsum('sgf,gfd->gsd', attn_low.astype(jnp.float32).reshape(FRAMES, N_TENSOR, head_group), out_wide.reshape(N_TENSOR, head_group, D))
        middle = token_rows + grouped_sum(attn_terms) + out_bias
        second_out, second_normed, second_inverse = layer_norm(middle, norm_two[0], norm_two[1])
        second_low = second_out.astype(jnp.bfloat16)
        pre_act = jnp.dot(second_low.astype(jnp.float32), up_wide) + up_bias
        act_low = gelu_value(pre_act).astype(jnp.bfloat16)
        down_terms = jnp.einsum('sgh,ghd->gsd', act_low.astype(jnp.float32).reshape(FRAMES, N_TENSOR, unit_group), down_wide.reshape(N_TENSOR, unit_group, D))
        result = (middle + grouped_sum(down_terms) + down_bias).astype(jnp.bfloat16)
        grad_top = grad_in.astype(jnp.float32)
        grad_down_bias = lax.optimization_barrier(jnp.sum(grad_top, axis=0))
        grad_down = jnp.dot(act_low.astype(jnp.float32).T, grad_top)
        grad_pre = jnp.dot(grad_top, down_wide.T) * gelu_slope(pre_act)
        grad_up_bias = lax.optimization_barrier(jnp.sum(grad_pre, axis=0))
        grad_pre_low = grad_pre.astype(jnp.bfloat16).astype(jnp.float32)
        grad_up = jnp.dot(second_low.astype(jnp.float32).T, grad_pre_low)
        second_terms = jnp.einsum('sgh,dgh->gsd', grad_pre_low.reshape(FRAMES, N_TENSOR, unit_group), up_wide.reshape(D, N_TENSOR, unit_group))
        grad_second = grouped_sum(second_terms)
        grad_norm_two = jnp.stack([lax.optimization_barrier(jnp.sum(grad_second * second_normed, axis=0)), lax.optimization_barrier(jnp.sum(grad_second, axis=0))])
        grad_middle = grad_top + norm_back(grad_second, second_normed, second_inverse, norm_two[0])
        grad_out_bias = lax.optimization_barrier(jnp.sum(grad_middle, axis=0))
        grad_middle_low = grad_middle.astype(jnp.bfloat16).astype(jnp.float32)
        grad_out = jnp.dot(attn_low.astype(jnp.float32).T, grad_middle_low)
        grad_attn = jnp.dot(grad_middle_low, out_wide.T).astype(jnp.bfloat16).reshape(FRAMES, HEADS, HEAD_DIM)
        grad_query, grad_keys, grad_values = attend_back(queries, keys_low, values_low, log_total, grad_attn)
        grad_query = grad_query.reshape(FRAMES, D)
        grad_keys = grad_keys.reshape(FRAMES, D)
        grad_values = grad_values.reshape(FRAMES, D)
        grad_qkv_bias = jnp.stack([lax.optimization_barrier(jnp.sum(grad_query, axis=0)), lax.optimization_barrier(jnp.sum(grad_values, axis=0))])
        stacked = jnp.stack([grad_query, grad_keys, grad_values]).astype(jnp.bfloat16).astype(jnp.float32)
        grad_qkv = jnp.einsum('sd,csf->dcf', first_low.astype(jnp.float32), stacked)
        first_terms = jnp.einsum('csgf,dcgf->gsd', stacked.reshape(3, FRAMES, N_TENSOR, head_group), qkv_wide.reshape(D, 3, N_TENSOR, head_group))
        grad_first = grouped_sum(first_terms)
        grad_norm_one = jnp.stack([lax.optimization_barrier(jnp.sum(grad_first * first_normed, axis=0)), lax.optimization_barrier(jnp.sum(grad_first, axis=0))])
        grad_rows = grad_middle + norm_back(grad_first, first_normed, first_inverse, norm_one[0])
        pieces = (grad_norm_one, grad_qkv, grad_qkv_bias, grad_out, grad_out_bias, grad_norm_two, grad_up, grad_up_bias, grad_down, grad_down_bias)
        totals = tuple((total + piece for total, piece in zip(totals, pieces)))
        return (totals, (result, grad_rows))
    zeros_init = (jnp.zeros((2, D), jnp.float32), jnp.zeros((D, 3, D), jnp.float32), jnp.zeros((2, D), jnp.float32), jnp.zeros((D, D), jnp.float32), jnp.zeros((D,), jnp.float32), jnp.zeros((2, D), jnp.float32), jnp.zeros((D, FF), jnp.float32), jnp.zeros((FF,), jnp.float32), jnp.zeros((FF, D), jnp.float32), jnp.zeros((D,), jnp.float32))
    totals, outputs = lax.scan(clip_step, zeros_init, (frames_in, cotangent))
    frames_out, grad_frames = outputs
    return (frames_out, grad_frames, totals[0], totals[1], totals[2], totals[3], totals[4], totals[5], totals[6], totals[7], totals[8], totals[9])
```

```python
import functools

import jax
import jax.numpy as jnp
from jax import lax
from jax.experimental import pallas as pl
from jax.experimental.pallas import tpu as pltpu
from jax.sharding import PartitionSpec as P

HEAD_DIM = 64
EPSILON = 1e-05
LOW = jnp.bfloat16
WIDE = jnp.float32
NEGATIVE = -1e30
NT = (((1,), (1,)), ((), ()))
TN = (((0,), (0,)), ((), ()))


def layer_norm(values, norm_gain, norm_shift):
    centre = jnp.mean(values, axis=-1, keepdims=True)
    centred = values - centre
    inverse = lax.rsqrt(jnp.mean(centred * centred, axis=-1, keepdims=True) + EPSILON)
    normed = centred * inverse
    return (normed * norm_gain + norm_shift, normed, inverse)


def norm_back(grad_out, normed, inverse, norm_gain):
    scaled = grad_out * norm_gain
    return inverse * (
        scaled
        - jnp.mean(scaled, axis=-1, keepdims=True)
        - normed * jnp.mean(scaled * normed, axis=-1, keepdims=True)
    )


def padded_rows(count):
    return -(-count // 512) * 512


def attend_kernel(q_ref, k_ref, v_ref, o_ref, l_ref, q_all, k_all, v_all, *, block):
    rows = q_ref.shape[0]
    padded = q_all.shape[0]
    fill = jnp.zeros((padded - rows, 128), LOW)
    q_all[...] = jnp.concatenate([q_ref[...] * LOW(HEAD_DIM**-0.5), fill], axis=0)
    k_all[...] = jnp.concatenate([k_ref[...], fill], axis=0)
    v_all[...] = jnp.concatenate([v_ref[...], fill], axis=0)
    valid = lax.broadcasted_iota(jnp.int32, (block, 256), 1) < rows - (padded - 256)
    upper = lax.broadcasted_iota(jnp.int32, (block, 128), 1) >= HEAD_DIM
    for step in range(padded // block):
        start = step * block
        parts = []
        for head in range(2):
            q_head = jnp.where(upper == (head == 1), q_all[start : start + block, :], LOW(0))
            scores = lax.dot_general(q_head, k_all[...], NT, preferred_element_type=WIDE)
            scores = jnp.concatenate(
                [
                    scores[:, : padded - 256],
                    jnp.where(valid, scores[:, padded - 256 :], NEGATIVE),
                ],
                axis=1,
            )
            highest = jnp.max(scores, axis=1, keepdims=True)
            weights = jnp.exp(scores - highest)
            total = jnp.sum(weights, axis=1, keepdims=True)
            blended = jnp.dot(weights.astype(LOW), v_all[...], preferred_element_type=WIDE)
            parts.append(blended * (1.0 / total))
            log_total = jnp.broadcast_to(highest + jnp.log(total), (block, 128)).T
            l_ref[head, :, start : start + block] = log_total[0:8, :]
        merged = jnp.where(upper, parts[1], parts[0]).astype(LOW)
        count = min(block, rows - start)
        o_ref[start : start + count, :] = merged[:count]


def attend(qkv):
    rows, width = qkv.shape
    pairs = width // 3 // 128
    padded = padded_rows(rows)

    def column(offset):
        return pl.BlockSpec((rows, 128), lambda p: (0, offset + p))

    return pl.pallas_call(
        functools.partial(attend_kernel, block=512),
        grid=(pairs,),
        in_specs=[column(0), column(pairs), column(2 * pairs)],
        out_specs=[column(0), pl.BlockSpec((2, 8, padded), lambda p: (p, 0, 0))],
        out_shape=[
            jax.ShapeDtypeStruct((rows, width // 3), LOW),
            jax.ShapeDtypeStruct((2 * pairs, 8, padded), WIDE),
        ],
        scratch_shapes=[pltpu.VMEM((padded, 128), LOW)] * 3,
        name="attend",
    )(qkv, qkv, qkv)


def attend_back_kernel(
    q_ref, k_ref, v_ref, g_ref, o_ref, l_ref, dq_ref, dk_ref, dv_ref, db_ref,
    q_all, k_all, v_all, g_all, dq_turned, centre_all, *, block,
):
    rows = q_ref.shape[0]
    padded = k_all.shape[0]
    fill = jnp.zeros((padded - rows, 128), LOW)

    def pad(value):
        return jnp.concatenate([value, fill], axis=0)

    upper = lax.broadcasted_iota(jnp.int32, (padded, 128), 1) >= HEAD_DIM
    upper8 = lax.broadcasted_iota(jnp.int32, (8, 128), 1) >= HEAD_DIM
    upper_block = lax.broadcasted_iota(jnp.int32, (block, 128), 1) >= HEAD_DIM
    scale = HEAD_DIM**-0.5
    k_all[...] = pad(k_ref[...])
    v_all[...] = pad(v_ref[...])
    q_full = pad(q_ref[...] * LOW(scale))
    g_full = pad(g_ref[...])
    product = g_full.astype(WIDE) * pad(o_ref[...]).astype(WIDE)
    coarse = product.astype(LOW)
    fine = (product - coarse.astype(WIDE)).astype(LOW)
    for head in range(2):
        mine = upper == (head == 1)
        q_all[head] = jnp.where(mine, q_full, LOW(0))
        g_all[head] = jnp.where(mine, g_full, LOW(0))
        ones = jnp.where(upper8 == (head == 1), 1.0, 0.0).astype(LOW)
        centre_all[head] = lax.dot_general(
            ones, coarse, NT, preferred_element_type=WIDE
        ) + lax.dot_general(ones, fine, NT, preferred_element_type=WIDE)
    dq_turned[...] = jnp.zeros_like(dq_turned)
    value_bias = jnp.zeros((1, 128), WIDE)
    for step in range(padded // block):
        start = step * block
        keys = k_all[start : start + block, :]
        values = v_all[start : start + block, :]
        grad_values = grad_keys = grad_query = None
        for head in range(2):
            scores = lax.dot_general(keys, q_all[head], NT, preferred_element_type=WIDE)
            chances = jnp.exp(scores - l_ref[head, 0:1, :])
            if start + block > rows:
                place = lax.broadcasted_iota(jnp.int32, (block, padded), 0)
                chances = jnp.where(place < rows - start, chances, 0.0)
            grad_weights = lax.dot_general(
                values, g_all[head], NT, preferred_element_type=WIDE
            )
            grad_scores = (chances * (grad_weights - centre_all[head, 0:1, :])).astype(LOW)
            from_values = jnp.dot(
                chances.astype(LOW), g_all[head], preferred_element_type=WIDE
            )
            from_keys = jnp.dot(grad_scores, q_all[head], preferred_element_type=WIDE)
            keys_head = jnp.where(upper_block == (head == 1), keys, LOW(0))
            from_query = jnp.dot(keys_head.T, grad_scores, preferred_element_type=WIDE)
            if head == 0:
                grad_values, grad_keys, grad_query = from_values, from_keys, from_query
            else:
                grad_values = grad_values + from_values
                grad_keys = grad_keys + from_keys
                grad_query = grad_query + from_query
        dq_turned[...] += grad_query
        count = min(block, rows - start)
        value_bias += jnp.sum(grad_values, axis=0, keepdims=True)
        dv_ref[start : start + count, :] = grad_values[:count].astype(LOW)
        dk_ref[start : start + count, :] = grad_keys[:count].astype(LOW)
    grad_query = (dq_turned[...] * scale).T
    dq_ref[...] = grad_query[:rows].astype(LOW)
    db_ref[0, 0:1, :] = jnp.sum(grad_query, axis=0, keepdims=True)
    db_ref[0, 1:2, :] = value_bias


def attend_back(qkv, grad_out, blended, log_total):
    rows, width = qkv.shape
    pairs = width // 3 // 128
    padded = padded_rows(rows)

    def column(offset):
        return pl.BlockSpec((rows, 128), lambda p: (0, offset + p))

    return pl.pallas_call(
        functools.partial(attend_back_kernel, block=512),
        grid=(pairs,),
        in_specs=[
            column(0),
            column(pairs),
            column(2 * pairs),
            column(0),
            column(0),
            pl.BlockSpec((2, 8, padded), lambda p: (p, 0, 0)),
        ],
        out_specs=[column(0)] * 3 + [pl.BlockSpec((1, 8, 128), lambda p: (p, 0, 0))],
        out_shape=[jax.ShapeDtypeStruct((rows, width // 3), LOW)] * 3
        + [jax.ShapeDtypeStruct((pairs, 8, 128), WIDE)],
        scratch_shapes=[
            pltpu.VMEM((2, padded, 128), LOW),
            pltpu.VMEM((padded, 128), LOW),
            pltpu.VMEM((padded, 128), LOW),
            pltpu.VMEM((2, padded, 128), LOW),
            pltpu.VMEM((128, padded), WIDE),
            pltpu.VMEM((2, 8, padded), WIDE),
        ],
        name="attend_back",
    )(qkv, qkv, qkv, grad_out, blended, log_total)


def swap_tensor(value, distance):
    size = lax.axis_size("tensor")
    return lax.ppermute(value, "tensor", [(i, i ^ distance) for i in range(size)])


def swap_fsdp(value, distance):
    size = lax.axis_size("fsdp")
    return lax.ppermute(value, "fsdp", [(i, i ^ distance) for i in range(size)])


def spread(piece, y_last):
    size = lax.axis_size("fsdp")
    held = {(0, 0): piece}
    for far in range(2, size, 2):
        held[(0, far)] = swap_fsdp(piece, far)
    for stage in ("x", "y") if y_last else ("y", "x"):
        if stage == "x":
            held.update({(y, f ^ 1): swap_fsdp(v, 1) for (y, f), v in held.items()})
        else:
            held.update({(1, f): swap_tensor(v, 2) for (y, f), v in held.items()})
    return held


def place_kernel(*refs, keys, rows):
    pieces, out, sems = refs[: len(keys)], refs[len(keys)], refs[len(keys) + 1]
    mine = lax.axis_index("fsdp")
    group = lax.axis_index("tensor") // 2
    copies = []
    for i, (y, f) in enumerate(keys):
        copy = pltpu.make_async_copy(pieces[i], out.at[group ^ y, mine ^ f], sems.at[i])
        copy.start()
        copies.append(copy)
    for copy in copies:
        copy.wait()


def place(held):
    keys = tuple(sorted(held))
    rows, columns = held[keys[0]].shape
    size = lax.axis_size("fsdp")
    hbm = pl.BlockSpec(memory_space=pl.ANY)
    return pl.pallas_call(
        functools.partial(place_kernel, keys=keys, rows=rows),
        in_specs=[hbm] * len(keys),
        out_specs=hbm,
        out_shape=jax.ShapeDtypeStruct((2, size, rows, columns), held[keys[0]].dtype),
        scratch_shapes=[pltpu.SemaphoreType.DMA((len(keys),))],
        name="place",
    )(*[held[k] for k in keys])


def pick(value, axis, index):
    return lax.dynamic_index_in_dim(value, index, axis, keepdims=False)


def collect(grads, y_first):
    size = lax.axis_size("fsdp")
    mine = lax.axis_index("fsdp")
    group = lax.axis_index("tensor") // 2
    rows, columns = grads.shape[2:]
    half = size // 2
    low, high = mine % 2, mine // 2

    def add(a, b):
        return (a.astype(WIDE) + b.astype(WIDE)).astype(LOW)

    if y_first:
        got = swap_tensor(pick(grads, 0, 1 - group), 2)
        grads = add(pick(grads, 0, group), got).reshape(half, 2, rows, columns)
        got = swap_fsdp(pick(grads, 1, 1 - low), 1)
        grads = add(pick(grads, 1, low), got)
    else:
        grads = grads.reshape(2, half, 2, rows, columns)
        got = swap_fsdp(pick(grads, 2, 1 - low), 1)
        grads = add(pick(grads, 2, low), got)
        got = swap_tensor(pick(grads, 0, 1 - group), 2)
        grads = add(pick(grads, 0, group), got)
    total = pick(grads, 0, high).astype(WIDE)
    for far in range(1, half):
        total = total + swap_fsdp(pick(grads, 0, high ^ far), 2 * far).astype(WIDE)
    return total


def pair_sum(value):
    low = value.astype(LOW)
    return low.astype(WIDE) + swap_tensor(low, 1).astype(WIDE)


def both_clips(low):
    core = lax.axis_index("tensor") % 2
    group = lax.axis_index("tensor") // 2
    half = low.shape[1] // 2
    mine = lax.dynamic_slice_in_dim(low, core * half, half, axis=1)
    direct = swap_tensor(mine, 2)
    across = swap_tensor(direct, 1)
    first = jnp.where(core == 0, direct, across)
    second = jnp.where(core == 0, across, direct)
    other = jnp.concatenate([first, second], axis=1)
    return jnp.stack([jnp.where(group == 0, low, other), jnp.where(group == 0, other, low)])


def local(
    frames_in, cotangent, ln_first, w_qkv, b_qv, w_out, b_out, ln_second, w_fc1, b_fc1, w_fc2, b_fc2
):
    clip_count, frame_count, model_width = frames_in.shape
    size = lax.axis_size("fsdp")
    part = w_qkv.shape[0]
    head_width = w_qkv.shape[2]
    unit_width = w_fc1.shape[1]
    tensor_index = lax.axis_index("tensor")
    group = tensor_index // 2
    mine = lax.axis_index("fsdp")

    bias_part = b_qv.shape[1]
    small = jnp.concatenate(
        [
            ln_first,
            ln_second,
            b_out[None],
            b_fc2[None],
            b_fc1[None],
            jnp.pad(b_qv.reshape(1, -1), ((0, 0), (0, part - 2 * bias_part))),
        ],
        axis=0,
    )
    small = jnp.pad(small, ((0, 0), (0, 3 * head_width - part)))
    attn_piece = jnp.concatenate([w_qkv.reshape(part, 3 * head_width), small], axis=0)
    attn_held = spread(attn_piece, True)
    out_held = spread(w_out.T, False)
    up_held = spread(w_fc1, False)
    down_held = spread(w_fc2.T, True)

    attn_all = place(attn_held)
    small_all = attn_all[:, :, part:, :part]
    rows_of = [small_all[0, :, i, :].reshape(1, model_width).astype(WIDE) for i in range(6)]
    gain_one, shift_one, gain_two, shift_two, out_bias, down_bias = rows_of
    up_bias = small_all[:, :, 6, :].reshape(1, 2 * unit_width).astype(WIDE)
    bias_all = small_all[:, :, 7, : 2 * bias_part].reshape(2, size, 2, bias_part)
    bias_all = bias_all.transpose(2, 0, 1, 3).reshape(2, 2 * head_width)
    qkv_bias = jnp.concatenate(
        [bias_all[0], jnp.zeros((2 * head_width,), LOW), bias_all[1]]
    ).astype(WIDE)
    qkv_full = attn_all[:, :, :part, :].reshape(2, model_width, 3, head_width)
    qkv_full = qkv_full.transpose(1, 2, 0, 3).reshape(model_width, 6 * head_width)

    frames_low = lax.dynamic_index_in_dim(frames_in, group, 0, keepdims=False)
    grad_low = lax.dynamic_index_in_dim(cotangent, group, 0, keepdims=False)
    token_rows = frames_low.astype(WIDE)
    first_out, first_normed, first_inverse = layer_norm(token_rows, gain_one, shift_one)
    first_low = first_out.astype(LOW)
    qkv = (jnp.dot(first_low, qkv_full, preferred_element_type=WIDE) + qkv_bias).astype(LOW)
    attn_low, log_total = attend(qkv)

    out_all = place(out_held).reshape(2, model_width, head_width)
    out_full = out_all.transpose(1, 0, 2).reshape(model_width, 2 * head_width)
    attn_terms = lax.dot_general(attn_low, out_full, NT, preferred_element_type=WIDE)
    middle = token_rows + pair_sum(attn_terms) + out_bias
    second_out, second_normed, second_inverse = layer_norm(middle, gain_two, shift_two)
    second_low = second_out.astype(LOW)

    up_all = place(up_held).reshape(2, model_width, unit_width)
    down_all = place(down_held).reshape(2, model_width, unit_width)
    acts, slopes, grads_pre = [], [], []
    down_terms = second_terms = None
    grad_up_bias = []
    for i in range(2):
        pre_act = jnp.dot(second_low, up_all[i], preferred_element_type=WIDE)
        pre_act = pre_act + up_bias[:, i * unit_width : (i + 1) * unit_width]
        below = 0.5 * (1.0 + lax.erf(pre_act * 0.7071067811865476))
        acts.append((pre_act * below).astype(LOW))
        slope = below + pre_act * jnp.exp(-0.5 * pre_act * pre_act) * 0.3989422804014327
        grad_pre = jnp.dot(grad_low, down_all[i], preferred_element_type=WIDE) * slope
        grad_up_bias.append(jnp.sum(grad_pre, axis=0))
        grads_pre.append(grad_pre.astype(LOW))
    second_terms = sum(
        lax.dot_general(grads_pre[i], up_all[i], NT, preferred_element_type=WIDE) for i in range(2)
    )
    grad_second = pair_sum(second_terms)
    down_terms = sum(
        lax.dot_general(acts[i], down_all[i], NT, preferred_element_type=WIDE) for i in range(2)
    )
    result = (middle + pair_sum(down_terms) + down_bias).astype(LOW)
    frames_out = both_clips(result)

    grad_top = grad_low.astype(WIDE)
    grad_down_bias = jnp.sum(grad_top, axis=0)
    grad_down = jnp.stack(
        [lax.dot_general(grad_low, acts[i], TN, preferred_element_type=WIDE) for i in range(2)]
    )
    grad_up = jnp.stack(
        [
            lax.dot_general(second_low, grads_pre[i], TN, preferred_element_type=WIDE)
            for i in range(2)
        ]
    )
    grad_down = collect(
        grad_down.astype(LOW).reshape(2, size, part, unit_width), False
    ).T
    grad_up = collect(grad_up.astype(LOW).reshape(2, size, part, unit_width), True)

    grad_norm_two = [jnp.sum(grad_second * second_normed, axis=0), jnp.sum(grad_second, axis=0)]
    grad_middle = grad_top + norm_back(grad_second, second_normed, second_inverse, gain_two)
    grad_out_bias = jnp.sum(grad_middle, axis=0)
    grad_middle_low = grad_middle.astype(LOW)
    grad_attn = jnp.dot(grad_middle_low, out_full, preferred_element_type=WIDE).astype(LOW)
    grad_out = lax.dot_general(grad_middle_low, attn_low, TN, preferred_element_type=WIDE)
    grad_out = grad_out.astype(LOW).reshape(model_width, 2, head_width).transpose(1, 0, 2)
    grad_out = collect(grad_out.reshape(2, size, part, head_width), False).T

    grad_query, grad_keys, grad_values, bias_sums = attend_back(qkv, grad_attn, attn_low, log_total)
    stacked = jnp.concatenate([grad_query, grad_keys, grad_values], axis=1)
    first_terms = lax.dot_general(stacked, qkv_full, NT, preferred_element_type=WIDE)
    grad_first = pair_sum(first_terms)
    grad_rows = grad_middle + norm_back(grad_first, first_normed, first_inverse, gain_one)
    grad_frames = both_clips(grad_rows.astype(LOW)).astype(WIDE)

    grad_qkv = lax.dot_general(first_low, stacked, TN, preferred_element_type=WIDE).astype(LOW)
    grad_qkv = grad_qkv.reshape(model_width, 3, 2, head_width).transpose(2, 0, 1, 3)
    grad_qkv = collect(grad_qkv.reshape(2, size, part, 3 * head_width), False)
    grad_qkv = grad_qkv.reshape(part, 3, head_width)

    grad_norm_one = [jnp.sum(grad_first * first_normed, axis=0), jnp.sum(grad_first, axis=0)]
    shared = jnp.stack(grad_norm_one + grad_norm_two + [grad_out_bias, grad_down_bias])
    shared = shared.reshape(1, 6, size, part).transpose(0, 2, 1, 3)
    shared = jnp.broadcast_to(shared, (2, size, 6, part))
    unit_bias = jnp.stack(grad_up_bias).reshape(2, size, 1, part)
    sums = bias_sums[:, :2, :].transpose(1, 0, 2).reshape(2, 2, size, bias_part)
    sums = sums.transpose(1, 2, 0, 3).reshape(2, size, 1, 2 * bias_part)
    sums = jnp.pad(sums, ((0, 0), (0, 0), (0, 0), (0, part - 2 * bias_part)))
    small_grads = jnp.concatenate([shared, unit_bias, sums], axis=2)
    small_grads = collect(small_grads.astype(LOW), True)

    return (
        frames_out,
        grad_frames,
        small_grads[0:2],
        grad_qkv,
        small_grads[7, : 2 * bias_part].reshape(2, bias_part),
        grad_out,
        small_grads[4],
        small_grads[2:4],
        grad_up,
        small_grads[6],
        grad_down,
        small_grads[5],
    )


def solution(mesh):
    in_specs = (
        P("fsdp", None, None),
        P("fsdp", None, None),
        P(None, "fsdp"),
        P("fsdp", None, "tensor"),
        P(None, ("tensor", "fsdp")),
        P("tensor", "fsdp"),
        P("fsdp"),
        P(None, "fsdp"),
        P("fsdp", "tensor"),
        P(("tensor", "fsdp")),
        P("tensor", "fsdp"),
        P("fsdp"),
    )
    out_specs = (
        P("fsdp", None, None),
        P("fsdp", None, None),
        P(None, "fsdp"),
        P("fsdp", None, "tensor"),
        P(None, ("tensor", "fsdp")),
        P("tensor", "fsdp"),
        P("fsdp"),
        P(None, "fsdp"),
        P("fsdp", "tensor"),
        P(("tensor", "fsdp")),
        P("tensor", "fsdp"),
        P("fsdp"),
    )
    return jax.shard_map(local, mesh=mesh, in_specs=in_specs, out_specs=out_specs, check_vma=False)
```

```python
import functools

import jax
import jax.numpy as jnp
from jax import lax
from jax.experimental import pallas as pl
from jax.experimental.pallas import tpu as pltpu
from jax.sharding import PartitionSpec as P

HEAD_DIM = 64
EPSILON = 1e-05
LOW = jnp.bfloat16
WIDE = jnp.float32
NEGATIVE = -1e30
NT = (((1,), (1,)), ((), ()))
TN = (((0,), (0,)), ((), ()))


def layer_norm(values, norm_gain, norm_shift):
    centre = jnp.mean(values, axis=-1, keepdims=True)
    centred = values - centre
    inverse = lax.rsqrt(jnp.mean(centred * centred, axis=-1, keepdims=True) + EPSILON)
    normed = centred * inverse
    return (normed * norm_gain + norm_shift, normed, inverse)


def norm_back(grad_out, normed, inverse, norm_gain):
    scaled = grad_out * norm_gain
    return inverse * (
        scaled
        - jnp.mean(scaled, axis=-1, keepdims=True)
        - normed * jnp.mean(scaled * normed, axis=-1, keepdims=True)
    )


def padded_rows(count):
    return -(-count // 512) * 512


def attend_kernel(q_ref, k_ref, v_ref, o_ref, l_ref, q_all, k_all, v_all, *, block):
    rows = q_ref.shape[0]
    padded = q_all.shape[0]
    fill = jnp.zeros((padded - rows, 128), LOW)
    q_all[...] = jnp.concatenate([q_ref[...] * LOW(HEAD_DIM**-0.5), fill], axis=0)
    k_all[...] = jnp.concatenate([k_ref[...], fill], axis=0)
    v_all[...] = jnp.concatenate([v_ref[...], fill], axis=0)
    valid = lax.broadcasted_iota(jnp.int32, (block, 256), 1) < rows - (padded - 256)
    upper = lax.broadcasted_iota(jnp.int32, (block, 128), 1) >= HEAD_DIM
    for step in range(padded // block):
        start = step * block
        parts = []
        for head in range(2):
            q_head = jnp.where(upper == (head == 1), q_all[start : start + block, :], LOW(0))
            scores = lax.dot_general(q_head, k_all[...], NT, preferred_element_type=WIDE)
            scores = jnp.concatenate(
                [
                    scores[:, : padded - 256],
                    jnp.where(valid, scores[:, padded - 256 :], NEGATIVE),
                ],
                axis=1,
            )
            highest = jnp.max(scores, axis=1, keepdims=True)
            weights = jnp.exp(scores - highest)
            total = jnp.sum(weights, axis=1, keepdims=True)
            blended = jnp.dot(weights.astype(LOW), v_all[...], preferred_element_type=WIDE)
            parts.append(blended * (1.0 / total))
            log_total = jnp.broadcast_to(highest + jnp.log(total), (block, 128)).T
            l_ref[head, :, start : start + block] = log_total[0:8, :]
        merged = jnp.where(upper, parts[1], parts[0]).astype(LOW)
        count = min(block, rows - start)
        o_ref[start : start + count, :] = merged[:count]


def attend(qkv):
    rows, width = qkv.shape
    pairs = width // 3 // 128
    padded = padded_rows(rows)

    def column(offset):
        return pl.BlockSpec((rows, 128), lambda p: (0, offset + p))

    return pl.pallas_call(
        functools.partial(attend_kernel, block=512),
        grid=(pairs,),
        in_specs=[column(0), column(pairs), column(2 * pairs)],
        out_specs=[column(0), pl.BlockSpec((2, 8, padded), lambda p: (p, 0, 0))],
        out_shape=[
            jax.ShapeDtypeStruct((rows, width // 3), LOW),
            jax.ShapeDtypeStruct((2 * pairs, 8, padded), WIDE),
        ],
        scratch_shapes=[pltpu.VMEM((padded, 128), LOW)] * 3,
        name="attend",
    )(qkv, qkv, qkv)


def attend_back_kernel(
    q_ref, k_ref, v_ref, g_ref, o_ref, l_ref, dq_ref, dk_ref, dv_ref, db_ref,
    q_all, k_all, v_all, g_all, dq_turned, centre_all, *, block,
):
    rows = q_ref.shape[0]
    padded = k_all.shape[0]
    fill = jnp.zeros((padded - rows, 128), LOW)

    def pad(value):
        return jnp.concatenate([value, fill], axis=0)

    upper = lax.broadcasted_iota(jnp.int32, (padded, 128), 1) >= HEAD_DIM
    upper8 = lax.broadcasted_iota(jnp.int32, (8, 128), 1) >= HEAD_DIM
    upper_block = lax.broadcasted_iota(jnp.int32, (block, 128), 1) >= HEAD_DIM
    scale = HEAD_DIM**-0.5
    k_all[...] = pad(k_ref[...])
    v_all[...] = pad(v_ref[...])
    q_full = pad(q_ref[...] * LOW(scale))
    g_full = pad(g_ref[...])
    product = g_full.astype(WIDE) * pad(o_ref[...]).astype(WIDE)
    coarse = product.astype(LOW)
    fine = (product - coarse.astype(WIDE)).astype(LOW)
    for head in range(2):
        mine = upper == (head == 1)
        q_all[head] = jnp.where(mine, q_full, LOW(0))
        g_all[head] = jnp.where(mine, g_full, LOW(0))
        ones = jnp.where(upper8 == (head == 1), 1.0, 0.0).astype(LOW)
        centre_all[head] = lax.dot_general(
            ones, coarse, NT, preferred_element_type=WIDE
        ) + lax.dot_general(ones, fine, NT, preferred_element_type=WIDE)
    dq_turned[...] = jnp.zeros_like(dq_turned)
    value_bias = jnp.zeros((1, 128), WIDE)
    for step in range(padded // block):
        start = step * block
        keys = k_all[start : start + block, :]
        values = v_all[start : start + block, :]
        grad_values = grad_keys = grad_query = None
        for head in range(2):
            scores = lax.dot_general(keys, q_all[head], NT, preferred_element_type=WIDE)
            chances = jnp.exp(scores - l_ref[head, 0:1, :])
            if start + block > rows:
                place = lax.broadcasted_iota(jnp.int32, (block, padded), 0)
                chances = jnp.where(place < rows - start, chances, 0.0)
            grad_weights = lax.dot_general(
                values, g_all[head], NT, preferred_element_type=WIDE
            )
            grad_scores = (chances * (grad_weights - centre_all[head, 0:1, :])).astype(LOW)
            from_values = jnp.dot(
                chances.astype(LOW), g_all[head], preferred_element_type=WIDE
            )
            from_keys = jnp.dot(grad_scores, q_all[head], preferred_element_type=WIDE)
            keys_head = jnp.where(upper_block == (head == 1), keys, LOW(0))
            from_query = jnp.dot(keys_head.T, grad_scores, preferred_element_type=WIDE)
            if head == 0:
                grad_values, grad_keys, grad_query = from_values, from_keys, from_query
            else:
                grad_values = grad_values + from_values
                grad_keys = grad_keys + from_keys
                grad_query = grad_query + from_query
        dq_turned[...] += grad_query
        count = min(block, rows - start)
        value_bias += jnp.sum(grad_values, axis=0, keepdims=True)
        dv_ref[start : start + count, :] = grad_values[:count].astype(LOW)
        dk_ref[start : start + count, :] = grad_keys[:count].astype(LOW)
    grad_query = (dq_turned[...] * scale).T
    dq_ref[...] = grad_query[:rows].astype(LOW)
    db_ref[0, 0:1, :] = jnp.sum(grad_query, axis=0, keepdims=True)
    db_ref[0, 1:2, :] = value_bias


def attend_back(qkv, grad_out, blended, log_total):
    rows, width = qkv.shape
    pairs = width // 3 // 128
    padded = padded_rows(rows)

    def column(offset):
        return pl.BlockSpec((rows, 128), lambda p: (0, offset + p))

    return pl.pallas_call(
        functools.partial(attend_back_kernel, block=512),
        grid=(pairs,),
        in_specs=[
            column(0),
            column(pairs),
            column(2 * pairs),
            column(0),
            column(0),
            pl.BlockSpec((2, 8, padded), lambda p: (p, 0, 0)),
        ],
        out_specs=[column(0)] * 3 + [pl.BlockSpec((1, 8, 128), lambda p: (p, 0, 0))],
        out_shape=[jax.ShapeDtypeStruct((rows, width // 3), LOW)] * 3
        + [jax.ShapeDtypeStruct((pairs, 8, 128), WIDE)],
        scratch_shapes=[
            pltpu.VMEM((2, padded, 128), LOW),
            pltpu.VMEM((padded, 128), LOW),
            pltpu.VMEM((padded, 128), LOW),
            pltpu.VMEM((2, padded, 128), LOW),
            pltpu.VMEM((128, padded), WIDE),
            pltpu.VMEM((2, 8, padded), WIDE),
        ],
        name="attend_back",
    )(qkv, qkv, qkv, grad_out, blended, log_total)


ROWS = 376


def take_clip_kernel(group_ref, frames_ref, grads_ref, frames_out, grads_out, sums_ref, *, rows):
    step = pl.program_id(0)
    group = group_ref[0]

    def own(ref):
        both = ref[...]
        return jnp.where(group == 0, both[:, 0, :].astype(WIDE), both[:, 1, :].astype(WIDE))

    frames_out[...] = own(frames_ref).astype(LOW)
    grads = own(grads_ref)
    grads_out[...] = grads.astype(LOW)
    place = lax.broadcasted_iota(jnp.int32, grads.shape, 0) + step * ROWS
    sums = jnp.sum(jnp.where(place < rows, grads, 0.0), axis=0, keepdims=True)

    @pl.when(step == 0)
    def _():
        sums_ref[...] = sums

    @pl.when(step > 0)
    def _():
        sums_ref[...] += sums


def take_clip(group, frames, grads):
    _, rows, width = frames.shape
    both = pl.BlockSpec((ROWS, 2, width), lambda i, g: (i, 0, 0))
    single = pl.BlockSpec((ROWS, width), lambda i, g: (i, 0))
    return pl.pallas_call(
        functools.partial(take_clip_kernel, rows=rows),
        grid_spec=pltpu.PrefetchScalarGridSpec(
            num_scalar_prefetch=1,
            grid=(pl.cdiv(rows, ROWS),),
            in_specs=[both, both],
            out_specs=[single, single, pl.BlockSpec((1, width), lambda i, g: (0, 0))],
        ),
        out_shape=[jax.ShapeDtypeStruct((rows, width), LOW)] * 2
        + [jax.ShapeDtypeStruct((1, width), WIDE)],
        name="take_clip",
    )(group.reshape(1), frames.transpose(1, 0, 2), grads.transpose(1, 0, 2))


def both_clips_kernel(place_ref, own_ref, direct_ref, across_ref, out_ref):
    group, core = place_ref[0], place_ref[1]
    own = own_ref[...].astype(WIDE)
    direct = direct_ref[...].astype(WIDE)
    across = across_ref[...].astype(WIDE)
    first = jnp.where(core == 0, direct, across)
    second = jnp.where(core == 0, across, direct)
    other = jnp.concatenate([first, second], axis=1)
    out_ref[:, 0, :] = jnp.where(group == 0, own, other).astype(out_ref.dtype)
    out_ref[:, 1, :] = jnp.where(group == 0, other, own).astype(out_ref.dtype)


def both_clips(low, dtype):
    tensor_index = lax.axis_index("tensor")
    core = tensor_index % 2
    group = tensor_index // 2
    rows, width = low.shape
    half = width // 2
    mine = lax.dynamic_slice_in_dim(low, core * half, half, axis=1)
    direct = swap_tensor(mine, 2)
    across = swap_tensor(direct, 1)
    single = pl.BlockSpec((ROWS, width), lambda i, g: (i, 0))
    narrow = pl.BlockSpec((ROWS, half), lambda i, g: (i, 0))
    out = pl.pallas_call(
        both_clips_kernel,
        grid_spec=pltpu.PrefetchScalarGridSpec(
            num_scalar_prefetch=1,
            grid=(pl.cdiv(rows, ROWS),),
            in_specs=[single, narrow, narrow],
            out_specs=pl.BlockSpec((ROWS, 2, width), lambda i, g: (i, 0, 0)),
        ),
        out_shape=jax.ShapeDtypeStruct((rows, 2, width), dtype),
        name="both_clips",
    )(jnp.stack([group, core]), low, direct, across)
    return out.transpose(1, 0, 2)


def swap_tensor(value, distance):
    size = lax.axis_size("tensor")
    return lax.ppermute(value, "tensor", [(i, i ^ distance) for i in range(size)])


def swap_fsdp(value, distance):
    size = lax.axis_size("fsdp")
    return lax.ppermute(value, "fsdp", [(i, i ^ distance) for i in range(size)])


def swap(value, axis, distance):
    return swap_fsdp(value, distance) if axis == "fsdp" else swap_tensor(value, distance)


def far_steps():
    size = lax.axis_size("fsdp")
    return [1 << i for i in range(1, size.bit_length() - 1)]


def spread(piece, stages, keys=((0, 0),)):
    if piece.ndim == 2:
        piece = piece[None]
    parts = [(piece, tuple(keys))]
    for axis, distance in stages:
        held = parts[0][0] if len(parts) == 1 else jnp.concatenate([p for p, _ in parts], axis=0)
        held_keys = tuple(k for _, ks in parts for k in ks)
        step = (1, 0) if axis == "tensor" else (0, distance)
        got_keys = tuple((y ^ step[0], f ^ step[1]) for y, f in held_keys)
        parts = parts + [(swap(held, axis, distance), got_keys)]
    return parts


def stack_of(parts):
    keys = tuple(k for _, ks in parts for k in ks)
    return jnp.concatenate([p for p, _ in parts], axis=0), keys


def place_kernel(*refs, keys, finish):
    count = len(keys)
    stacks = refs[:count]
    outs, held, sem = refs[count:-2], refs[-2], refs[-1]
    mine = lax.axis_index("fsdp")
    group = lax.axis_index("tensor") // 2
    copies = []
    for stack, names in zip(stacks, keys):
        for i, (y, f) in enumerate(names):
            copy = pltpu.make_async_copy(
                stack.at[i], held.at[group ^ y, mine ^ f], sem.at[len(copies)]
            )
            copy.start()
            copies.append(copy)
    for copy in copies:
        copy.wait()
    finish(held, outs)


def place(parts, finish, out_shapes, name):
    size = lax.axis_size("fsdp")
    _, rows, columns = parts[0][0].shape
    total = sum(len(ks) for _, ks in parts)
    return pl.pallas_call(
        functools.partial(place_kernel, keys=tuple(ks for _, ks in parts), finish=finish),
        in_specs=[pl.BlockSpec(memory_space=pl.ANY)] * len(parts),
        out_specs=[pl.BlockSpec(memory_space=pltpu.VMEM)] * len(out_shapes),
        out_shape=[jax.ShapeDtypeStruct(s, LOW) for s in out_shapes],
        scratch_shapes=[
            pltpu.VMEM((2, size, rows, columns), LOW),
            pltpu.SemaphoreType.DMA((total,)),
        ],
        name=name,
    )(*[p for p, _ in parts])


def finish_qkv(held, outs, *, head_width):
    _, size, part, _ = held.shape
    for f in range(size):
        a, b = held[0, f], held[1, f]
        pieces = []
        for c in range(3):
            span = slice(c * head_width, (c + 1) * head_width)
            pieces += [a[:, span], b[:, span]]
        outs[0][f * part : (f + 1) * part, :] = jnp.concatenate(pieces, axis=1)


def finish_up(held, outs, *, unit_width):
    _, size, part, _ = held.shape
    for f in range(size):
        rows = slice(f * part, (f + 1) * part)
        for y in range(2):
            outs[0][y, rows, :] = held[y, f, :, :unit_width]
        outs[1][rows, :] = jnp.concatenate(
            [held[0, f, :, unit_width:], held[1, f, :, unit_width:]], axis=1
        )


def finish_plain(held, outs):
    _, size, part, _ = held.shape
    for f in range(size):
        for y in range(2):
            outs[0][y, f * part : (f + 1) * part, :] = held[y, f]


def pick(value, axis, index):
    return lax.dynamic_index_in_dim(value, index, axis, keepdims=False)


def add_low(a, b):
    return (a.astype(WIDE) + b.astype(WIDE)).astype(LOW)


def collect(grads, y_first):
    size = lax.axis_size("fsdp")
    mine = lax.axis_index("fsdp")
    group = lax.axis_index("tensor") // 2
    rows, columns = grads.shape[2:]
    half = size // 2
    low, high = mine % 2, mine // 2
    if y_first:
        got = swap_tensor(pick(grads, 0, 1 - group), 2)
        grads = add_low(pick(grads, 0, group), got).reshape(half, 2, rows, columns)
        got = swap_fsdp(pick(grads, 1, 1 - low), 1)
        grads = add_low(pick(grads, 1, low), got)
    else:
        grads = grads.reshape(2, half, 2, rows, columns)
        got = swap_fsdp(pick(grads, 2, 1 - low), 1)
        grads = add_low(pick(grads, 2, low), got)
        got = swap_tensor(pick(grads, 0, 1 - group), 2)
        grads = add_low(pick(grads, 0, group), got)
    while half > 2:
        half //= 2
        bit = (high // half) % 2
        grads = grads.reshape(2, half, rows, columns)
        got = swap_fsdp(pick(grads, 0, 1 - bit), 2 * half)
        grads = add_low(pick(grads, 0, bit), got)
    if half == 2:
        bit = high % 2
        got = swap_fsdp(pick(grads, 0, 1 - bit), 2)
        return pick(grads, 0, bit).astype(WIDE) + got.astype(WIDE)
    return grads[0].astype(WIDE)


def pair_sum(value):
    low = value.astype(LOW)
    return low.astype(WIDE) + swap_tensor(low, 1).astype(WIDE)


def local(
    frames_in, cotangent, ln_first, w_qkv, b_qv, w_out, b_out, ln_second, w_fc1, b_fc1, w_fc2, b_fc2
):
    _, frame_count, model_width = frames_in.shape
    size = lax.axis_size("fsdp")
    part = w_qkv.shape[0]
    head_width = w_qkv.shape[2]
    unit_width = w_fc1.shape[1]
    bias_part = b_qv.shape[1]
    group = lax.axis_index("tensor") // 2
    mine = lax.axis_index("fsdp")
    far = [("fsdp", d) for d in far_steps()]
    near, side = ("fsdp", 1), ("tensor", 2)

    def in_row(vectors, width, start):
        rows = jnp.zeros((vectors.shape[0], width), LOW)
        return lax.dynamic_update_slice(rows, vectors, (0, start))

    vectors = jnp.concatenate(
        [ln_first, ln_second, b_out[None], b_fc2[None], b_fc1[None]], axis=0
    )
    biases = in_row(b_qv, model_width, mine * bias_part)
    small = jnp.concatenate(
        [in_row(vectors, model_width, mine * part), biases], axis=0
    )
    small = jnp.pad(small, ((0, 16 - small.shape[0]), (0, 0)))
    for axis, distance in far + [near]:
        small = add_low(small, swap(small, axis, distance))
    small_other = swap(small, *side)
    small_wide = small.astype(WIDE)
    gain_one, shift_one, gain_two, shift_two, out_bias, down_bias = [
        small_wide[i : i + 1] for i in range(6)
    ]
    by_group = [
        jnp.where(group == 0, small, small_other)[6:9].astype(WIDE),
        jnp.where(group == 0, small_other, small)[6:9].astype(WIDE),
    ]
    up_bias = [b[0:1] for b in by_group]
    query_bias = [b[1, :head_width] for b in by_group]
    value_bias = [b[2, :head_width] for b in by_group]
    qkv_bias = jnp.concatenate(query_bias + [jnp.zeros((2 * head_width,), WIDE)] + value_bias)

    qkv_parts = spread(w_qkv.reshape(part, 3 * head_width), far)
    qkv_stack, qkv_keys = stack_of(qkv_parts)
    upper = spread(qkv_stack[:, : part // 2], [near, side], qkv_keys)
    lower = spread(qkv_stack[:, part // 2 :], [side, near], qkv_keys)
    upper_stack, upper_keys = stack_of(upper)
    lower_stack, lower_keys = stack_of(lower)
    order = [lower_keys.index(k) for k in upper_keys]
    lower_stack = jnp.concatenate([lower_stack[i : i + 1] for i in order], axis=0)
    (qkv_full,) = place(
        [(jnp.concatenate([upper_stack, lower_stack], axis=1), upper_keys)],
        functools.partial(finish_qkv, head_width=head_width),
        [(model_width, 6 * head_width)],
        "place_qkv",
    )
    up_parts = spread(jnp.concatenate([w_fc1, w_out.T], axis=1), far + [near, side])
    down_parts = spread(w_fc2.T, far + [side, near])

    frames_low, grad_low, grad_down_bias = take_clip(group, frames_in, cotangent)
    token_rows = frames_low.astype(WIDE)
    first_out, first_normed, first_inverse = layer_norm(token_rows, gain_one, shift_one)
    first_low = first_out.astype(LOW)
    qkv = (jnp.dot(first_low, qkv_full, preferred_element_type=WIDE) + qkv_bias).astype(LOW)
    attn_low, log_total = attend(qkv)

    up_all, out_full = place(
        up_parts,
        functools.partial(finish_up, unit_width=unit_width),
        [(2, model_width, unit_width), (model_width, 2 * head_width)],
        "place_up",
    )
    attn_terms = lax.dot_general(attn_low, out_full, NT, preferred_element_type=WIDE)
    middle = token_rows + pair_sum(attn_terms) + out_bias
    second_out, second_normed, second_inverse = layer_norm(middle, gain_two, shift_two)
    second_low = second_out.astype(LOW)

    (down_all,) = place(down_parts, finish_plain, [(2, model_width, unit_width)], "place_down")
    acts, grads_pre, grad_up_bias = [], [], []
    for i in range(2):
        pre_act = jnp.dot(second_low, up_all[i], preferred_element_type=WIDE) + up_bias[i]
        below = 0.5 * (1.0 + lax.erf(pre_act * 0.7071067811865476))
        acts.append((pre_act * below).astype(LOW))
        slope = below + pre_act * jnp.exp(-0.5 * pre_act * pre_act) * 0.3989422804014327
        grad_pre = jnp.dot(grad_low, down_all[i], preferred_element_type=WIDE) * slope
        grad_up_bias.append(jnp.sum(grad_pre, axis=0))
        grads_pre.append(grad_pre.astype(LOW))
    second_terms = sum(
        lax.dot_general(grads_pre[i], up_all[i], NT, preferred_element_type=WIDE) for i in range(2)
    )
    grad_second = pair_sum(second_terms)
    down_terms = sum(
        lax.dot_general(acts[i], down_all[i], NT, preferred_element_type=WIDE) for i in range(2)
    )
    result = (middle + pair_sum(down_terms) + down_bias).astype(LOW)
    frames_out = both_clips(result, LOW)

    grad_top = grad_low.astype(WIDE)
    grad_down = jnp.stack(
        [lax.dot_general(grad_low, acts[i], TN, preferred_element_type=WIDE) for i in range(2)]
    )
    grad_up = jnp.stack(
        [
            lax.dot_general(second_low, grads_pre[i], TN, preferred_element_type=WIDE)
            for i in range(2)
        ]
    )
    grad_down = collect(grad_down.astype(LOW).reshape(2, size, part, unit_width), False).T
    grad_up = collect(grad_up.astype(LOW).reshape(2, size, part, unit_width), True)

    grad_norm_two = [jnp.sum(grad_second * second_normed, axis=0), jnp.sum(grad_second, axis=0)]
    grad_middle = grad_top + norm_back(grad_second, second_normed, second_inverse, gain_two)
    grad_out_bias = jnp.sum(grad_middle, axis=0)
    grad_middle_low = grad_middle.astype(LOW)
    grad_attn = jnp.dot(grad_middle_low, out_full, preferred_element_type=WIDE).astype(LOW)
    grad_out = lax.dot_general(grad_middle_low, attn_low, TN, preferred_element_type=WIDE)
    grad_out = grad_out.astype(LOW).reshape(model_width, 2, head_width).transpose(1, 0, 2)
    grad_out = collect(grad_out.reshape(2, size, part, head_width), False).T

    grad_query, grad_keys, grad_values, bias_sums = attend_back(qkv, grad_attn, attn_low, log_total)
    stacked = jnp.concatenate([grad_query, grad_keys, grad_values], axis=1)
    first_terms = lax.dot_general(stacked, qkv_full, NT, preferred_element_type=WIDE)
    grad_first = pair_sum(first_terms)
    grad_rows = grad_middle + norm_back(grad_first, first_normed, first_inverse, gain_one)
    grad_frames = both_clips(grad_rows.astype(LOW), WIDE)

    grad_qkv = lax.dot_general(first_low, stacked, TN, preferred_element_type=WIDE).astype(LOW)
    grad_qkv = grad_qkv.reshape(model_width, 3, 2, head_width).transpose(2, 0, 1, 3)
    grad_qkv = collect(grad_qkv.reshape(2, size, part, 3 * head_width), False)
    grad_qkv = grad_qkv.reshape(part, 3, head_width)

    shared = jnp.stack(
        [jnp.sum(grad_first * first_normed, axis=0), jnp.sum(grad_first, axis=0)]
        + grad_norm_two
        + [grad_out_bias, grad_down_bias[0]]
    )
    sums = bias_sums[:, :2, :].transpose(1, 0, 2).reshape(2, 2, head_width).transpose(1, 0, 2)
    sums = jnp.pad(sums, ((0, 0), (0, 0), (0, model_width - head_width)))
    own = jnp.concatenate([jnp.stack(grad_up_bias)[:, None], sums], axis=1)
    vectors = jnp.concatenate([shared, pick(own, 0, group)], axis=0)
    sent = jnp.concatenate([shared, pick(own, 0, 1 - group)], axis=0)
    vectors = vectors + swap(sent, *side)
    for axis, distance in [near] + far:
        vectors = vectors + swap(vectors, axis, distance)
    slices = lax.dynamic_slice_in_dim(vectors, mine * part, part, axis=1)
    bias_slices = lax.dynamic_slice_in_dim(vectors[7:9], mine * bias_part, bias_part, axis=1)

    return (
        frames_out,
        grad_frames,
        slices[0:2],
        grad_qkv,
        bias_slices,
        grad_out,
        slices[4],
        slices[2:4],
        grad_up,
        slices[6],
        grad_down,
        slices[5],
    )


def solution(mesh):
    in_specs = (
        P("fsdp", None, None),
        P("fsdp", None, None),
        P(None, "fsdp"),
        P("fsdp", None, "tensor"),
        P(None, ("tensor", "fsdp")),
        P("tensor", "fsdp"),
        P("fsdp"),
        P(None, "fsdp"),
        P("fsdp", "tensor"),
        P(("tensor", "fsdp")),
        P("tensor", "fsdp"),
        P("fsdp"),
    )
    out_specs = (
        P("fsdp", None, None),
        P("fsdp", None, None),
        P(None, "fsdp"),
        P("fsdp", None, "tensor"),
        P(None, ("tensor", "fsdp")),
        P("tensor", "fsdp"),
        P("fsdp"),
        P(None, "fsdp"),
        P("fsdp", "tensor"),
        P(("tensor", "fsdp")),
        P("tensor", "fsdp"),
        P("fsdp"),
    )
    return jax.shard_map(local, mesh=mesh, in_specs=in_specs, out_specs=out_specs, check_vma=False)
```

```python
import functools

import jax
import jax.numpy as jnp
from jax import lax
from jax.experimental import pallas as pl
from jax.experimental.pallas import tpu as pltpu
from jax.sharding import PartitionSpec as P

HEAD_DIM = 64
EPSILON = 1e-05
LOW = jnp.bfloat16
WIDE = jnp.float32
NEGATIVE = -1e30
NT = (((1,), (1,)), ((), ()))
TN = (((0,), (0,)), ((), ()))


def layer_norm(values, norm_gain, norm_shift):
    centre = jnp.mean(values, axis=-1, keepdims=True)
    centred = values - centre
    inverse = lax.rsqrt(jnp.mean(centred * centred, axis=-1, keepdims=True) + EPSILON)
    normed = centred * inverse
    return (normed * norm_gain + norm_shift, normed, inverse)


def norm_back(grad_out, normed, inverse, norm_gain):
    scaled = grad_out * norm_gain
    return inverse * (
        scaled
        - jnp.mean(scaled, axis=-1, keepdims=True)
        - normed * jnp.mean(scaled * normed, axis=-1, keepdims=True)
    )


def cost(microseconds, size):
    return pl.CostEstimate(
        flops=int(microseconds * 1e9), transcendentals=0, bytes_accessed=int(size)
    )


def padded_rows(count):
    return -(-count // 512) * 512


def attend_kernel(q_ref, k_ref, v_ref, o_ref, l_ref, q_all, k_all, v_all, *, block):
    rows = q_ref.shape[0]
    padded = q_all.shape[0]
    fill = jnp.zeros((padded - rows, 128), LOW)
    q_all[...] = jnp.concatenate([q_ref[...] * LOW(HEAD_DIM**-0.5), fill], axis=0)
    k_all[...] = jnp.concatenate([k_ref[...], fill], axis=0)
    v_all[...] = jnp.concatenate([v_ref[...], fill], axis=0)
    valid = lax.broadcasted_iota(jnp.int32, (block, 256), 1) < rows - (padded - 256)
    upper = lax.broadcasted_iota(jnp.int32, (block, 128), 1) >= HEAD_DIM
    for step in range(padded // block):
        start = step * block
        parts = []
        for head in range(2):
            q_head = jnp.where(upper == (head == 1), q_all[start : start + block, :], LOW(0))
            scores = lax.dot_general(q_head, k_all[...], NT, preferred_element_type=WIDE)
            scores = jnp.concatenate(
                [
                    scores[:, : padded - 256],
                    jnp.where(valid, scores[:, padded - 256 :], NEGATIVE),
                ],
                axis=1,
            )
            highest = jnp.max(scores, axis=1, keepdims=True)
            weights = jnp.exp(scores - highest)
            total = jnp.sum(weights, axis=1, keepdims=True)
            blended = jnp.dot(weights.astype(LOW), v_all[...], preferred_element_type=WIDE)
            parts.append(blended * (1.0 / total))
            log_total = jnp.broadcast_to(highest + jnp.log(total), (block, 128)).T
            l_ref[head, :, start : start + block] = log_total[0:8, :]
        merged = jnp.where(upper, parts[1], parts[0]).astype(LOW)
        count = min(block, rows - start)
        o_ref[start : start + count, :] = merged[:count]


def attend(qkv):
    rows, width = qkv.shape
    pairs = width // 3 // 128
    padded = padded_rows(rows)

    def column(which):
        return pl.BlockSpec((rows, 128), lambda p: (0, 3 * p + which))

    return pl.pallas_call(
        functools.partial(attend_kernel, block=512),
        grid=(pairs,),
        in_specs=[column(0), column(1), column(2)],
        out_specs=[
            pl.BlockSpec((rows, 128), lambda p: (0, p)),
            pl.BlockSpec((2, 8, padded), lambda p: (p, 0, 0)),
        ],
        out_shape=[
            jax.ShapeDtypeStruct((rows, width // 3), LOW),
            jax.ShapeDtypeStruct((2 * pairs, 8, padded), WIDE),
        ],
        scratch_shapes=[pltpu.VMEM((padded, 128), LOW)] * 3,
        cost_estimate=cost(22, rows * width * 3),
        name="attend",
    )(qkv, qkv, qkv)


def attend_back_kernel(
    q_ref, k_ref, v_ref, g_ref, o_ref, l_ref, d_ref, db_ref,
    q_all, k_all, v_all, g_all, dq_turned, centre_all, *, block,
):
    rows = q_ref.shape[0]
    padded = k_all.shape[0]
    fill = jnp.zeros((padded - rows, 128), LOW)

    def pad(value):
        return jnp.concatenate([value, fill], axis=0)

    upper = lax.broadcasted_iota(jnp.int32, (padded, 128), 1) >= HEAD_DIM
    upper8 = lax.broadcasted_iota(jnp.int32, (8, 128), 1) >= HEAD_DIM
    upper_block = lax.broadcasted_iota(jnp.int32, (block, 128), 1) >= HEAD_DIM
    scale = HEAD_DIM**-0.5
    k_all[...] = pad(k_ref[...])
    v_all[...] = pad(v_ref[...])
    q_full = pad(q_ref[...] * LOW(scale))
    g_full = pad(g_ref[...])
    product = g_full.astype(WIDE) * pad(o_ref[...]).astype(WIDE)
    coarse = product.astype(LOW)
    fine = (product - coarse.astype(WIDE)).astype(LOW)
    for head in range(2):
        mine = upper == (head == 1)
        q_all[head] = jnp.where(mine, q_full, LOW(0))
        g_all[head] = jnp.where(mine, g_full, LOW(0))
        ones = jnp.where(upper8 == (head == 1), 1.0, 0.0).astype(LOW)
        centre_all[head] = lax.dot_general(
            ones, coarse, NT, preferred_element_type=WIDE
        ) + lax.dot_general(ones, fine, NT, preferred_element_type=WIDE)
    dq_turned[...] = jnp.zeros_like(dq_turned)
    value_bias = jnp.zeros((1, 128), WIDE)
    for step in range(padded // block):
        start = step * block
        keys = k_all[start : start + block, :]
        values = v_all[start : start + block, :]
        grad_values = grad_keys = grad_query = None
        for head in range(2):
            scores = lax.dot_general(keys, q_all[head], NT, preferred_element_type=WIDE)
            chances = jnp.exp(scores - l_ref[head, 0:1, :])
            if start + block > rows:
                place = lax.broadcasted_iota(jnp.int32, (block, padded), 0)
                chances = jnp.where(place < rows - start, chances, 0.0)
            grad_weights = lax.dot_general(
                values, g_all[head], NT, preferred_element_type=WIDE
            )
            grad_scores = (chances * (grad_weights - centre_all[head, 0:1, :])).astype(LOW)
            from_values = jnp.dot(
                chances.astype(LOW), g_all[head], preferred_element_type=WIDE
            )
            from_keys = jnp.dot(grad_scores, q_all[head], preferred_element_type=WIDE)
            keys_head = jnp.where(upper_block == (head == 1), keys, LOW(0))
            from_query = jnp.dot(keys_head.T, grad_scores, preferred_element_type=WIDE)
            if head == 0:
                grad_values, grad_keys, grad_query = from_values, from_keys, from_query
            else:
                grad_values = grad_values + from_values
                grad_keys = grad_keys + from_keys
                grad_query = grad_query + from_query
        dq_turned[...] += grad_query
        count = min(block, rows - start)
        value_bias += jnp.sum(grad_values, axis=0, keepdims=True)
        d_ref[start : start + count, 256:384] = grad_values[:count].astype(LOW)
        d_ref[start : start + count, 128:256] = grad_keys[:count].astype(LOW)
    grad_query = (dq_turned[...] * scale).T
    d_ref[:, 0:128] = grad_query[:rows].astype(LOW)
    db_ref[0:1, :] = jnp.sum(grad_query, axis=0, keepdims=True)
    db_ref[1:2, :] = value_bias


def attend_back(pair, qkv, grad_out, blended, log_total):
    rows = qkv.shape[0]
    padded = padded_rows(rows)

    def column(index):
        return pl.BlockSpec((rows, 128), lambda i: (0, index))

    return pl.pallas_call(
        functools.partial(attend_back_kernel, block=512),
        grid=(1,),
        in_specs=[
            column(3 * pair),
            column(3 * pair + 1),
            column(3 * pair + 2),
            column(pair),
            column(pair),
            pl.BlockSpec((2, 8, padded), lambda i: (pair, 0, 0)),
        ],
        out_specs=[
            pl.BlockSpec((rows, 384), lambda i: (0, 0)),
            pl.BlockSpec((8, 128), lambda i: (0, 0)),
        ],
        out_shape=[
            jax.ShapeDtypeStruct((rows, 384), LOW),
            jax.ShapeDtypeStruct((8, 128), WIDE),
        ],
        scratch_shapes=[
            pltpu.VMEM((2, padded, 128), LOW),
            pltpu.VMEM((padded, 128), LOW),
            pltpu.VMEM((padded, 128), LOW),
            pltpu.VMEM((2, padded, 128), LOW),
            pltpu.VMEM((128, padded), WIDE),
            pltpu.VMEM((2, 8, padded), WIDE),
        ],
        cost_estimate=cost(13, rows * 128 * 16),
        name="attend_back",
    )(qkv, qkv, qkv, grad_out, blended, log_total)


def merge_kernel(*refs, count):
    parts, weight_ref, out_ref = refs[:count], refs[count], refs[count + 1]
    total = None
    for i, part in enumerate(parts):
        width = part.shape[1]
        term = lax.dot_general(
            part[...],
            weight_ref[:, i * width : (i + 1) * width],
            NT,
            preferred_element_type=WIDE,
        )
        total = term if total is None else total + term
    out_ref[...] = total.astype(LOW)


def merge(parts, weight):
    rows, width = parts[0].shape
    return pl.pallas_call(
        functools.partial(merge_kernel, count=len(parts)),
        grid=(pl.cdiv(rows, ROWS),),
        in_specs=[pl.BlockSpec((ROWS, width), lambda i: (i, 0))] * len(parts)
        + [pl.BlockSpec(weight.shape, lambda i: (0, 0))],
        out_specs=pl.BlockSpec((ROWS, weight.shape[0]), lambda i: (i, 0)),
        out_shape=jax.ShapeDtypeStruct((rows, weight.shape[0]), LOW),
        cost_estimate=cost(4, rows * weight.shape[1] * 4),
        name="merge",
    )(*parts, weight)


ROWS = 376


def take_clip_kernel(group_ref, both_ref, own_ref, sums_ref, *, rows):
    step = pl.program_id(0)
    both = both_ref[...]
    own = jnp.where(group_ref[0] == 0, both[:, 0, :].astype(WIDE), both[:, 1, :].astype(WIDE))
    own_ref[...] = own.astype(LOW)
    place = lax.broadcasted_iota(jnp.int32, own.shape, 0) + step * ROWS
    sums = jnp.sum(jnp.where(place < rows, own, 0.0), axis=0, keepdims=True)

    @pl.when(step == 0)
    def _():
        sums_ref[...] = sums

    @pl.when(step > 0)
    def _():
        sums_ref[...] += sums


def take_clip(group, both):
    _, rows, width = both.shape
    return pl.pallas_call(
        functools.partial(take_clip_kernel, rows=rows),
        grid_spec=pltpu.PrefetchScalarGridSpec(
            num_scalar_prefetch=1,
            grid=(pl.cdiv(rows, ROWS),),
            in_specs=[pl.BlockSpec((ROWS, 2, width), lambda i, g: (i, 0, 0))],
            out_specs=[
                pl.BlockSpec((ROWS, width), lambda i, g: (i, 0)),
                pl.BlockSpec((1, width), lambda i, g: (0, 0)),
            ],
        ),
        out_shape=[
            jax.ShapeDtypeStruct((rows, width), LOW),
            jax.ShapeDtypeStruct((1, width), WIDE),
        ],
        cost_estimate=cost(9, rows * width * 6),
        name="take_clip",
    )(group.reshape(1), both.transpose(1, 0, 2))


def both_clips_kernel(place_ref, own_ref, direct_ref, across_ref, out_ref):
    group, core = place_ref[0], place_ref[1]
    own = own_ref[...].astype(WIDE)
    direct = direct_ref[...].astype(WIDE)
    across = across_ref[...].astype(WIDE)
    first = jnp.where(core == 0, direct, across)
    second = jnp.where(core == 0, across, direct)
    other = jnp.concatenate([first, second], axis=1)
    out_ref[:, 0, :] = jnp.where(group == 0, own, other).astype(out_ref.dtype)
    out_ref[:, 1, :] = jnp.where(group == 0, other, own).astype(out_ref.dtype)


def both_clips(low, dtype):
    tensor_index = lax.axis_index("tensor")
    core = tensor_index % 2
    group = tensor_index // 2
    rows, width = low.shape
    half = width // 2
    mine = lax.dynamic_slice_in_dim(low, core * half, half, axis=1)
    direct = swap_tensor(mine, 2)
    across = swap_tensor(direct, 1)
    single = pl.BlockSpec((ROWS, width), lambda i, g: (i, 0))
    narrow = pl.BlockSpec((ROWS, half), lambda i, g: (i, 0))
    out = pl.pallas_call(
        both_clips_kernel,
        grid_spec=pltpu.PrefetchScalarGridSpec(
            num_scalar_prefetch=1,
            grid=(pl.cdiv(rows, ROWS),),
            in_specs=[single, narrow, narrow],
            out_specs=pl.BlockSpec((ROWS, 2, width), lambda i, g: (i, 0, 0)),
        ),
        out_shape=jax.ShapeDtypeStruct((rows, 2, width), dtype),
        cost_estimate=cost(8, rows * width * 12),
        name="both_clips",
    )(jnp.stack([group, core]), low, direct, across)
    return out.transpose(1, 0, 2)


def swap_tensor(value, distance):
    size = lax.axis_size("tensor")
    return lax.ppermute(value, "tensor", [(i, i ^ distance) for i in range(size)])


def swap_fsdp(value, distance):
    size = lax.axis_size("fsdp")
    return lax.ppermute(value, "fsdp", [(i, i ^ distance) for i in range(size)])


def swap_both(value):
    width = lax.axis_size("tensor")
    count = lax.axis_size("fsdp") * width
    pairs = [(i, ((i // width) ^ 1) * width + ((i % width) ^ 2)) for i in range(count)]
    return lax.ppermute(value, ("fsdp", "tensor"), pairs)


def after(value, *others):
    return lax.optimization_barrier((value, others))[0]


def spread_far(piece):
    far = lax.axis_size("fsdp") // 2
    return jnp.stack([piece] + [swap_fsdp(piece, 2 * i) for i in range(1, far)])


def spread_near(stack):
    far = stack.shape[0]
    return [
        (value, tuple((y, 2 * i + x) for i in range(far)))
        for y, x, value in (
            (0, 0, stack),
            (0, 1, swap_fsdp(stack, 1)),
            (1, 0, swap_tensor(stack, 2)),
            (1, 1, swap_both(stack)),
        )
    ]


def place_kernel(*refs, keys, finish):
    count = len(keys)
    stacks = refs[:count]
    outs, held, sem = refs[count:-2], refs[-2], refs[-1]
    mine = lax.axis_index("fsdp")
    group = lax.axis_index("tensor") // 2
    copies = []
    for stack, names in zip(stacks, keys):
        for i, (y, f) in enumerate(names):
            copy = pltpu.make_async_copy(
                stack.at[i], held.at[group ^ y, mine ^ f], sem.at[len(copies)]
            )
            copy.start()
            copies.append(copy)
    for copy in copies:
        copy.wait()
    finish(held, outs)


def place(parts, finish, out_shapes, name):
    size = lax.axis_size("fsdp")
    _, rows, columns = parts[0][0].shape
    total = sum(len(ks) for _, ks in parts)
    return pl.pallas_call(
        functools.partial(place_kernel, keys=tuple(ks for _, ks in parts), finish=finish),
        in_specs=[pl.BlockSpec(memory_space=pl.ANY)] * len(parts),
        out_specs=[pl.BlockSpec(memory_space=pltpu.VMEM)] * len(out_shapes),
        out_shape=[jax.ShapeDtypeStruct(*s) for s in out_shapes],
        scratch_shapes=[
            pltpu.VMEM((2, size, rows, columns), LOW),
            pltpu.SemaphoreType.DMA((total,)),
        ],
        cost_estimate=cost(3.5, 4 * size * rows * columns * 2),
        name=name,
    )(*[p for p, _ in parts])


def finish_qkv(held, outs, *, part, head_width, bias_part):
    _, size, _, _ = held.shape
    pairs = 2 * head_width // 128
    for f in range(size):
        a, b = held[0, f, :part], held[1, f, :part]
        wide = []
        for c in range(3):
            span = slice(c * head_width, (c + 1) * head_width)
            wide.append(jnp.concatenate([a[:, span], b[:, span]], axis=1))
        for p in range(pairs):
            for c in range(3):
                outs[0][f * part : (f + 1) * part, (3 * p + c) * 128 : (3 * p + c + 1) * 128] = (
                    wide[c][:, p * 128 : (p + 1) * 128]
                )
    rows = [[held[y, f, part:].astype(WIDE) for f in range(size)] for y in range(2)]
    for y in range(2):
        outs[1][y] = jnp.concatenate([r[:, :part] for r in rows[y]], axis=1)
    biases = []
    for c in range(2):
        span = slice(c * bias_part, (c + 1) * bias_part)
        biases.append(jnp.concatenate([r[7:8, span] for y in range(2) for r in rows[y]], axis=1))
    nothing = jnp.zeros((1, 128), WIDE)
    for p in range(pairs):
        span = slice(p * 128, (p + 1) * 128)
        outs[2][:, 3 * p * 128 : (3 * p + 1) * 128] = biases[0][:, span]
        outs[2][:, (3 * p + 1) * 128 : (3 * p + 2) * 128] = nothing
        outs[2][:, (3 * p + 2) * 128 : (3 * p + 3) * 128] = biases[1][:, span]


def finish_up(held, outs, *, unit_width):
    _, size, part, _ = held.shape
    for f in range(size):
        rows = slice(f * part, (f + 1) * part)
        for y in range(2):
            outs[0][y, rows, :] = held[y, f, :, :unit_width]
        outs[1][rows, :] = jnp.concatenate(
            [held[0, f, :, unit_width:], held[1, f, :, unit_width:]], axis=1
        )


def finish_plain(held, outs):
    _, size, part, _ = held.shape
    for f in range(size):
        for y in range(2):
            outs[0][y, f * part : (f + 1) * part, :] = held[y, f]


def pick(value, axis, index):
    return lax.dynamic_index_in_dim(value, index, axis, keepdims=False)


def add_low(a, b):
    return (a.astype(WIDE) + b.astype(WIDE)).astype(LOW)


def near_far():
    mine = lax.axis_index("fsdp")
    return mine % 2, mine // 2


def fold_near(grads):
    low, _ = near_far()
    axis = grads.ndim - 3
    got = swap_fsdp(pick(grads, axis, 1 - low), 1)
    return add_low(pick(grads, axis, low), got)


def fold_cross(grads):
    low, _ = near_far()
    group = lax.axis_index("tensor") // 2

    def at(y, x):
        return pick(pick(grads, 0, y), 1, x)

    side = swap_tensor(at(1 - group, low), 2)
    near = swap_fsdp(at(group, 1 - low), 1)
    both = swap_both(at(1 - group, 1 - low))
    total = at(group, low).astype(WIDE) + side.astype(WIDE)
    return (total + (near.astype(WIDE) + both.astype(WIDE))).astype(LOW)


def fold_far(grads):
    _, high = near_far()
    axis = grads.ndim - 3
    total = pick(grads, axis, high).astype(WIDE)
    for i in range(1, grads.shape[axis]):
        total = total + swap_fsdp(pick(grads, axis, high ^ i), 2 * i).astype(WIDE)
    return total


def fold_side(grads):
    group = lax.axis_index("tensor") // 2
    got = swap_tensor(pick(grads, 0, 1 - group), 2)
    return pick(grads, 0, group).astype(WIDE) + got.astype(WIDE)


def pair_sum(value):
    low = value.astype(LOW)
    return low.astype(WIDE) + swap_tensor(low, 1).astype(WIDE)


def local(
    frames_in, cotangent, ln_first, w_qkv, b_qv, w_out, b_out, ln_second, w_fc1, b_fc1, w_fc2, b_fc2
):
    _, frame_count, model_width = frames_in.shape
    size = lax.axis_size("fsdp")
    part = w_qkv.shape[0]
    head_width = w_qkv.shape[2]
    unit_width = w_fc1.shape[1]
    bias_part = b_qv.shape[1]
    group = lax.axis_index("tensor") // 2
    mine = lax.axis_index("fsdp")
    far = size // 2

    vectors = jnp.concatenate(
        [
            ln_first,
            ln_second,
            b_out[None],
            b_fc2[None],
            b_fc1[None],
            jnp.pad(b_qv.reshape(1, -1), ((0, 0), (0, part - 2 * bias_part))),
        ],
        axis=0,
    )
    vectors = jnp.pad(vectors, ((0, 0), (0, 3 * head_width - part)))
    qkv_piece = jnp.concatenate([w_qkv.reshape(part, 3 * head_width), vectors], axis=0)
    qkv_far = spread_far(qkv_piece)
    up_far = spread_far(jnp.concatenate([w_fc1, w_out.T], axis=1))
    down_far = spread_far(w_fc2.T)
    frames_low, _ = take_clip(group, frames_in)
    qkv_parts = spread_near(qkv_far)
    grad_low, grad_down_bias = take_clip(after(group, qkv_far), cotangent)
    up_parts = spread_near(up_far)
    down_parts = spread_near(down_far)
    qkv_full, vectors, qkv_bias = place(
        qkv_parts,
        functools.partial(finish_qkv, part=part, head_width=head_width, bias_part=bias_part),
        [
            ((model_width, 6 * head_width), LOW),
            ((2, 8, model_width), WIDE),
            ((1, 6 * head_width), WIDE),
        ],
        "place_qkv",
    )
    gain_one, shift_one, gain_two, shift_two, out_bias, down_bias = [
        vectors[0, i : i + 1] for i in range(6)
    ]
    up_bias = [vectors[i, 6:7] for i in range(2)]

    token_rows = frames_low.astype(WIDE)
    first_out, first_normed, first_inverse = layer_norm(token_rows, gain_one, shift_one)
    first_low = first_out.astype(LOW)
    qkv = (jnp.dot(first_low, qkv_full, preferred_element_type=WIDE) + qkv_bias).astype(LOW)
    attn_low, log_total = attend(after(qkv, up_far, down_far, grad_low))

    up_all, out_full = place(
        up_parts,
        functools.partial(finish_up, unit_width=unit_width),
        [((2, model_width, unit_width), LOW), ((model_width, 2 * head_width), LOW)],
        "place_up",
    )
    attn_terms = lax.dot_general(attn_low, out_full, NT, preferred_element_type=WIDE)
    middle = token_rows + pair_sum(attn_terms) + out_bias
    second_out, second_normed, second_inverse = layer_norm(middle, gain_two, shift_two)
    second_low = second_out.astype(LOW)

    (down_all,) = place(
        down_parts, finish_plain, [((2, model_width, unit_width), LOW)], "place_down"
    )
    acts, slopes = [], []
    for i in range(2):
        pre_act = jnp.dot(second_low, up_all[i], preferred_element_type=WIDE) + up_bias[i]
        below = 0.5 * (1.0 + lax.erf(pre_act * 0.7071067811865476))
        acts.append((pre_act * below).astype(LOW))
        slopes.append(below + pre_act * jnp.exp(-0.5 * pre_act * pre_act) * 0.3989422804014327)
    grad_down = jnp.stack(
        [lax.dot_general(grad_low, acts[i], TN, preferred_element_type=WIDE) for i in range(2)]
    ).astype(LOW)
    grad_down = grad_down.reshape(2, far, 2, part, unit_width)
    grad_down = fold_near(grad_down)

    down_terms = sum(
        lax.dot_general(acts[i], down_all[i], NT, preferred_element_type=WIDE) for i in range(2)
    )
    result = (middle + pair_sum(down_terms) + down_bias).astype(LOW)
    frames_out = both_clips(result, LOW)

    grads_pre, grad_up_bias = [], []
    for i in range(2):
        grad_pre = jnp.dot(grad_low, down_all[i], preferred_element_type=WIDE) * slopes[i]
        grad_up_bias.append(jnp.sum(grad_pre, axis=0))
        grads_pre.append(grad_pre.astype(LOW))
    second_terms = sum(
        lax.dot_general(grads_pre[i], up_all[i], NT, preferred_element_type=WIDE) for i in range(2)
    )
    grad_second = pair_sum(second_terms)
    grad_up = jnp.stack(
        [
            lax.dot_general(second_low, grads_pre[i], TN, preferred_element_type=WIDE)
            for i in range(2)
        ]
    ).astype(LOW)
    grad_up = fold_cross(grad_up.reshape(2, far, 2, part, unit_width))

    grad_norm_two = [jnp.sum(grad_second * second_normed, axis=0), jnp.sum(grad_second, axis=0)]
    grad_middle = grad_low.astype(WIDE) + norm_back(
        grad_second, second_normed, second_inverse, gain_two
    )
    grad_out_bias = jnp.sum(grad_middle, axis=0)
    grad_middle_low = grad_middle.astype(LOW)
    grad_attn = jnp.dot(grad_middle_low, out_full, preferred_element_type=WIDE).astype(LOW)
    grad_out = lax.dot_general(grad_middle_low, attn_low, TN, preferred_element_type=WIDE)
    grad_out = fold_near(grad_out.astype(LOW).reshape(far, 2, part, 2 * head_width))

    pairs = 2 * head_width // 128
    grads_qkv, grads_pair, bias_sums = [], [], []
    for p in range(pairs):
        grad_pair, sums = attend_back(p, qkv, grad_attn, attn_low, log_total)
        grads_pair.append(grad_pair)
        bias_sums.append(sums)
        if p + 1 < pairs:
            grad_attn = after(grad_attn, grad_pair)
        if p == 0:
            grad_down = fold_far(grad_down)
            grad_down = fold_side(grad_down.astype(LOW)).T
            grad_out = fold_far(grad_out).astype(LOW)
            grad_out = grad_out.reshape(part, 2, head_width).transpose(1, 0, 2)
            grad_out = fold_side(grad_out).T
        if p == 1:
            grad_up = fold_far(grad_up)
        grad = lax.dot_general(first_low, grad_pair, TN, preferred_element_type=WIDE)
        grads_qkv.append(fold_near(grad.astype(LOW).reshape(far, 2, part, 384)))
    first_terms = merge(grads_pair, qkv_full)
    grad_first = first_terms.astype(WIDE) + swap_tensor(first_terms, 1).astype(WIDE)
    grad_rows = grad_middle + norm_back(grad_first, first_normed, first_inverse, gain_one)
    grad_frames = both_clips(grad_rows.astype(LOW), WIDE)

    grad_qkv = jnp.stack([fold_far(g) for g in grads_qkv]).astype(LOW)
    grad_qkv = grad_qkv.reshape(pairs, part, 3, 128).transpose(2, 1, 0, 3)
    grad_qkv = grad_qkv.reshape(3, part, 2, head_width).transpose(2, 0, 1, 3)
    grad_qkv = fold_side(grad_qkv).transpose(1, 0, 2)

    shared = jnp.stack(
        [jnp.sum(grad_first * first_normed, axis=0), jnp.sum(grad_first, axis=0)]
        + grad_norm_two
        + [grad_out_bias, grad_down_bias[0]]
    )
    sums = jnp.concatenate([b[0:2] for b in bias_sums], axis=1)
    sums = sums.reshape(2, 2, head_width).transpose(1, 0, 2)
    sums = jnp.pad(sums, ((0, 0), (0, 0), (0, model_width - head_width)))
    own = jnp.concatenate([jnp.stack(grad_up_bias)[:, None], sums], axis=1)
    vectors = jnp.concatenate([shared, pick(own, 0, group)], axis=0)
    sent = jnp.concatenate([shared, pick(own, 0, 1 - group)], axis=0)
    vectors = (vectors + swap_tensor(sent, 2)) + (swap_fsdp(vectors, 1) + swap_both(sent))
    total = vectors
    for i in range(1, far):
        total = total + swap_fsdp(vectors, 2 * i)
    slices = lax.dynamic_slice_in_dim(total, mine * part, part, axis=1)
    bias_slices = lax.dynamic_slice_in_dim(total[7:9], mine * bias_part, bias_part, axis=1)

    return (
        frames_out,
        grad_frames,
        slices[0:2],
        grad_qkv,
        bias_slices,
        grad_out,
        slices[4],
        slices[2:4],
        grad_up,
        slices[6],
        grad_down,
        slices[5],
    )


def solution(mesh):
    in_specs = (
        P("fsdp", None, None),
        P("fsdp", None, None),
        P(None, "fsdp"),
        P("fsdp", None, "tensor"),
        P(None, ("tensor", "fsdp")),
        P("tensor", "fsdp"),
        P("fsdp"),
        P(None, "fsdp"),
        P("fsdp", "tensor"),
        P(("tensor", "fsdp")),
        P("tensor", "fsdp"),
        P("fsdp"),
    )
    out_specs = (
        P("fsdp", None, None),
        P("fsdp", None, None),
        P(None, "fsdp"),
        P("fsdp", None, "tensor"),
        P(None, ("tensor", "fsdp")),
        P("tensor", "fsdp"),
        P("fsdp"),
        P(None, "fsdp"),
        P("fsdp", "tensor"),
        P(("tensor", "fsdp")),
        P("tensor", "fsdp"),
        P("fsdp"),
    )
    return jax.shard_map(local, mesh=mesh, in_specs=in_specs, out_specs=out_specs, check_vma=False)
```

```python
import functools

import jax
import jax.numpy as jnp
from jax import lax
from jax.experimental import pallas as pl
from jax.experimental.pallas import tpu as pltpu
from jax.sharding import PartitionSpec as P


HEAD_DIM = 64
EPSILON = 1e-05
LOW = jnp.bfloat16
WIDE = jnp.float32
NEGATIVE = -1e30
NT = (((1,), (1,)), ((), ()))
TN = (((0,), (0,)), ((), ()))


def layer_norm(values, norm_gain, norm_shift):
    centre = jnp.mean(values, axis=-1, keepdims=True)
    centred = values - centre
    inverse = lax.rsqrt(jnp.mean(centred * centred, axis=-1, keepdims=True) + EPSILON)
    normed = centred * inverse
    return (normed * norm_gain + norm_shift, normed, inverse)


def cost(microseconds, size):
    return pl.CostEstimate(
        flops=int(microseconds * 1e9), transcendentals=0, bytes_accessed=int(size)
    )


def padded_rows(count):
    return -(-count // 512) * 512


def attend_kernel(q_ref, k_ref, v_ref, o_ref, l_ref, q_all, k_all, v_all, *, block):
    rows = q_ref.shape[0]
    padded = q_all.shape[0]
    fill = jnp.zeros((padded - rows, 128), LOW)
    q_all[...] = jnp.concatenate([q_ref[...] * LOW(HEAD_DIM**-0.5), fill], axis=0)
    k_all[...] = jnp.concatenate([k_ref[...], fill], axis=0)
    v_all[...] = jnp.concatenate([v_ref[...], fill], axis=0)
    valid = lax.broadcasted_iota(jnp.int32, (block, 256), 1) < rows - (padded - 256)
    upper = lax.broadcasted_iota(jnp.int32, (block, 128), 1) >= HEAD_DIM
    for step in range(padded // block):
        start = step * block
        parts = []
        for head in range(2):
            q_head = jnp.where(upper == (head == 1), q_all[start : start + block, :], LOW(0))
            scores = lax.dot_general(q_head, k_all[...], NT, preferred_element_type=WIDE)
            scores = jnp.concatenate(
                [
                    scores[:, : padded - 256],
                    jnp.where(valid, scores[:, padded - 256 :], NEGATIVE),
                ],
                axis=1,
            )
            highest = jnp.max(scores, axis=1, keepdims=True)
            weights = jnp.exp(scores - highest)
            total = jnp.sum(weights, axis=1, keepdims=True)
            blended = jnp.dot(weights.astype(LOW), v_all[...], preferred_element_type=WIDE)
            parts.append(blended * (1.0 / total))
            log_total = jnp.broadcast_to(highest + jnp.log(total), (block, 128)).T
            l_ref[head, :, start : start + block] = log_total[0:8, :]
        merged = jnp.where(upper, parts[1], parts[0]).astype(LOW)
        count = min(block, rows - start)
        o_ref[start : start + count, :] = merged[:count]


def attend(qkv):
    rows, width = qkv.shape
    pairs = width // 3 // 128
    padded = padded_rows(rows)

    def column(which):
        return pl.BlockSpec((rows, 128), lambda p: (0, 3 * p + which))

    return pl.pallas_call(
        functools.partial(attend_kernel, block=512),
        grid=(pairs,),
        in_specs=[column(0), column(1), column(2)],
        out_specs=[
            pl.BlockSpec((rows, 128), lambda p: (0, p)),
            pl.BlockSpec((2, 8, padded), lambda p: (p, 0, 0)),
        ],
        out_shape=[
            jax.ShapeDtypeStruct((rows, width // 3), LOW),
            jax.ShapeDtypeStruct((2 * pairs, 8, padded), WIDE),
        ],
        scratch_shapes=[pltpu.VMEM((padded, 128), LOW)] * 3,
        cost_estimate=cost(22, rows * width * 3),
        name="fa",
    )(qkv, qkv, qkv)


def attend_back_kernel(
    q_ref, k_ref, v_ref, g_ref, o_ref, l_ref, d_ref, db_ref,
    q_all, k_all, v_all, g_all, dq_turned, centre_all, *, rows, block,
):
    padded = k_all.shape[0]
    fill = jnp.zeros((padded - rows, 128), LOW)

    def pad(value):
        return jnp.concatenate([value, fill], axis=0)

    upper = lax.broadcasted_iota(jnp.int32, (padded, 128), 1) >= HEAD_DIM
    upper8 = lax.broadcasted_iota(jnp.int32, (8, 128), 1) >= HEAD_DIM
    upper_block = lax.broadcasted_iota(jnp.int32, (block, 128), 1) >= HEAD_DIM
    row_block = lax.broadcasted_iota(jnp.int32, (block, 128), 0)
    scale = HEAD_DIM**-0.5
    keys = k_ref[...]
    k_all[...] = jnp.concatenate([keys, keys[: padded - rows]], axis=0)
    v_all[...] = pad(v_ref[...])
    q_full = pad(q_ref[...] * LOW(scale))
    g_full = pad(g_ref[...])
    product = g_full.astype(WIDE) * pad(o_ref[...]).astype(WIDE)
    coarse = product.astype(LOW)
    fine = (product - coarse.astype(WIDE)).astype(LOW)
    for head in range(2):
        mine = upper == (head == 1)
        q_all[head] = jnp.where(mine, q_full, LOW(0))
        g_all[head] = jnp.where(mine, g_full, LOW(0))
        ones = jnp.where(upper8 == (head == 1), 1.0, 0.0).astype(LOW)
        centre_all[head] = lax.dot_general(
            ones, coarse, NT, preferred_element_type=WIDE
        ) + lax.dot_general(ones, fine, NT, preferred_element_type=WIDE)
    dq_turned[...] = jnp.zeros_like(dq_turned)

    def step(index, value_bias):
        span = pl.ds(pl.multiple_of(index * block, block), block)
        keys, values = k_all[span, :], v_all[span, :]
        real = row_block < rows - index * block
        grad_values = grad_keys = grad_query = None
        for head in range(2):
            scores = lax.dot_general(keys, q_all[head], NT, preferred_element_type=WIDE)
            chances = jnp.exp(scores - l_ref[head, 0:1, :])
            grad_weights = lax.dot_general(
                values, g_all[head], NT, preferred_element_type=WIDE
            )
            grad_scores = (chances * (grad_weights - centre_all[head, 0:1, :])).astype(LOW)
            from_values = jnp.dot(
                chances.astype(LOW), g_all[head], preferred_element_type=WIDE
            )
            from_keys = jnp.dot(grad_scores, q_all[head], preferred_element_type=WIDE)
            keys_head = jnp.where(real & (upper_block == (head == 1)), keys, LOW(0))
            from_query = jnp.dot(keys_head.T, grad_scores, preferred_element_type=WIDE)
            if head == 0:
                grad_values, grad_keys, grad_query = from_values, from_keys, from_query
            else:
                grad_values = grad_values + from_values
                grad_keys = grad_keys + from_keys
                grad_query = grad_query + from_query
        dq_turned[...] += grad_query
        d_ref[span, 128:256] = grad_keys.astype(LOW)
        d_ref[span, 256:384] = grad_values.astype(LOW)
        return value_bias + jnp.sum(jnp.where(real, grad_values, 0.0), axis=0, keepdims=True)

    value_bias = lax.fori_loop(0, padded // block, step, jnp.zeros((1, 128), WIDE))
    grad_query = (dq_turned[...] * scale).T
    d_ref[:, 0:128] = grad_query.astype(LOW)
    db_ref[0:1, :] = jnp.sum(grad_query, axis=0, keepdims=True)
    db_ref[1:2, :] = value_bias


def attend_back(pair, qkv, grad_out, blended, log_total):
    rows = qkv.shape[0]
    padded = padded_rows(rows)

    def column(index):
        return pl.BlockSpec((rows, 128), lambda i: (0, index))

    return pl.pallas_call(
        functools.partial(attend_back_kernel, rows=rows, block=512),
        grid=(1,),
        in_specs=[
            column(3 * pair),
            column(3 * pair + 1),
            column(3 * pair + 2),
            column(pair),
            column(pair),
            pl.BlockSpec((2, 8, padded), lambda i: (pair, 0, 0)),
        ],
        out_specs=[
            pl.BlockSpec((padded, 384), lambda i: (0, 0)),
            pl.BlockSpec((8, 128), lambda i: (0, 0)),
        ],
        out_shape=[
            jax.ShapeDtypeStruct((rows, 384), LOW),
            jax.ShapeDtypeStruct((8, 128), WIDE),
        ],
        scratch_shapes=[
            pltpu.VMEM((2, padded, 128), LOW),
            pltpu.VMEM((padded, 128), LOW),
            pltpu.VMEM((padded, 128), LOW),
            pltpu.VMEM((2, padded, 128), LOW),
            pltpu.VMEM((128, padded), WIDE),
            pltpu.VMEM((2, 8, padded), WIDE),
        ],
        cost_estimate=cost(13, rows * 128 * 16),
    )(qkv, qkv, qkv, grad_out, blended, log_total)


def merge_kernel(*refs, count):
    parts, weight_ref, out_ref = refs[:count], refs[count], refs[count + 1]
    terms = jnp.concatenate([part[...] for part in parts], axis=1)
    total = lax.dot_general(terms, weight_ref[...], NT, preferred_element_type=WIDE)
    out_ref[...] = total.astype(LOW)


def merge(parts, weight):
    rows, width = parts[0].shape
    size = 512
    return pl.pallas_call(
        functools.partial(merge_kernel, count=len(parts)),
        grid=(pl.cdiv(rows, size),),
        in_specs=[pl.BlockSpec((size, width), lambda i: (i, 0))] * len(parts)
        + [pl.BlockSpec(weight.shape, lambda i: (0, 0))],
        out_specs=pl.BlockSpec((size, weight.shape[0]), lambda i: (i, 0)),
        out_shape=jax.ShapeDtypeStruct((rows, weight.shape[0]), LOW),
        cost_estimate=cost(6, rows * weight.shape[1] * 4),
        name="mg",
    )(*parts, weight)


def norm_two_kernel(frames_ref, own_ref, other_ref, gain_ref, shift_ref, bias_ref, out_ref, mid_ref):
    terms = own_ref[...].astype(WIDE) + other_ref[...].astype(WIDE)
    value = frames_ref[...].astype(WIDE) + terms + bias_ref[...]
    mid_ref[...] = value.astype(LOW)
    out_ref[...] = layer_norm(value, gain_ref[...], shift_ref[...])[0].astype(LOW)


def norm_two(frames, own, other, gain, shift, bias):
    rows, width = frames.shape
    whole = pl.BlockSpec((ROWS, width), lambda i: (i, 0))
    row = pl.BlockSpec((1, width), lambda i: (0, 0))
    return pl.pallas_call(
        norm_two_kernel,
        grid=(pl.cdiv(rows, ROWS),),
        in_specs=[whole] * 3 + [row] * 3,
        out_specs=[whole, whole],
        out_shape=[jax.ShapeDtypeStruct((rows, width), LOW)] * 2,
        cost_estimate=cost(6, rows * width * 10),
        name="n2",
    )(frames, own, other, gain, shift, bias)


def norm_back_kernel(
    core_ref, own_ref, other_ref, base_ref, gain_ref, value_ref, out_ref, *refs, rows
):
    *half_refs, sums_ref = refs
    step = pl.program_id(0)
    grad = own_ref[...].astype(WIDE) + other_ref[...].astype(WIDE)
    value = value_ref[...].astype(WIDE)
    centred = value - jnp.mean(value, axis=-1, keepdims=True)
    inverse = lax.rsqrt(jnp.mean(centred * centred, axis=-1, keepdims=True) + EPSILON)
    normed = centred * inverse
    scaled = grad * gain_ref[...]
    change = inverse * (
        scaled
        - jnp.mean(scaled, axis=-1, keepdims=True)
        - normed * jnp.mean(scaled * normed, axis=-1, keepdims=True)
    )
    total = base_ref[...].astype(WIDE) + change
    low = total.astype(LOW)
    out_ref[...] = low
    if half_refs:
        half = low.shape[1] // 2
        mine = jnp.where(core_ref[0] == 0, low[:, :half], low[:, half:])

        @pl.when(step < 2)
        def _():
            half_refs[0][...] = mine

        @pl.when(step >= 2)
        def _():
            half_refs[1][...] = mine

    valid = lax.broadcasted_iota(jnp.int32, grad.shape, 0) + step * grad.shape[0] < rows

    def column(summed):
        return jnp.sum(jnp.where(valid, summed, 0.0), axis=0, keepdims=True)

    sums = jnp.concatenate(
        [column(grad * normed), column(grad), column(total), jnp.zeros((5, grad.shape[1]), WIDE)],
        axis=0,
    )

    @pl.when(step == 0)
    def _():
        sums_ref[...] = sums

    @pl.when(step > 0)
    def _():
        sums_ref[...] += sums


def norm_back(core, own, other, base, gain, value, halves):
    rows, width = base.shape
    whole = pl.BlockSpec((ROWS, width), lambda i, c: (i, 0))
    row = pl.BlockSpec((1, width), lambda i, c: (0, 0))
    specs, shapes = [], []
    if halves:
        specs = [
            pl.BlockSpec((ROWS, width // 2), lambda i, c: (jnp.minimum(i, 1), 0)),
            pl.BlockSpec((ROWS, width // 2), lambda i, c: (jnp.maximum(i - 2, 0), 0)),
        ]
        shapes = [jax.ShapeDtypeStruct((2 * ROWS, width // 2), LOW)] * 2
    return pl.pallas_call(
        functools.partial(norm_back_kernel, rows=rows),
        grid_spec=pltpu.PrefetchScalarGridSpec(
            num_scalar_prefetch=1,
            grid=(pl.cdiv(rows, ROWS),),
            in_specs=[whole, whole, whole, row, whole],
            out_specs=[whole] + specs + [pl.BlockSpec((8, width), lambda i, c: (0, 0))],
        ),
        out_shape=[jax.ShapeDtypeStruct((rows, width), LOW)]
        + shapes
        + [jax.ShapeDtypeStruct((8, width), WIDE)],
        cost_estimate=cost(8, rows * width * 12),
    )(core.reshape(1), own, other, base, gain, value)


ROWS = 376
SHORT = 8


def take_clip_kernel(group_ref, both_ref, own_ref):
    def step(index, carry):
        span = pl.ds(pl.multiple_of(index * SHORT, SHORT), SHORT)
        both = both_ref[span]
        own = jnp.where(group_ref[0] == 0, both[:, 0, :].astype(WIDE), both[:, 1, :].astype(WIDE))
        own_ref[span, :] = own.astype(LOW)
        return carry

    lax.fori_loop(0, ROWS // SHORT, step, 0, unroll=False)


def take_clip(group, both):
    _, rows, width = both.shape
    return pl.pallas_call(
        take_clip_kernel,
        grid_spec=pltpu.PrefetchScalarGridSpec(
            num_scalar_prefetch=1,
            grid=(pl.cdiv(rows, ROWS),),
            in_specs=[pl.BlockSpec((ROWS, 2, width), lambda i, g: (i, 0, 0))],
            out_specs=pl.BlockSpec((ROWS, width), lambda i, g: (i, 0)),
        ),
        out_shape=jax.ShapeDtypeStruct((rows, width), LOW),
        cost_estimate=cost(9, rows * width * 6),
    )(group.reshape(1), both.transpose(1, 0, 2))


def both_clips_kernel(place_ref, own_ref, direct_ref, across_ref, *refs):
    out_ref = refs[-1]
    group, core = place_ref[0], place_ref[1]

    def step(index, carry):
        span = pl.ds(pl.multiple_of(index * SHORT, SHORT), SHORT)
        own = own_ref[span, :].astype(WIDE)
        direct = direct_ref[span, :].astype(WIDE)
        across = across_ref[span, :].astype(WIDE)
        first = jnp.where(core == 0, direct, across)
        second = jnp.where(core == 0, across, direct)
        other = jnp.concatenate([first, second], axis=1)
        out_ref[span, 0, :] = jnp.where(group == 0, own, other).astype(out_ref.dtype)
        out_ref[span, 1, :] = jnp.where(group == 0, other, own).astype(out_ref.dtype)
        return carry

    lax.fori_loop(0, ROWS // SHORT, step, 0, unroll=False)


def both_clips(own, direct, across, dtype, first, count, previous):
    tensor_index = lax.axis_index("tensor")
    place = jnp.stack([tensor_index // 2, tensor_index % 2])
    rows, width = own.shape
    narrow = pl.BlockSpec((ROWS, width // 2), lambda i, g: (i, 0))
    more = [] if previous is None else [previous]
    return pl.pallas_call(
        both_clips_kernel,
        grid_spec=pltpu.PrefetchScalarGridSpec(
            num_scalar_prefetch=1,
            grid=(count,),
            in_specs=[pl.BlockSpec((ROWS, width), lambda i, g: (i + first, 0)), narrow, narrow]
            + [pl.BlockSpec(memory_space=pl.ANY)] * len(more),
            out_specs=pl.BlockSpec((ROWS, 2, width), lambda i, g: (i + first, 0, 0)),
        ),
        out_shape=jax.ShapeDtypeStruct((rows, 2, width), dtype),
        input_output_aliases={4: 0} if more else {},
        cost_estimate=cost(2 * count, count * ROWS * width * 12),
    )(place, own, direct, across, *more)


def swap_tensor(value, distance):
    size = lax.axis_size("tensor")
    return lax.ppermute(value, "tensor", [(i, i ^ distance) for i in range(size)])


def swap_fsdp(value, distance):
    size = lax.axis_size("fsdp")
    return lax.ppermute(value, "fsdp", [(i, i ^ distance) for i in range(size)])


def swap_both(value):
    width = lax.axis_size("tensor")
    count = lax.axis_size("fsdp") * width
    pairs = [(i, ((i // width) ^ 1) * width + ((i % width) ^ 2)) for i in range(count)]
    return lax.ppermute(value, ("fsdp", "tensor"), pairs)


def after(value, *others):
    return lax.optimization_barrier((value, others))[0]


def spread_far(piece):
    far = lax.axis_size("fsdp") // 2
    return [piece] + [swap_fsdp(piece, 2 * i) for i in range(1, far)]


def spread_near(stack):
    far = stack.shape[0]
    return [
        (value, tuple((y, 2 * i + x) for i in range(far)))
        for y, x, value in (
            (0, 0, stack),
            (0, 1, swap_fsdp(stack, 1)),
            (1, 0, swap_tensor(stack, 2)),
            (1, 1, swap_both(stack)),
        )
    ]


def place_kernel(*refs, keys, finish):
    count = len(keys)
    stacks = refs[:count]
    outs, held, sem = refs[count:-2], refs[-2], refs[-1]
    mine = lax.axis_index("fsdp")
    group = lax.axis_index("tensor") // 2
    copies = []
    for stack, names in zip(stacks, keys):
        for i, (y, f) in enumerate(names):
            copy = pltpu.make_async_copy(
                stack.at[i], held.at[group ^ y, mine ^ f], sem.at[len(copies)]
            )
            copy.start()
            copies.append(copy)
    for copy in copies:
        copy.wait()
    finish(held, outs)


def place(parts, finish, out_shapes):
    size = lax.axis_size("fsdp")
    _, rows, columns = parts[0][0].shape
    total = sum(len(ks) for _, ks in parts)
    return pl.pallas_call(
        functools.partial(place_kernel, keys=tuple(ks for _, ks in parts), finish=finish),
        in_specs=[pl.BlockSpec(memory_space=pl.ANY)] * len(parts),
        out_specs=[pl.BlockSpec(memory_space=pltpu.VMEM)] * len(out_shapes),
        out_shape=[jax.ShapeDtypeStruct(*s) for s in out_shapes],
        scratch_shapes=[
            pltpu.VMEM((2, size, rows, columns), LOW),
            pltpu.SemaphoreType.DMA((total,)),
        ],
        cost_estimate=cost(3.5, 4 * size * rows * columns * 2),
    )(*[p for p, _ in parts])


def finish_qkv(held, outs, *, part, head_width, bias_part):
    _, size, _, _ = held.shape
    pairs = 2 * head_width // 128
    for f in range(size):
        a, b = held[0, f, :part], held[1, f, :part]
        wide = []
        for c in range(3):
            span = slice(c * head_width, (c + 1) * head_width)
            wide.append(jnp.concatenate([a[:, span], b[:, span]], axis=1))
        for p in range(pairs):
            for c in range(3):
                outs[0][f * part : (f + 1) * part, (3 * p + c) * 128 : (3 * p + c + 1) * 128] = (
                    wide[c][:, p * 128 : (p + 1) * 128]
                )
    rows = [[held[y, f, part:].astype(WIDE) for f in range(size)] for y in range(2)]
    full = [jnp.concatenate([r[:, :part] for r in rows[y]], axis=1) for y in range(2)]
    for i in range(6):
        outs[2 + i][...] = full[0][i : i + 1]
    for y in range(2):
        outs[8 + y][...] = full[y][6:7]
    biases = []
    for c in range(2):
        span = slice(c * bias_part, (c + 1) * bias_part)
        biases.append(jnp.concatenate([r[7:8, span] for y in range(2) for r in rows[y]], axis=1))
    nothing = jnp.zeros((1, 128), WIDE)
    for p in range(pairs):
        span = slice(p * 128, (p + 1) * 128)
        outs[1][:, 3 * p * 128 : (3 * p + 1) * 128] = biases[0][:, span]
        outs[1][:, (3 * p + 1) * 128 : (3 * p + 2) * 128] = nothing
        outs[1][:, (3 * p + 2) * 128 : (3 * p + 3) * 128] = biases[1][:, span]


def finish_up(held, outs, *, unit_width):
    _, size, part, _ = held.shape
    for f in range(size):
        rows = slice(f * part, (f + 1) * part)
        for y in range(2):
            outs[0][y, rows, :] = held[y, f, :, :unit_width]
        outs[1][rows, :] = jnp.concatenate(
            [held[0, f, :, unit_width:], held[1, f, :, unit_width:]], axis=1
        )


def finish_plain(held, outs):
    _, size, part, _ = held.shape
    for f in range(size):
        for y in range(2):
            outs[0][y, f * part : (f + 1) * part, :] = held[y, f]


def pick(value, axis, index):
    return lax.dynamic_index_in_dim(value, index, axis, keepdims=False)


def add_low(a, b):
    return (a.astype(WIDE) + b.astype(WIDE)).astype(LOW)


def near_far():
    mine = lax.axis_index("fsdp")
    return mine % 2, mine // 2


def fold_near(grads):
    low, _ = near_far()
    axis = grads.ndim - 3
    got = swap_fsdp(pick(grads, axis, 1 - low), 1)
    return pick(grads, axis, low), got


def fold_cross(grads):
    low, _ = near_far()
    group = lax.axis_index("tensor") // 2

    def at(y, x):
        return pick(pick(grads, 0, y), 1, x)

    side = swap_tensor(at(1 - group, low), 2)
    near = swap_fsdp(at(group, 1 - low), 1)
    both = swap_both(at(1 - group, 1 - low))
    return at(group, low), side, near, both


def cross_sum(own, side, near, both):
    total = own.astype(WIDE) + side.astype(WIDE)
    return (total + (near.astype(WIDE) + both.astype(WIDE))).astype(LOW)


def fold_far(grads):
    _, high = near_far()
    axis = grads.ndim - 3
    total = pick(grads, axis, high).astype(WIDE)
    for i in range(1, grads.shape[axis]):
        total = total + swap_fsdp(pick(grads, axis, high ^ i), 2 * i).astype(WIDE)
    return total


def fold_side(grads):
    group = lax.axis_index("tensor") // 2
    got = swap_tensor(pick(grads, 0, 1 - group), 2)
    return pick(grads, 0, group).astype(WIDE) + got.astype(WIDE)


def local(
    frames_in, cotangent, ln_first, w_qkv, b_qv, w_out, b_out, ln_second, w_fc1, b_fc1, w_fc2, b_fc2
):
    _, frame_count, model_width = frames_in.shape
    size = lax.axis_size("fsdp")
    part = w_qkv.shape[0]
    head_width = w_qkv.shape[2]
    unit_width = w_fc1.shape[1]
    bias_part = b_qv.shape[1]
    group = lax.axis_index("tensor") // 2
    core = lax.axis_index("tensor") % 2
    far = size // 2

    vectors = jnp.concatenate(
        [
            ln_first,
            ln_second,
            b_out[None],
            b_fc2[None],
            b_fc1[None],
            jnp.pad(b_qv.reshape(1, -1), ((0, 0), (0, part - 2 * bias_part))),
        ],
        axis=0,
    )
    vectors = jnp.pad(vectors, ((0, 0), (0, 3 * head_width - part)))
    qkv_piece = jnp.concatenate([w_qkv.reshape(part, 3 * head_width), vectors], axis=0)
    qkv_far = jnp.stack(spread_far(qkv_piece))
    frames_low = take_clip(group, frames_in)
    qkv_parts = spread_near(qkv_far)
    up_far = spread_far(jnp.concatenate([w_fc1, w_out.T], axis=1))
    down_far = spread_far(w_fc2.T)
    grad_low = take_clip(after(group, frames_low, qkv_far), cotangent)
    row = ((1, model_width), WIDE)
    (
        qkv_full, qkv_bias, gain_one, shift_one, gain_two, shift_two, out_bias, down_bias, *up_bias
    ) = place(
        qkv_parts,
        functools.partial(finish_qkv, part=part, head_width=head_width, bias_part=bias_part),
        [((model_width, 6 * head_width), LOW), ((1, 6 * head_width), WIDE)] + [row] * 8,
    )

    up_parts = spread_near(jnp.stack(after(up_far, qkv_full)))
    token_rows = frames_low.astype(WIDE)
    first_low = layer_norm(token_rows, gain_one, shift_one)[0].astype(LOW)
    qkv = (jnp.dot(first_low, qkv_full, preferred_element_type=WIDE) + qkv_bias).astype(LOW)
    down_parts = spread_near(jnp.stack(after(down_far, qkv)))
    attn_low, log_total = attend(qkv)

    up_all, out_full = place(
        up_parts,
        functools.partial(finish_up, unit_width=unit_width),
        [((2, model_width, unit_width), LOW), ((model_width, 2 * head_width), LOW)],
    )
    attn_terms = lax.dot_general(attn_low, out_full, NT, preferred_element_type=WIDE).astype(LOW)
    attn_other = swap_tensor(attn_terms, 1)
    second_low, middle = norm_two(
        frames_low, attn_terms, attn_other, gain_two, shift_two, out_bias
    )

    acts, slopes = [], []
    for i in range(2):
        pre_act = jnp.dot(second_low, up_all[i], preferred_element_type=WIDE) + up_bias[i]
        below = 0.5 * (1.0 + lax.erf(pre_act * 0.7071067811865476))
        acts.append((pre_act * below).astype(LOW))
        slopes.append(below + pre_act * jnp.exp(-0.5 * pre_act * pre_act) * 0.3989422804014327)
    grad_down = jnp.stack(
        [lax.dot_general(grad_low, acts[i], TN, preferred_element_type=WIDE) for i in range(2)]
    ).astype(LOW)
    down_cross = fold_cross(grad_down.reshape(2, far, 2, part, unit_width))

    (stack, keys), *others = down_parts
    (down_all,) = place(
        [(after(stack, grad_down), keys)] + others,
        finish_plain,
        [((2, model_width, unit_width), LOW)],
    )
    grads_pre, grad_up_bias = [], []
    for i in range(2):
        grad_pre = jnp.dot(grad_low, down_all[i], preferred_element_type=WIDE) * slopes[i]
        grad_up_bias.append(jnp.sum(grad_pre, axis=0))
        grads_pre.append(grad_pre.astype(LOW))
    second_terms = sum(
        lax.dot_general(grads_pre[i], up_all[i], NT, preferred_element_type=WIDE) for i in range(2)
    ).astype(LOW)
    second_other = swap_tensor(second_terms, 1)
    grad_up = jnp.stack(
        [
            lax.dot_general(
                after(second_low, second_terms), grads_pre[i], TN, preferred_element_type=WIDE
            )
            for i in range(2)
        ]
    ).astype(LOW)
    up_cross = fold_cross(grad_up.reshape(2, far, 2, part, unit_width))
    down_terms = sum(
        lax.dot_general(after(acts[i], grad_up), down_all[i], NT, preferred_element_type=WIDE)
        for i in range(2)
    ).astype(LOW)
    down_other = swap_tensor(down_terms, 1)
    result = middle.astype(WIDE) + (down_terms.astype(WIDE) + down_other.astype(WIDE)) + down_bias
    result = result.astype(LOW)

    middle_low, sums_two = norm_back(
        core, second_terms, second_other, grad_low, gain_two, middle, False
    )
    grad_attn = jnp.dot(middle_low, out_full, preferred_element_type=WIDE).astype(LOW)
    grad_out = lax.dot_general(middle_low, attn_low, TN, preferred_element_type=WIDE)
    out_fold = fold_near(grad_out.astype(LOW).reshape(far, 2, part, 2 * head_width))

    half = model_width // 2
    out_direct = swap_tensor(lax.dynamic_slice_in_dim(result, core * half, half, axis=1), 2)
    out_across = swap_tensor(out_direct, 1)

    pairs = 2 * head_width // 128
    grads_pair, bias_sums, folds = [], [], [out_fold]
    grad_attn = after(grad_attn, out_fold[0], result)
    for p in range(pairs):
        grad_pair, sums = attend_back(p, qkv, grad_attn, attn_low, log_total)
        grads_pair.append(grad_pair)
        bias_sums.append(sums)
        if p == 0:
            units = jnp.stack(
                [cross_sum(*after(c, grad_pair)) for c in (down_cross, up_cross)]
            )
            grad_attn = after(grad_attn, units)
        grad = lax.dot_general(first_low, grad_pair, TN, preferred_element_type=WIDE)
        folds.append(fold_near(grad.astype(LOW).reshape(far, 2, part, 384)))
        if p + 1 < pairs:
            grad_attn = after(grad_attn, folds[-1][0])

    first_terms = merge(grads_pair, qkv_full)
    tail = jnp.concatenate([add_low(own, after(got, first_terms)) for own, got in folds], axis=1)
    tail = fold_far(tail)
    first_other = swap_tensor(first_terms, 1)
    rows_low, *halves, sums_one = norm_back(
        core, first_terms, first_other, middle_low, gain_one, frames_low, True
    )
    direct = [swap_tensor(h, 2) for h in halves]
    across = [swap_tensor(d, 1) for d in direct]

    ones = jnp.ones((8, frame_count), LOW)
    grad_down_bias = jnp.dot(ones, after(grad_low, rows_low), preferred_element_type=WIDE)[0:1]
    shared = jnp.concatenate([sums_one[0:2], sums_two[0:3], grad_down_bias], axis=0)
    sums = jnp.concatenate([b[0:2] for b in bias_sums], axis=1)
    sums = sums.reshape(2, 2, size, bias_part).transpose(2, 1, 0, 3)
    rows = jnp.concatenate([shared] + [b[None] for b in grad_up_bias], axis=0)
    rows = rows.reshape(8, size, part).transpose(1, 0, 2)
    sums = jnp.pad(
        sums.reshape(size, 2, 2 * bias_part), ((0, 0), (0, 0), (0, part - 2 * bias_part))
    )
    vectors = jnp.concatenate([rows, sums], axis=1)
    vectors = jnp.pad(vectors, ((0, 0), (0, 6), (0, 128 - part))).astype(LOW)
    vectors = fold_far(add_low(*fold_near(vectors.reshape(far, 2, 16, 128))))

    blocks = pl.cdiv(frame_count, ROWS)
    frames_out = both_clips(result, out_direct, out_across, LOW, 0, blocks, None)
    grad_frames = None
    for i in range(2):
        grad_frames = both_clips(rows_low, direct[i], across[i], WIDE, 2 * i, 2, grad_frames)

    units = fold_far(units)
    grad_down, grad_up = units[0].T, units[1]
    per_pair = tail[part:].reshape(pairs, part, 384)
    vectors = vectors[:, :part]
    grad_qkv = per_pair.reshape(pairs, part, 3, 128).transpose(2, 1, 0, 3)
    heads = jnp.concatenate([tail[:part][None], grad_qkv.reshape(3, part, 2 * head_width)])
    heads = heads.reshape(4 * part, 2, head_width).transpose(1, 0, 2)
    by_group = jnp.stack(
        [jnp.concatenate([vectors[:6], vectors[6 + g : 7 + g], vectors[8 + g : 9 + g]]) for g in range(2)]
    )
    by_group = jnp.pad(by_group, ((0, 0), (0, 0), (0, head_width - part)))
    heads = fold_side(jnp.concatenate([heads, by_group], axis=1).astype(LOW))
    grad_out = heads[:part].T
    grad_qkv = heads[part : 4 * part].reshape(3, part, head_width).transpose(1, 0, 2)
    slices = heads[4 * part :, :part]

    return (
        frames_out.transpose(1, 0, 2),
        grad_frames.transpose(1, 0, 2),
        slices[0:2],
        grad_qkv,
        slices[7, : 2 * bias_part].reshape(2, bias_part),
        grad_out,
        slices[4],
        slices[2:4],
        grad_up,
        slices[6],
        grad_down,
        slices[5],
    )


def solution(mesh):
    in_specs = (
        P("fsdp", None, None),
        P("fsdp", None, None),
        P(None, "fsdp"),
        P("fsdp", None, "tensor"),
        P(None, ("tensor", "fsdp")),
        P("tensor", "fsdp"),
        P("fsdp"),
        P(None, "fsdp"),
        P("fsdp", "tensor"),
        P(("tensor", "fsdp")),
        P("tensor", "fsdp"),
        P("fsdp"),
    )
    out_specs = (
        P("fsdp", None, None),
        P("fsdp", None, None),
        P(None, "fsdp"),
        P("fsdp", None, "tensor"),
        P(None, ("tensor", "fsdp")),
        P("tensor", "fsdp"),
        P("fsdp"),
        P(None, "fsdp"),
        P("fsdp", "tensor"),
        P(("tensor", "fsdp")),
        P("tensor", "fsdp"),
        P("fsdp"),
    )
    return jax.shard_map(local, mesh=mesh, in_specs=in_specs, out_specs=out_specs, check_vma=False)
```

```python
import functools

import jax
import jax.numpy as jnp
from jax import lax
from jax.experimental import pallas as pl
from jax.experimental.pallas import tpu as pltpu
from jax.sharding import PartitionSpec as P


HEAD_DIM = 64
EPSILON = 1e-05
LOW = jnp.bfloat16
WIDE = jnp.float32
NEGATIVE = -1e30
NT = (((1,), (1,)), ((), ()))
TN = (((0,), (0,)), ((), ()))


def layer_norm(values, norm_gain, norm_shift):
    centre = jnp.mean(values, axis=-1, keepdims=True)
    centred = values - centre
    inverse = lax.rsqrt(jnp.mean(centred * centred, axis=-1, keepdims=True) + EPSILON)
    normed = centred * inverse
    return (normed * norm_gain + norm_shift, normed, inverse)


def cost(microseconds, size):
    return pl.CostEstimate(
        flops=int(microseconds * 1e9), transcendentals=0, bytes_accessed=int(size)
    )


def padded_rows(count):
    return -(-count // 512) * 512


def attend_kernel(q_ref, k_ref, v_ref, o_ref, l_ref, q_all, k_all, v_all, *, block):
    rows = q_ref.shape[0]
    padded = q_all.shape[0]
    fill = jnp.zeros((padded - rows, 128), LOW)
    q_all[...] = jnp.concatenate([q_ref[...] * LOW(HEAD_DIM**-0.5), fill], axis=0)
    k_all[...] = jnp.concatenate([k_ref[...], fill], axis=0)
    v_all[:, :128] = jnp.concatenate([v_ref[...], fill], axis=0)
    v_all[:, 128:] = jnp.ones((padded, 128), LOW)
    valid = lax.broadcasted_iota(jnp.int32, (block, 256), 1) < rows - (padded - 256)
    upper = lax.broadcasted_iota(jnp.int32, (block, 128), 1) >= HEAD_DIM
    for step in range(padded // block):
        start = step * block
        parts = []
        for head in range(2):
            q_head = jnp.where(upper == (head == 1), q_all[start : start + block, :], LOW(0))
            scores = lax.dot_general(q_head, k_all[...], NT, preferred_element_type=WIDE)
            scores = jnp.concatenate(
                [
                    scores[:, : padded - 256],
                    jnp.where(valid, scores[:, padded - 256 :], NEGATIVE),
                ],
                axis=1,
            )
            highest = jnp.max(scores, axis=1, keepdims=True)
            weights = jnp.exp(scores - highest).astype(LOW)
            blended = jnp.dot(weights, v_all[...], preferred_element_type=WIDE)
            total = blended[:, 128:]
            parts.append(blended[:, :128] * (1.0 / total))
            log_total = (highest + jnp.log(total)).T
            l_ref[head, :, start : start + block] = log_total[0:8, :]
        merged = jnp.where(upper, parts[1], parts[0]).astype(LOW)
        count = min(block, rows - start)
        o_ref[start : start + count, :] = merged[:count]


def attend(qkv):
    rows, width = qkv.shape
    pairs = width // 3 // 128
    padded = padded_rows(rows)

    def column(which):
        return pl.BlockSpec((rows, 128), lambda p: (0, 3 * p + which))

    return pl.pallas_call(
        functools.partial(attend_kernel, block=512),
        grid=(pairs,),
        in_specs=[column(0), column(1), column(2)],
        out_specs=[
            pl.BlockSpec((rows, 128), lambda p: (0, p)),
            pl.BlockSpec((2, 8, padded), lambda p: (p, 0, 0)),
        ],
        out_shape=[
            jax.ShapeDtypeStruct((rows, width // 3), LOW),
            jax.ShapeDtypeStruct((2 * pairs, 8, padded), WIDE),
        ],
        scratch_shapes=[pltpu.VMEM((padded, 128), LOW)] * 2 + [pltpu.VMEM((padded, 256), LOW)],
        cost_estimate=cost(22, rows * width * 3),
        name="fa",
    )(qkv, qkv, qkv)


def attend_back_kernel(
    q_ref, k_ref, v_ref, g_ref, o_ref, l_ref, d_ref, db_ref,
    q_all, k_all, v_all, g_all, dq_turned, centre_all, *, rows, block,
):
    padded = k_all.shape[0]
    fill = jnp.zeros((padded - rows, 128), LOW)

    def pad(value):
        return jnp.concatenate([value, fill], axis=0)

    upper = lax.broadcasted_iota(jnp.int32, (padded, 128), 1) >= HEAD_DIM
    upper8 = lax.broadcasted_iota(jnp.int32, (8, 128), 1) >= HEAD_DIM
    upper_block = lax.broadcasted_iota(jnp.int32, (block, 128), 1) >= HEAD_DIM
    row_block = lax.broadcasted_iota(jnp.int32, (block, 128), 0)
    scale = HEAD_DIM**-0.5
    keys = k_ref[...]
    k_all[...] = jnp.concatenate([keys, keys[: padded - rows]], axis=0)
    v_all[...] = pad(v_ref[...])
    q_full = pad(q_ref[...] * LOW(scale))
    g_full = pad(g_ref[...])
    product = g_full.astype(WIDE) * pad(o_ref[...]).astype(WIDE)
    coarse = product.astype(LOW)
    fine = (product - coarse.astype(WIDE)).astype(LOW)
    for head in range(2):
        mine = upper == (head == 1)
        q_all[head] = jnp.where(mine, q_full, LOW(0))
        g_all[head] = jnp.where(mine, g_full, LOW(0))
        ones = jnp.where(upper8 == (head == 1), 1.0, 0.0).astype(LOW)
        centre_all[head] = lax.dot_general(
            ones, coarse, NT, preferred_element_type=WIDE
        ) + lax.dot_general(ones, fine, NT, preferred_element_type=WIDE)
    dq_turned[...] = jnp.zeros_like(dq_turned)

    def step(index, value_bias):
        span = pl.ds(pl.multiple_of(index * block, block), block)
        keys, values = k_all[span, :], v_all[span, :]
        real = row_block < rows - index * block
        grad_values = grad_keys = grad_query = None
        for head in range(2):
            scores = lax.dot_general(keys, q_all[head], NT, preferred_element_type=WIDE)
            chances = jnp.exp(scores - l_ref[head, 0:1, :])
            grad_weights = lax.dot_general(
                values, g_all[head], NT, preferred_element_type=WIDE
            )
            grad_scores = (chances * (grad_weights - centre_all[head, 0:1, :])).astype(LOW)
            from_values = jnp.dot(
                chances.astype(LOW), g_all[head], preferred_element_type=WIDE
            )
            from_keys = jnp.dot(grad_scores, q_all[head], preferred_element_type=WIDE)
            keys_head = jnp.where(real & (upper_block == (head == 1)), keys, LOW(0))
            from_query = jnp.dot(keys_head.T, grad_scores, preferred_element_type=WIDE)
            if head == 0:
                grad_values, grad_keys, grad_query = from_values, from_keys, from_query
            else:
                grad_values = grad_values + from_values
                grad_keys = grad_keys + from_keys
                grad_query = grad_query + from_query
        dq_turned[...] += grad_query
        d_ref[span, 128:256] = grad_keys.astype(LOW)
        d_ref[span, 256:384] = grad_values.astype(LOW)
        return value_bias + jnp.sum(jnp.where(real, grad_values, 0.0), axis=0, keepdims=True)

    value_bias = lax.fori_loop(0, padded // block, step, jnp.zeros((1, 128), WIDE))
    grad_query = (dq_turned[...] * scale).T
    d_ref[:, 0:128] = grad_query.astype(LOW)
    db_ref[0:1, :] = jnp.sum(grad_query, axis=0, keepdims=True)
    db_ref[1:2, :] = value_bias


def attend_back(pair, qkv, grad_out, blended, log_total):
    rows = qkv.shape[0]
    padded = padded_rows(rows)

    def column(index):
        return pl.BlockSpec((rows, 128), lambda i: (0, index))

    return pl.pallas_call(
        functools.partial(attend_back_kernel, rows=rows, block=512),
        grid=(1,),
        in_specs=[
            column(3 * pair),
            column(3 * pair + 1),
            column(3 * pair + 2),
            column(pair),
            column(pair),
            pl.BlockSpec((2, 8, padded), lambda i: (pair, 0, 0)),
        ],
        out_specs=[
            pl.BlockSpec((padded, 384), lambda i: (0, 0)),
            pl.BlockSpec((8, 128), lambda i: (0, 0)),
        ],
        out_shape=[
            jax.ShapeDtypeStruct((rows, 384), LOW),
            jax.ShapeDtypeStruct((8, 128), WIDE),
        ],
        scratch_shapes=[
            pltpu.VMEM((2, padded, 128), LOW),
            pltpu.VMEM((padded, 128), LOW),
            pltpu.VMEM((padded, 128), LOW),
            pltpu.VMEM((2, padded, 128), LOW),
            pltpu.VMEM((128, padded), WIDE),
            pltpu.VMEM((2, 8, padded), WIDE),
        ],
        cost_estimate=cost(13, rows * 128 * 16),
    )(qkv, qkv, qkv, grad_out, blended, log_total)


def merge_kernel(*refs, count):
    parts, weight_ref, out_ref = refs[:count], refs[count], refs[count + 1]
    terms = jnp.concatenate([part[...] for part in parts], axis=1)
    total = lax.dot_general(terms, weight_ref[...], NT, preferred_element_type=WIDE)
    out_ref[...] = total.astype(LOW)


def merge(parts, weight):
    rows, width = parts[0].shape
    size = 512
    return pl.pallas_call(
        functools.partial(merge_kernel, count=len(parts)),
        grid=(pl.cdiv(rows, size),),
        in_specs=[pl.BlockSpec((size, width), lambda i: (i, 0))] * len(parts)
        + [pl.BlockSpec(weight.shape, lambda i: (0, 0))],
        out_specs=pl.BlockSpec((size, weight.shape[0]), lambda i: (i, 0)),
        out_shape=jax.ShapeDtypeStruct((rows, weight.shape[0]), LOW),
        cost_estimate=cost(6, rows * weight.shape[1] * 4),
        name="mg",
    )(*parts, weight)


def norm_two_kernel(frames_ref, own_ref, other_ref, gain_ref, shift_ref, bias_ref, out_ref, mid_ref):
    terms = own_ref[...].astype(WIDE) + other_ref[...].astype(WIDE)
    value = frames_ref[...].astype(WIDE) + terms + bias_ref[...]
    mid_ref[...] = value.astype(LOW)
    out_ref[...] = layer_norm(value, gain_ref[...], shift_ref[...])[0].astype(LOW)


def norm_two(frames, own, other, gain, shift, bias):
    rows, width = frames.shape
    whole = pl.BlockSpec((ROWS, width), lambda i: (i, 0))
    row = pl.BlockSpec((1, width), lambda i: (0, 0))
    return pl.pallas_call(
        norm_two_kernel,
        grid=(pl.cdiv(rows, ROWS),),
        in_specs=[whole] * 3 + [row] * 3,
        out_specs=[whole, whole],
        out_shape=[jax.ShapeDtypeStruct((rows, width), LOW)] * 2,
        cost_estimate=cost(6, rows * width * 10),
        name="n2",
    )(frames, own, other, gain, shift, bias)


def norm_back_kernel(
    core_ref, own_ref, other_ref, base_ref, gain_ref, value_ref, out_ref, *refs, rows
):
    *half_refs, sums_ref = refs
    step = pl.program_id(0)
    grad = own_ref[...].astype(WIDE) + other_ref[...].astype(WIDE)
    value = value_ref[...].astype(WIDE)
    centred = value - jnp.mean(value, axis=-1, keepdims=True)
    inverse = lax.rsqrt(jnp.mean(centred * centred, axis=-1, keepdims=True) + EPSILON)
    normed = centred * inverse
    scaled = grad * gain_ref[...]
    change = inverse * (
        scaled
        - jnp.mean(scaled, axis=-1, keepdims=True)
        - normed * jnp.mean(scaled * normed, axis=-1, keepdims=True)
    )
    base = base_ref[...].astype(WIDE)
    total = base + change
    low = total.astype(LOW)
    out_ref[...] = low
    if half_refs:
        half = low.shape[1] // 2
        mine = jnp.where(core_ref[0] == 0, low[:, :half], low[:, half:])

        @pl.when(step < 2)
        def _():
            half_refs[0][...] = mine

        @pl.when(step >= 2)
        def _():
            half_refs[1][...] = mine

    valid = lax.broadcasted_iota(jnp.int32, grad.shape, 0) + step * grad.shape[0] < rows

    def column(summed):
        return jnp.sum(jnp.where(valid, summed, 0.0), axis=0, keepdims=True)

    sums = jnp.concatenate(
        [
            column(grad * normed),
            column(grad),
            column(total),
            column(base),
            jnp.zeros((4, grad.shape[1]), WIDE),
        ],
        axis=0,
    )

    @pl.when(step == 0)
    def _():
        sums_ref[...] = sums

    @pl.when(step > 0)
    def _():
        sums_ref[...] += sums


def norm_back(core, own, other, base, gain, value, halves):
    rows, width = base.shape
    whole = pl.BlockSpec((ROWS, width), lambda i, c: (i, 0))
    row = pl.BlockSpec((1, width), lambda i, c: (0, 0))
    specs, shapes = [], []
    if halves:
        specs = [
            pl.BlockSpec((ROWS, width // 2), lambda i, c: (jnp.minimum(i, 1), 0)),
            pl.BlockSpec((ROWS, width // 2), lambda i, c: (jnp.maximum(i - 2, 0), 0)),
        ]
        shapes = [jax.ShapeDtypeStruct((2 * ROWS, width // 2), LOW)] * 2
    return pl.pallas_call(
        functools.partial(norm_back_kernel, rows=rows),
        grid_spec=pltpu.PrefetchScalarGridSpec(
            num_scalar_prefetch=1,
            grid=(pl.cdiv(rows, ROWS),),
            in_specs=[whole, whole, whole, row, whole],
            out_specs=[whole] + specs + [pl.BlockSpec((8, width), lambda i, c: (0, 0))],
        ),
        out_shape=[jax.ShapeDtypeStruct((rows, width), LOW)]
        + shapes
        + [jax.ShapeDtypeStruct((8, width), WIDE)],
        cost_estimate=cost(8, rows * width * 12),
    )(core.reshape(1), own, other, base, gain, value)


ROWS = 376
SHORT = 8


def take_clip_kernel(group_ref, both_ref, own_ref):
    def step(index, carry):
        span = pl.ds(pl.multiple_of(index * SHORT, SHORT), SHORT)
        both = both_ref[span]
        own = jnp.where(group_ref[0] == 0, both[:, 0, :].astype(WIDE), both[:, 1, :].astype(WIDE))
        own_ref[span, :] = own.astype(LOW)
        return carry

    lax.fori_loop(0, ROWS // SHORT, step, 0, unroll=False)


def take_clip(group, both):
    _, rows, width = both.shape
    return pl.pallas_call(
        take_clip_kernel,
        grid_spec=pltpu.PrefetchScalarGridSpec(
            num_scalar_prefetch=1,
            grid=(pl.cdiv(rows, ROWS),),
            in_specs=[pl.BlockSpec((ROWS, 2, width), lambda i, g: (i, 0, 0))],
            out_specs=pl.BlockSpec((ROWS, width), lambda i, g: (i, 0)),
        ),
        out_shape=jax.ShapeDtypeStruct((rows, width), LOW),
        cost_estimate=cost(9, rows * width * 6),
    )(group.reshape(1), both.transpose(1, 0, 2))


def both_clips_kernel(place_ref, own_ref, direct_ref, across_ref, *refs):
    out_ref = refs[-1]
    group, core = place_ref[0], place_ref[1]

    def step(index, carry):
        span = pl.ds(pl.multiple_of(index * SHORT, SHORT), SHORT)
        own = own_ref[span, :].astype(WIDE)
        direct = direct_ref[span, :].astype(WIDE)
        across = across_ref[span, :].astype(WIDE)
        first = jnp.where(core == 0, direct, across)
        second = jnp.where(core == 0, across, direct)
        other = jnp.concatenate([first, second], axis=1)
        out_ref[span, 0, :] = jnp.where(group == 0, own, other).astype(out_ref.dtype)
        out_ref[span, 1, :] = jnp.where(group == 0, other, own).astype(out_ref.dtype)
        return carry

    lax.fori_loop(0, ROWS // SHORT, step, 0, unroll=False)


def both_clips(own, direct, across, dtype, first, count, previous):
    tensor_index = lax.axis_index("tensor")
    place = jnp.stack([tensor_index // 2, tensor_index % 2])
    rows, width = own.shape
    narrow = pl.BlockSpec((ROWS, width // 2), lambda i, g: (i, 0))
    more = [] if previous is None else [previous]
    return pl.pallas_call(
        both_clips_kernel,
        grid_spec=pltpu.PrefetchScalarGridSpec(
            num_scalar_prefetch=1,
            grid=(count,),
            in_specs=[pl.BlockSpec((ROWS, width), lambda i, g: (i + first, 0)), narrow, narrow]
            + [pl.BlockSpec(memory_space=pl.ANY)] * len(more),
            out_specs=pl.BlockSpec((ROWS, 2, width), lambda i, g: (i + first, 0, 0)),
        ),
        out_shape=jax.ShapeDtypeStruct((rows, 2, width), dtype),
        input_output_aliases={4: 0} if more else {},
        cost_estimate=cost(2 * count, count * ROWS * width * 12),
    )(place, own, direct, across, *more)


def swap_tensor(value, distance):
    size = lax.axis_size("tensor")
    return lax.ppermute(value, "tensor", [(i, i ^ distance) for i in range(size)])


def swap_fsdp(value, distance):
    size = lax.axis_size("fsdp")
    return lax.ppermute(value, "fsdp", [(i, i ^ distance) for i in range(size)])


def swap_both(value):
    width = lax.axis_size("tensor")
    count = lax.axis_size("fsdp") * width
    pairs = [(i, ((i // width) ^ 1) * width + ((i % width) ^ 2)) for i in range(count)]
    return lax.ppermute(value, ("fsdp", "tensor"), pairs)


def after(value, *others):
    return lax.optimization_barrier((value, others))[0]


def spread_far(piece):
    far = lax.axis_size("fsdp") // 2
    return [piece] + [swap_fsdp(piece, 2 * i) for i in range(1, far)]


def spread_near(stack):
    far = stack.shape[0]
    return [
        (value, tuple((y, 2 * i + x) for i in range(far)))
        for y, x, value in (
            (0, 0, stack),
            (0, 1, swap_fsdp(stack, 1)),
            (1, 0, swap_tensor(stack, 2)),
            (1, 1, swap_both(stack)),
        )
    ]


def place_kernel(*refs, keys, finish):
    count = len(keys)
    stacks = refs[:count]
    outs, held, sem = refs[count:-2], refs[-2], refs[-1]
    mine = lax.axis_index("fsdp")
    group = lax.axis_index("tensor") // 2
    copies = []
    for stack, names in zip(stacks, keys):
        for i, (y, f) in enumerate(names):
            copy = pltpu.make_async_copy(
                stack.at[i], held.at[group ^ y, mine ^ f], sem.at[len(copies)]
            )
            copy.start()
            copies.append(copy)
    for copy in copies:
        copy.wait()
    finish(held, outs)


def place(parts, finish, out_shapes):
    size = lax.axis_size("fsdp")
    _, rows, columns = parts[0][0].shape
    total = sum(len(ks) for _, ks in parts)
    return pl.pallas_call(
        functools.partial(place_kernel, keys=tuple(ks for _, ks in parts), finish=finish),
        in_specs=[pl.BlockSpec(memory_space=pl.ANY)] * len(parts),
        out_specs=[pl.BlockSpec(memory_space=pltpu.VMEM)] * len(out_shapes),
        out_shape=[jax.ShapeDtypeStruct(*s) for s in out_shapes],
        scratch_shapes=[
            pltpu.VMEM((2, size, rows, columns), LOW),
            pltpu.SemaphoreType.DMA((total,)),
        ],
        cost_estimate=cost(3.5, 4 * size * rows * columns * 2),
    )(*[p for p, _ in parts])


def finish_qkv(held, outs, *, part, head_width, bias_part):
    _, size, _, _ = held.shape
    pairs = 2 * head_width // 128
    for f in range(size):
        a, b = held[0, f, :part], held[1, f, :part]
        wide = []
        for c in range(3):
            span = slice(c * head_width, (c + 1) * head_width)
            wide.append(jnp.concatenate([a[:, span], b[:, span]], axis=1))
        for p in range(pairs):
            for c in range(3):
                outs[0][f * part : (f + 1) * part, (3 * p + c) * 128 : (3 * p + c + 1) * 128] = (
                    wide[c][:, p * 128 : (p + 1) * 128]
                )
    rows = [[held[y, f, part:].astype(WIDE) for f in range(size)] for y in range(2)]
    full = [jnp.concatenate([r[:, :part] for r in rows[y]], axis=1) for y in range(2)]
    for i in range(6):
        outs[2 + i][...] = full[0][i : i + 1]
    outs[8][...] = jnp.concatenate([full[0][6:7], full[1][6:7]], axis=1)
    biases = []
    for c in range(2):
        span = slice(c * bias_part, (c + 1) * bias_part)
        biases.append(jnp.concatenate([r[7:8, span] for y in range(2) for r in rows[y]], axis=1))
    nothing = jnp.zeros((1, 128), WIDE)
    for p in range(pairs):
        span = slice(p * 128, (p + 1) * 128)
        outs[1][:, 3 * p * 128 : (3 * p + 1) * 128] = biases[0][:, span]
        outs[1][:, (3 * p + 1) * 128 : (3 * p + 2) * 128] = nothing
        outs[1][:, (3 * p + 2) * 128 : (3 * p + 3) * 128] = biases[1][:, span]


def finish_up(held, outs, *, unit_width):
    _, size, part, _ = held.shape
    for f in range(size):
        rows = slice(f * part, (f + 1) * part)
        for y in range(2):
            outs[0][rows, y * unit_width : (y + 1) * unit_width] = held[y, f, :, :unit_width]
        outs[1][rows, :] = jnp.concatenate(
            [held[0, f, :, unit_width:], held[1, f, :, unit_width:]], axis=1
        )


def finish_plain(held, outs):
    _, size, part, width = held.shape
    for f in range(size):
        for y in range(2):
            outs[0][f * part : (f + 1) * part, y * width : (y + 1) * width] = held[y, f]


def pick(value, axis, index):
    return lax.dynamic_index_in_dim(value, index, axis, keepdims=False)


def add_low(a, b):
    return (a.astype(WIDE) + b.astype(WIDE)).astype(LOW)


def near_far():
    mine = lax.axis_index("fsdp")
    return mine % 2, mine // 2


def fold_near(grads):
    low, _ = near_far()
    axis = grads.ndim - 3
    got = swap_fsdp(pick(grads, axis, 1 - low), 1)
    return pick(grads, axis, low), got


def fold_cross(grads):
    low, _ = near_far()
    group = lax.axis_index("tensor") // 2
    size = lax.axis_size("fsdp")
    part, columns = grads.shape[0] // size, grads.shape[1] // 2
    grads = grads.reshape(size // 2, 2, part, 2 * columns)

    def at(y, x):
        span = (size // 2, 1, part, columns)
        return lax.dynamic_slice(grads, (0, x, 0, y * columns), span)[:, 0]

    side = swap_tensor(at(1 - group, low), 2)
    near = swap_fsdp(at(group, 1 - low), 1)
    both = swap_both(at(1 - group, 1 - low))
    return at(group, low), side, near, both


def cross_sum(own, side, near, both):
    total = own.astype(WIDE) + side.astype(WIDE)
    return (total + (near.astype(WIDE) + both.astype(WIDE))).astype(LOW)


def fold_far(grads):
    _, high = near_far()
    axis = grads.ndim - 3
    total = pick(grads, axis, high).astype(WIDE)
    for i in range(1, grads.shape[axis]):
        total = total + swap_fsdp(pick(grads, axis, high ^ i), 2 * i).astype(WIDE)
    return total


VMEM = pl.BlockSpec(memory_space=pltpu.VMEM)
SMEM = pl.BlockSpec(memory_space=pltpu.SMEM)


def small_call(kernel, place, inputs, shapes, scratch):
    return pl.pallas_call(
        kernel,
        in_specs=[SMEM] + [VMEM] * len(inputs),
        out_specs=[VMEM] * len(shapes),
        out_shape=[jax.ShapeDtypeStruct(*s) for s in shapes],
        scratch_shapes=scratch,
        cost_estimate=cost(1.5, 4 << 20),
    )(place, *inputs)


def vector_kernel(place_ref, one_ref, two_ref, up_ref, *refs, part, bias_part, head_width):
    *bias_refs, own_ref, sent_ref, held = refs
    width = one_ref.shape[1]
    rows = jnp.concatenate(
        [one_ref[0:2, :], two_ref[0:4, :], up_ref[:, :width], up_ref[:, width:]], axis=0
    )
    query = jnp.concatenate([b[0:1, :] for b in bias_refs], axis=1)
    value = jnp.concatenate([b[1:2, :] for b in bias_refs], axis=1)
    held[...] = jnp.zeros_like(held)
    for f in range(held.shape[0]):
        held[f, 0:8, 0:part] = rows[:, f * part : (f + 1) * part]
        for y in range(2):
            start = y * head_width + f * bias_part
            span = slice(start, start + bias_part)
            held[f, 8 + y : 9 + y, 0 : 2 * bias_part] = jnp.concatenate(
                [query[:, span], value[:, span]], axis=1
            )
    first = place_ref[0] % 2 == 0
    for i in range(own_ref.shape[0]):
        even, odd = held[2 * i], held[2 * i + 1]
        own_ref[i] = jnp.where(first, even, odd).astype(LOW)
        sent_ref[i] = jnp.where(first, odd, even).astype(LOW)


def tail_kernel(place_ref, *refs, count):
    folds, outs = refs[: 2 * count], refs[2 * count :]
    high = place_ref[0] // 2
    part = folds[0].shape[1]
    for i, out in enumerate(outs):
        for k in range(count):
            total = folds[2 * k][high ^ i].astype(WIDE) + folds[2 * k + 1][high ^ i].astype(WIDE)
            out[k * part : (k + 1) * part, :] = total.astype(LOW)


def sum_of(refs):
    total = refs[0][...].astype(WIDE)
    for ref in refs[1:]:
        total = total + ref[...].astype(WIDE)
    return total


def heads_kernel(place_ref, *refs, far, part, head_width):
    tail = sum_of(refs[:far])
    vectors = sum_of(refs[far : 2 * far])
    own_ref, sent_ref = refs[2 * far :]
    first = place_ref[1] == 0
    pairs = tail.shape[0] // part - 1
    blocks = [tail[:part, :]]
    for c in range(3):
        span = slice(c * 128, (c + 1) * 128)
        blocks.append(
            jnp.concatenate(
                [tail[(1 + p) * part : (2 + p) * part, span] for p in range(pairs)], axis=1
            )
        )
    for k, block in enumerate(blocks):
        rows = slice(k * part, (k + 1) * part)
        low, high = block[:, :head_width], block[:, head_width:]
        own_ref[rows, :] = jnp.where(first, low, high).astype(LOW)
        sent_ref[rows, :] = jnp.where(first, high, low).astype(LOW)
    own_ref[4 * part :, :] = jnp.zeros((8, head_width), LOW)
    sent_ref[4 * part :, :] = jnp.zeros((8, head_width), LOW)
    low, high = [
        jnp.concatenate([vectors[:6], vectors[6 + y : 7 + y], vectors[8 + y : 9 + y]], axis=0)
        for y in range(2)
    ]
    own_ref[4 * part :, 0:128] = jnp.where(first, low, high).astype(LOW)
    sent_ref[4 * part :, 0:128] = jnp.where(first, high, low).astype(LOW)


def final_kernel(place_ref, own_ref, got_ref, *outs, part, bias_part):
    total = own_ref[...].astype(WIDE) + got_ref[...].astype(WIDE)
    out_ref, qkv_ref, one_ref, two_ref, *rows_refs, bias_ref = outs
    out_ref[...] = total[:part, :].T
    for c in range(3):
        qkv_ref[c] = total[(1 + c) * part : (2 + c) * part, :]
    vectors = total[4 * part :, :part]
    one_ref[...] = vectors[0:2]
    two_ref[...] = vectors[2:4]
    for i, ref in enumerate(rows_refs):
        ref[...] = vectors[4 + i : 5 + i]
    bias_ref[...] = jnp.concatenate(
        [vectors[7:8, :bias_part], vectors[7:8, bias_part : 2 * bias_part]], axis=0
    )


def local(
    frames_in, cotangent, ln_first, w_qkv, b_qv, w_out, b_out, ln_second, w_fc1, b_fc1, w_fc2, b_fc2
):
    _, frame_count, model_width = frames_in.shape
    size = lax.axis_size("fsdp")
    part = w_qkv.shape[0]
    head_width = w_qkv.shape[2]
    unit_width = w_fc1.shape[1]
    bias_part = b_qv.shape[1]
    group = lax.axis_index("tensor") // 2
    core = lax.axis_index("tensor") % 2
    mine = lax.axis_index("fsdp")
    far = size // 2

    vectors = jnp.concatenate(
        [
            ln_first,
            ln_second,
            b_out[None],
            b_fc2[None],
            b_fc1[None],
            jnp.pad(b_qv.reshape(1, -1), ((0, 0), (0, part - 2 * bias_part))),
        ],
        axis=0,
    )
    vectors = jnp.pad(vectors, ((0, 0), (0, 3 * head_width - part)))
    qkv_piece = jnp.concatenate([w_qkv.reshape(part, 3 * head_width), vectors], axis=0)
    qkv_far = jnp.stack(spread_far(qkv_piece))
    frames_low = take_clip(group, frames_in)
    qkv_parts = spread_near(qkv_far)
    up_far = spread_far(jnp.concatenate([w_fc1, w_out.T], axis=1))
    down_far = spread_far(w_fc2.T)
    grad_low = take_clip(after(group, frames_low, qkv_far), cotangent)
    row = ((1, model_width), WIDE)
    (
        qkv_full, qkv_bias, gain_one, shift_one, gain_two, shift_two, out_bias, down_bias, up_bias
    ) = place(
        qkv_parts,
        functools.partial(finish_qkv, part=part, head_width=head_width, bias_part=bias_part),
        [((model_width, 6 * head_width), LOW), ((1, 6 * head_width), WIDE)]
        + [row] * 6
        + [((1, 2 * unit_width), WIDE)],
    )

    up_parts = spread_near(jnp.stack(after(up_far, qkv_full)))
    token_rows = after(frames_low, qkv_far).astype(WIDE)
    first_low = layer_norm(token_rows, gain_one, shift_one)[0].astype(LOW)
    qkv = (jnp.dot(first_low, qkv_full, preferred_element_type=WIDE) + qkv_bias).astype(LOW)
    down_parts = spread_near(jnp.stack(after(down_far, qkv)))
    attn_low, log_total = attend(qkv)

    up_all, out_full = place(
        up_parts,
        functools.partial(finish_up, unit_width=unit_width),
        [((model_width, 2 * unit_width), LOW), ((model_width, 2 * head_width), LOW)],
    )
    attn_terms = lax.dot_general(attn_low, out_full, NT, preferred_element_type=WIDE).astype(LOW)
    attn_other = swap_tensor(attn_terms, 1)
    second_low, middle = norm_two(
        frames_low, attn_terms, attn_other, gain_two, shift_two, out_bias
    )

    pre_act = jnp.dot(second_low, up_all, preferred_element_type=WIDE) + up_bias
    below = 0.5 * (1.0 + lax.erf(pre_act * 0.7071067811865476))
    slope = below + pre_act * jnp.exp(-0.5 * pre_act * pre_act) * 0.3989422804014327
    act, slope = lax.optimization_barrier(((pre_act * below).astype(LOW), slope.astype(LOW)))
    grad_down = lax.dot_general(grad_low, act, TN, preferred_element_type=WIDE).astype(LOW)
    down_cross = fold_cross(grad_down)

    (stack, keys), *others = down_parts
    (down_all,) = place(
        [(after(stack, grad_down), keys)] + others,
        finish_plain,
        [((model_width, 2 * unit_width), LOW)],
    )
    grad_pre = jnp.dot(grad_low, down_all, preferred_element_type=WIDE) * slope.astype(WIDE)
    grad_up_bias = jnp.sum(grad_pre, axis=0, keepdims=True)
    grad_pre = grad_pre.astype(LOW)
    second_terms = lax.dot_general(grad_pre, up_all, NT, preferred_element_type=WIDE).astype(LOW)
    second_other = swap_tensor(second_terms, 1)
    grad_up = lax.dot_general(
        after(second_low, second_terms), grad_pre, TN, preferred_element_type=WIDE
    ).astype(LOW)
    up_cross = fold_cross(grad_up)
    down_terms = lax.dot_general(
        after(act, grad_up), down_all, NT, preferred_element_type=WIDE
    ).astype(LOW)
    down_other = swap_tensor(down_terms, 1)
    result = middle.astype(WIDE) + (down_terms.astype(WIDE) + down_other.astype(WIDE)) + down_bias
    result = result.astype(LOW)

    middle_low, sums_two = norm_back(
        core, second_terms, second_other, grad_low, gain_two, middle, False
    )
    grad_attn = jnp.dot(middle_low, out_full, preferred_element_type=WIDE).astype(LOW)
    grad_out = lax.dot_general(middle_low, attn_low, TN, preferred_element_type=WIDE)
    out_fold = fold_near(grad_out.astype(LOW).reshape(far, 2, part, 2 * head_width))

    half = model_width // 2
    out_direct = swap_tensor(lax.dynamic_slice_in_dim(result, core * half, half, axis=1), 2)
    out_across = swap_tensor(out_direct, 1)

    pairs = 2 * head_width // 128
    grads_pair, bias_sums, folds = [], [], [out_fold]
    grad_attn = after(grad_attn, out_fold[0], result)
    for p in range(pairs):
        grad_pair, sums = attend_back(p, qkv, grad_attn, attn_low, log_total)
        grads_pair.append(grad_pair)
        bias_sums.append(sums)
        if p == 0:
            units = jnp.stack(
                [cross_sum(*after(c, grad_pair)) for c in (down_cross, up_cross)]
            )
            grad_attn = after(grad_attn, units)
        grad = lax.dot_general(first_low, grad_pair, TN, preferred_element_type=WIDE)
        folds.append(fold_near(grad.astype(LOW).reshape(far, 2, part, 384)))
        if p + 1 < pairs:
            grad_attn = after(grad_attn, folds[-1][0])

    first_terms = merge(grads_pair, qkv_full)
    place_now = jnp.stack([mine, group])
    folded = [after(value, first_terms) for fold in folds for value in fold]
    tail = small_call(
        functools.partial(tail_kernel, count=len(folds)),
        place_now,
        folded,
        [((len(folds) * part, 384), LOW)] * far,
        [],
    )
    tail = [tail[0]] + [swap_fsdp(tail[i], 2 * i) for i in range(1, far)]
    first_other = swap_tensor(first_terms, 1)
    rows_low, *halves, sums_one = norm_back(
        core, first_terms, first_other, middle_low, gain_one, frames_low, True
    )
    direct = [swap_tensor(h, 2) for h in halves]
    across = [swap_tensor(d, 1) for d in direct]

    own, sent = small_call(
        functools.partial(
            vector_kernel, part=part, bias_part=bias_part, head_width=head_width
        ),
        place_now,
        [sums_one, sums_two, grad_up_bias, *bias_sums],
        [((far, 16, 128), LOW)] * 2,
        [pltpu.VMEM((size, 16, 128), WIDE)],
    )
    vectors = add_low(own, swap_fsdp(sent, 1))
    _, high = near_far()
    vectors = [pick(vectors, 0, high ^ i) for i in range(far)]
    vectors = vectors[:1] + [swap_fsdp(vectors[i], 2 * i) for i in range(1, far)]
    own, sent = small_call(
        functools.partial(heads_kernel, far=far, part=part, head_width=head_width),
        place_now,
        tail + vectors,
        [((4 * part + 8, head_width), LOW)] * 2,
        [],
    )
    row = ((1, part), WIDE)
    grad_out, grad_qkv, grad_one, grad_two, row_out, row_down, row_up, grad_bias = small_call(
        functools.partial(final_kernel, part=part, bias_part=bias_part),
        place_now,
        [own, swap_tensor(sent, 2)],
        [((head_width, part), WIDE), ((3, part, head_width), WIDE), ((2, part), WIDE)]
        + [((2, part), WIDE), row, row, row, ((2, bias_part), WIDE)],
        [],
    )

    blocks = pl.cdiv(frame_count, ROWS)
    frames_out = both_clips(result, out_direct, out_across, LOW, 0, blocks, None)
    grad_frames = None
    for i in range(2):
        grad_frames = both_clips(rows_low, direct[i], across[i], WIDE, 2 * i, 2, grad_frames)

    units = fold_far(units)
    grad_down, grad_up = units[0].T, units[1]

    return (
        frames_out.transpose(1, 0, 2),
        grad_frames.transpose(1, 0, 2),
        grad_one,
        grad_qkv.transpose(1, 0, 2),
        grad_bias,
        grad_out,
        row_out[0],
        grad_two,
        grad_up,
        row_up[0],
        grad_down,
        row_down[0],
    )


def solution(mesh):
    in_specs = (
        P("fsdp", None, None),
        P("fsdp", None, None),
        P(None, "fsdp"),
        P("fsdp", None, "tensor"),
        P(None, ("tensor", "fsdp")),
        P("tensor", "fsdp"),
        P("fsdp"),
        P(None, "fsdp"),
        P("fsdp", "tensor"),
        P(("tensor", "fsdp")),
        P("tensor", "fsdp"),
        P("fsdp"),
    )
    out_specs = (
        P("fsdp", None, None),
        P("fsdp", None, None),
        P(None, "fsdp"),
        P("fsdp", None, "tensor"),
        P(None, ("tensor", "fsdp")),
        P("tensor", "fsdp"),
        P("fsdp"),
        P(None, "fsdp"),
        P("fsdp", "tensor"),
        P(("tensor", "fsdp")),
        P("tensor", "fsdp"),
        P("fsdp"),
    )
    return jax.shard_map(local, mesh=mesh, in_specs=in_specs, out_specs=out_specs, check_vma=False)
```

```python
import functools

import jax
import jax.numpy as jnp
from jax import lax
from jax.experimental import pallas as pl
from jax.experimental.pallas import tpu as pltpu
from jax.sharding import PartitionSpec as P


HEAD_DIM = 64
EPSILON = 1e-05
LOW = jnp.bfloat16
WIDE = jnp.float32
NEGATIVE = -1e30
NT = (((1,), (1,)), ((), ()))
TN = (((0,), (0,)), ((), ()))


def layer_norm(values, norm_gain, norm_shift):
    centre = jnp.mean(values, axis=-1, keepdims=True)
    centred = values - centre
    inverse = lax.rsqrt(jnp.mean(centred * centred, axis=-1, keepdims=True) + EPSILON)
    normed = centred * inverse
    return (normed * norm_gain + norm_shift, normed, inverse)


def cost(microseconds, size):
    return pl.CostEstimate(
        flops=int(microseconds * 1e9), transcendentals=0, bytes_accessed=int(size)
    )


def padded_rows(count):
    return -(-count // 512) * 512


def attend_kernel(q_ref, k_ref, v_ref, o_ref, l_ref, q_all, v_all, *, rows, block):
    padded = q_all.shape[0]
    q_all[...] = q_ref[...] * LOW(HEAD_DIM**-0.5)
    v_all[:, :128] = v_ref[...]
    v_all[:, 128:] = jnp.ones((padded, 128), LOW)
    valid = lax.broadcasted_iota(jnp.int32, (block, 256), 1) < rows - (padded - 256)
    upper = lax.broadcasted_iota(jnp.int32, (block, 128), 1) >= HEAD_DIM
    for step in range(padded // block):
        start = step * block
        parts = []
        for head in range(2):
            q_head = jnp.where(upper == (head == 1), q_all[start : start + block, :], LOW(0))
            scores = lax.dot_general(q_head, k_ref[...], NT, preferred_element_type=WIDE)
            scores = jnp.concatenate(
                [
                    scores[:, : padded - 256],
                    jnp.where(valid, scores[:, padded - 256 :], NEGATIVE),
                ],
                axis=1,
            )
            highest = jnp.max(scores, axis=1, keepdims=True)
            weights = jnp.exp(scores - highest).astype(LOW)
            blended = jnp.dot(weights, v_all[...], preferred_element_type=WIDE)
            total = blended[:, 128:]
            parts.append(blended[:, :128] * (1.0 / total))
            log_total = (highest + jnp.log(total)).T
            l_ref[head, :, start : start + block] = log_total[0:8, :]
        o_ref[start : start + block, :] = jnp.where(upper, parts[1], parts[0]).astype(LOW)


def attend(qkv, rows):
    padded, width = qkv.shape
    pairs = width // 3 // 128

    def column(which):
        return pl.BlockSpec((padded, 128), lambda p: (0, 3 * p + which))

    return pl.pallas_call(
        functools.partial(attend_kernel, rows=rows, block=512),
        grid=(pairs,),
        in_specs=[column(0), column(1), column(2)],
        out_specs=[
            pl.BlockSpec((padded, 128), lambda p: (0, p)),
            pl.BlockSpec((2, 8, padded), lambda p: (p, 0, 0)),
        ],
        out_shape=[
            jax.ShapeDtypeStruct((rows, width // 3), LOW),
            jax.ShapeDtypeStruct((2 * pairs, 8, padded), WIDE),
        ],
        scratch_shapes=[pltpu.VMEM((padded, 128), LOW), pltpu.VMEM((padded, 256), LOW)],
        cost_estimate=cost(22, padded * width * 3),
        name="fa",
    )(qkv, qkv, qkv)


def attend_back_kernel(
    near_ref, q_ref, k_ref, v_ref, g_ref, o_ref, l_ref, h_ref, d_ref, db_ref, own_ref, sent_ref,
    q_all, k_all, g_all, dq_turned, centre_all, *, rows, block,
):
    padded = k_all.shape[0]
    fill = jnp.zeros((padded - rows, 128), LOW)

    def pad(value):
        return jnp.concatenate([value, fill], axis=0)

    upper = lax.broadcasted_iota(jnp.int32, (padded, 128), 1) >= HEAD_DIM
    upper8 = lax.broadcasted_iota(jnp.int32, (8, 128), 1) >= HEAD_DIM
    upper_block = lax.broadcasted_iota(jnp.int32, (block, 128), 1) >= HEAD_DIM
    row_block = lax.broadcasted_iota(jnp.int32, (block, 128), 0)
    scale = HEAD_DIM**-0.5
    keys = k_ref[...]
    k_all[...] = jnp.concatenate([keys[:rows], keys[: padded - rows]], axis=0)
    q_full = q_ref[...] * LOW(scale)
    g_full = pad(g_ref[...])
    product = g_full.astype(WIDE) * pad(o_ref[...]).astype(WIDE)
    coarse = product.astype(LOW)
    fine = (product - coarse.astype(WIDE)).astype(LOW)
    for head in range(2):
        mine = upper == (head == 1)
        q_all[head] = jnp.where(mine, q_full, LOW(0))
        g_all[head] = jnp.where(mine, g_full, LOW(0))
        ones = jnp.where(upper8 == (head == 1), 1.0, 0.0).astype(LOW)
        centre_all[head] = lax.dot_general(
            ones, coarse, NT, preferred_element_type=WIDE
        ) + lax.dot_general(ones, fine, NT, preferred_element_type=WIDE)
    dq_turned[...] = jnp.zeros_like(dq_turned)

    def step(index, value_bias):
        span = pl.ds(pl.multiple_of(index * block, block), block)
        keys, values = k_all[span, :], v_ref[span, :]
        real = row_block < rows - index * block
        grad_values = grad_keys = grad_query = None
        for head in range(2):
            scores = lax.dot_general(keys, q_all[head], NT, preferred_element_type=WIDE)
            chances = jnp.exp(scores - l_ref[head, 0:1, :])
            grad_weights = lax.dot_general(
                values, g_all[head], NT, preferred_element_type=WIDE
            )
            grad_scores = (chances * (grad_weights - centre_all[head, 0:1, :])).astype(LOW)
            from_values = jnp.dot(
                chances.astype(LOW), g_all[head], preferred_element_type=WIDE
            )
            from_keys = jnp.dot(grad_scores, q_all[head], preferred_element_type=WIDE)
            keys_head = jnp.where(real & (upper_block == (head == 1)), keys, LOW(0))
            from_query = jnp.dot(keys_head.T, grad_scores, preferred_element_type=WIDE)
            if head == 0:
                grad_values, grad_keys, grad_query = from_values, from_keys, from_query
            else:
                grad_values = grad_values + from_values
                grad_keys = grad_keys + from_keys
                grad_query = grad_query + from_query
        dq_turned[...] += grad_query
        grad_values = jnp.where(real, grad_values, 0.0)
        d_ref[span, 128:256] = jnp.where(real, grad_keys, 0.0).astype(LOW)
        d_ref[span, 256:384] = grad_values.astype(LOW)
        return value_bias + jnp.sum(grad_values, axis=0, keepdims=True)

    value_bias = lax.fori_loop(0, padded // block, step, jnp.zeros((1, 128), WIDE))
    turned = dq_turned[...] * scale
    grad_query = turned.T
    d_ref[:, 0:128] = grad_query.astype(LOW)
    db_ref[0:1, :] = jnp.sum(grad_query, axis=0, keepdims=True)
    db_ref[1:2, :] = value_bias
    turned = jnp.concatenate(
        [turned.astype(LOW), d_ref[:, 128:256].T, d_ref[:, 256:384].T], axis=0
    )
    weight = jnp.dot(turned, h_ref[...], preferred_element_type=WIDE).T
    part = own_ref.shape[1]
    first = near_ref[0] == 0
    for i in range(own_ref.shape[0]):
        even = weight[2 * i * part : (2 * i + 1) * part, :]
        odd = weight[(2 * i + 1) * part : (2 * i + 2) * part, :]
        own_ref[i] = jnp.where(first, even, odd).astype(LOW)
        sent_ref[i] = jnp.where(first, odd, even).astype(LOW)


def attend_back(pair, near, qkv, grad_out, blended, log_total, normed):
    rows = grad_out.shape[0]
    padded, width = normed.shape
    size = lax.axis_size("fsdp")

    def column(index, height=padded):
        return pl.BlockSpec((height, 128), lambda i, n: (0, index))

    half = (size // 2, width // size, 384)
    return pl.pallas_call(
        functools.partial(attend_back_kernel, rows=rows, block=512),
        grid_spec=pltpu.PrefetchScalarGridSpec(
            num_scalar_prefetch=1,
            grid=(1,),
            in_specs=[
                column(3 * pair),
                column(3 * pair + 1),
                column(3 * pair + 2),
                column(pair, rows),
                column(pair, rows),
                pl.BlockSpec((2, 8, padded), lambda i, n: (pair, 0, 0)),
                pl.BlockSpec((padded, width), lambda i, n: (0, 0)),
            ],
            out_specs=[
                pl.BlockSpec((padded, 384), lambda i, n: (0, 0)),
                pl.BlockSpec((8, 128), lambda i, n: (0, 0)),
                pl.BlockSpec(half, lambda i, n: (0, 0, 0)),
                pl.BlockSpec(half, lambda i, n: (0, 0, 0)),
            ],
            scratch_shapes=[
                pltpu.VMEM((2, padded, 128), LOW),
                pltpu.VMEM((padded, 128), LOW),
                pltpu.VMEM((2, padded, 128), LOW),
                pltpu.VMEM((128, padded), WIDE),
                pltpu.VMEM((2, 8, padded), WIDE),
            ],
        ),
        out_shape=[
            jax.ShapeDtypeStruct((rows, 384), LOW),
            jax.ShapeDtypeStruct((8, 128), WIDE),
            jax.ShapeDtypeStruct(half, LOW),
            jax.ShapeDtypeStruct(half, LOW),
        ],
        cost_estimate=cost(15, rows * 128 * 16),
    )(near.reshape(1), qkv, qkv, qkv, grad_out, blended, log_total, normed)


def merge_kernel(*refs, count):
    parts, weight_ref, out_ref = refs[:count], refs[count], refs[count + 1]
    terms = jnp.concatenate([part[...] for part in parts], axis=1)
    total = lax.dot_general(terms, weight_ref[...], NT, preferred_element_type=WIDE)
    out_ref[...] = total.astype(LOW)


def merge(parts, weight):
    rows, width = parts[0].shape
    size = 512
    return pl.pallas_call(
        functools.partial(merge_kernel, count=len(parts)),
        grid=(pl.cdiv(rows, size),),
        in_specs=[pl.BlockSpec((size, width), lambda i: (i, 0))] * len(parts)
        + [pl.BlockSpec(weight.shape, lambda i: (0, 0))],
        out_specs=pl.BlockSpec((size, weight.shape[0]), lambda i: (i, 0)),
        out_shape=jax.ShapeDtypeStruct((rows, weight.shape[0]), LOW),
        cost_estimate=cost(6, rows * weight.shape[1] * 4),
        name="mg",
    )(*parts, weight)


def norm_two_kernel(frames_ref, own_ref, other_ref, gain_ref, shift_ref, bias_ref, out_ref, mid_ref):
    terms = own_ref[...].astype(WIDE) + other_ref[...].astype(WIDE)
    value = frames_ref[...].astype(WIDE) + terms + bias_ref[...]
    mid_ref[...] = value.astype(LOW)
    out_ref[...] = layer_norm(value, gain_ref[...], shift_ref[...])[0].astype(LOW)


def norm_two(frames, own, other, gain, shift, bias):
    rows, width = own.shape
    whole = pl.BlockSpec((ROWS, width), lambda i: (i, 0))
    row = pl.BlockSpec((1, width), lambda i: (0, 0))
    return pl.pallas_call(
        norm_two_kernel,
        grid=(pl.cdiv(rows, ROWS),),
        in_specs=[whole] * 3 + [row] * 3,
        out_specs=[whole, whole],
        out_shape=[jax.ShapeDtypeStruct((rows, width), LOW)] * 2,
        cost_estimate=cost(6, rows * width * 10),
        name="n2",
    )(frames, own, other, gain, shift, bias)


def norm_back_kernel(
    core_ref, own_ref, other_ref, base_ref, gain_ref, value_ref, out_ref, *refs, rows
):
    *half_refs, sums_ref = refs
    step = pl.program_id(0)
    grad = own_ref[...].astype(WIDE) + other_ref[...].astype(WIDE)
    value = value_ref[...].astype(WIDE)
    centred = value - jnp.mean(value, axis=-1, keepdims=True)
    inverse = lax.rsqrt(jnp.mean(centred * centred, axis=-1, keepdims=True) + EPSILON)
    normed = centred * inverse
    scaled = grad * gain_ref[...]
    change = inverse * (
        scaled
        - jnp.mean(scaled, axis=-1, keepdims=True)
        - normed * jnp.mean(scaled * normed, axis=-1, keepdims=True)
    )
    base = base_ref[...].astype(WIDE)
    total = base + change
    low = total.astype(LOW)
    out_ref[...] = low
    if half_refs:
        half = low.shape[1] // 2
        mine = jnp.where(core_ref[0] == 0, low[:, :half], low[:, half:])

        @pl.when(step < 2)
        def _():
            half_refs[0][...] = mine

        @pl.when(step >= 2)
        def _():
            half_refs[1][...] = mine

    valid = lax.broadcasted_iota(jnp.int32, grad.shape, 0) + step * grad.shape[0] < rows

    def column(summed):
        return jnp.sum(jnp.where(valid, summed, 0.0), axis=0, keepdims=True)

    sums = jnp.concatenate(
        [
            column(grad * normed),
            column(grad),
        ]
        + ([] if half_refs else [column(total), column(base)])
        + [jnp.zeros((6 if half_refs else 4, grad.shape[1]), WIDE)],
        axis=0,
    )

    @pl.when(step == 0)
    def _():
        sums_ref[...] = sums

    @pl.when(step > 0)
    def _():
        sums_ref[...] += sums


def norm_back(core, own, other, base, gain, value, halves):
    rows, width = base.shape
    whole = pl.BlockSpec((ROWS, width), lambda i, c: (i, 0))
    row = pl.BlockSpec((1, width), lambda i, c: (0, 0))
    specs, shapes = [], []
    if halves:
        specs = [
            pl.BlockSpec((ROWS, width // 2), lambda i, c: (jnp.minimum(i, 1), 0)),
            pl.BlockSpec((ROWS, width // 2), lambda i, c: (jnp.maximum(i - 2, 0), 0)),
        ]
        shapes = [jax.ShapeDtypeStruct((2 * ROWS, width // 2), LOW)] * 2
    return pl.pallas_call(
        functools.partial(norm_back_kernel, rows=rows),
        grid_spec=pltpu.PrefetchScalarGridSpec(
            num_scalar_prefetch=1,
            grid=(pl.cdiv(rows, ROWS),),
            in_specs=[whole, whole, whole, row, whole],
            out_specs=[whole] + specs + [pl.BlockSpec((8, width), lambda i, c: (0, 0))],
        ),
        out_shape=[jax.ShapeDtypeStruct((rows, width), LOW)]
        + shapes
        + [jax.ShapeDtypeStruct((8, width), WIDE)],
        cost_estimate=cost(8, rows * width * 12),
    )(core.reshape(1), own, other, base, gain, value)


ROWS = 376
SHORT = 8


def take_clip_kernel(group_ref, both_ref, own_ref, *, rows):
    size = own_ref.shape[0]
    place = lax.broadcasted_iota(jnp.int32, (SHORT, own_ref.shape[1]), 0)

    def step(index, carry):
        start = pl.multiple_of(index * SHORT, SHORT)
        both = both_ref[pl.ds(start, SHORT)]
        own = jnp.where(group_ref[0] == 0, both[:, 0, :].astype(WIDE), both[:, 1, :].astype(WIDE))
        real = place + start < rows - pl.program_id(0) * size
        own_ref[pl.ds(start, SHORT), :] = jnp.where(real, own, 0.0).astype(LOW)
        return carry

    lax.fori_loop(0, size // SHORT, step, 0, unroll=False)


def take_clip(group, both, padded, size):
    _, rows, width = both.shape
    return pl.pallas_call(
        functools.partial(take_clip_kernel, rows=rows),
        grid_spec=pltpu.PrefetchScalarGridSpec(
            num_scalar_prefetch=1,
            grid=(pl.cdiv(padded, size),),
            in_specs=[pl.BlockSpec((size, 2, width), lambda i, g: (i, 0, 0))],
            out_specs=pl.BlockSpec((size, width), lambda i, g: (i, 0)),
        ),
        out_shape=jax.ShapeDtypeStruct((padded, width), LOW),
        cost_estimate=cost(9, rows * width * 6),
    )(group.reshape(1), both.transpose(1, 0, 2))


def both_clips_kernel(place_ref, own_ref, direct_ref, across_ref, *refs):
    out_ref = refs[-1]
    group, core = place_ref[0], place_ref[1]

    def step(index, carry):
        span = pl.ds(pl.multiple_of(index * SHORT, SHORT), SHORT)
        own = own_ref[span, :].astype(WIDE)
        direct = direct_ref[span, :].astype(WIDE)
        across = across_ref[span, :].astype(WIDE)
        first = jnp.where(core == 0, direct, across)
        second = jnp.where(core == 0, across, direct)
        other = jnp.concatenate([first, second], axis=1)
        out_ref[span, 0, :] = jnp.where(group == 0, own, other).astype(out_ref.dtype)
        out_ref[span, 1, :] = jnp.where(group == 0, other, own).astype(out_ref.dtype)
        return carry

    lax.fori_loop(0, ROWS // SHORT, step, 0, unroll=False)


def both_clips(own, direct, across, dtype, first, count, previous):
    tensor_index = lax.axis_index("tensor")
    place = jnp.stack([tensor_index // 2, tensor_index % 2])
    rows, width = own.shape
    narrow = pl.BlockSpec((ROWS, width // 2), lambda i, g: (i, 0))
    more = [] if previous is None else [previous]
    return pl.pallas_call(
        both_clips_kernel,
        grid_spec=pltpu.PrefetchScalarGridSpec(
            num_scalar_prefetch=1,
            grid=(count,),
            in_specs=[pl.BlockSpec((ROWS, width), lambda i, g: (i + first, 0)), narrow, narrow]
            + [pl.BlockSpec(memory_space=pl.ANY)] * len(more),
            out_specs=pl.BlockSpec((ROWS, 2, width), lambda i, g: (i + first, 0, 0)),
        ),
        out_shape=jax.ShapeDtypeStruct((rows, 2, width), dtype),
        input_output_aliases={4: 0} if more else {},
        cost_estimate=cost(2 * count, count * ROWS * width * 12),
    )(place, own, direct, across, *more)


def swap_tensor(value, distance):
    size = lax.axis_size("tensor")
    return lax.ppermute(value, "tensor", [(i, i ^ distance) for i in range(size)])


def swap_fsdp(value, distance):
    size = lax.axis_size("fsdp")
    return lax.ppermute(value, "fsdp", [(i, i ^ distance) for i in range(size)])


def swap_both(value):
    width = lax.axis_size("tensor")
    count = lax.axis_size("fsdp") * width
    pairs = [(i, ((i // width) ^ 1) * width + ((i % width) ^ 2)) for i in range(count)]
    return lax.ppermute(value, ("fsdp", "tensor"), pairs)


def after(value, *others):
    return lax.optimization_barrier((value, others))[0]


def spread_far(piece):
    far = lax.axis_size("fsdp") // 2
    return [piece] + [swap_fsdp(piece, 2 * i) for i in range(1, far)]


def spread_near(stack):
    far = stack.shape[0]
    return [
        (value, tuple((y, 2 * i + x) for i in range(far)))
        for y, x, value in (
            (0, 0, stack),
            (0, 1, swap_fsdp(stack, 1)),
            (1, 0, swap_tensor(stack, 2)),
            (1, 1, swap_both(stack)),
        )
    ]


def place_kernel(*refs, keys, finish):
    count = len(keys)
    stacks = refs[:count]
    outs, held, sem = refs[count:-2], refs[-2], refs[-1]
    mine = lax.axis_index("fsdp")
    group = lax.axis_index("tensor") // 2
    copies = []
    for stack, names in zip(stacks, keys):
        for i, (y, f) in enumerate(names):
            copy = pltpu.make_async_copy(
                stack.at[i], held.at[group ^ y, mine ^ f], sem.at[len(copies)]
            )
            copy.start()
            copies.append(copy)
    for copy in copies:
        copy.wait()
    finish(held, outs)


def place(parts, finish, out_shapes):
    size = lax.axis_size("fsdp")
    _, rows, columns = parts[0][0].shape
    total = sum(len(ks) for _, ks in parts)
    return pl.pallas_call(
        functools.partial(place_kernel, keys=tuple(ks for _, ks in parts), finish=finish),
        in_specs=[pl.BlockSpec(memory_space=pl.ANY)] * len(parts),
        out_specs=[pl.BlockSpec(memory_space=pltpu.VMEM)] * len(out_shapes),
        out_shape=[jax.ShapeDtypeStruct(*s) for s in out_shapes],
        scratch_shapes=[
            pltpu.VMEM((2, size, rows, columns), LOW),
            pltpu.SemaphoreType.DMA((total,)),
        ],
        cost_estimate=cost(3.5, 4 * size * rows * columns * 2),
    )(*[p for p, _ in parts])


def finish_qkv(held, outs, *, part, head_width, bias_part):
    _, size, _, _ = held.shape
    pairs = 2 * head_width // 128
    for f in range(size):
        a, b = held[0, f, :part], held[1, f, :part]
        wide = []
        for c in range(3):
            span = slice(c * head_width, (c + 1) * head_width)
            wide.append(jnp.concatenate([a[:, span], b[:, span]], axis=1))
        for p in range(pairs):
            for c in range(3):
                outs[0][f * part : (f + 1) * part, (3 * p + c) * 128 : (3 * p + c + 1) * 128] = (
                    wide[c][:, p * 128 : (p + 1) * 128]
                )
    rows = [[held[y, f, part:].astype(WIDE) for f in range(size)] for y in range(2)]
    full = [jnp.concatenate([r[:, :part] for r in rows[y]], axis=1) for y in range(2)]
    for i in range(6):
        outs[2 + i][...] = full[0][i : i + 1]
    outs[8][...] = jnp.concatenate([full[0][6:7], full[1][6:7]], axis=1)
    biases = []
    for c in range(2):
        span = slice(c * bias_part, (c + 1) * bias_part)
        biases.append(jnp.concatenate([r[7:8, span] for y in range(2) for r in rows[y]], axis=1))
    nothing = jnp.zeros((1, 128), WIDE)
    for p in range(pairs):
        span = slice(p * 128, (p + 1) * 128)
        outs[1][:, 3 * p * 128 : (3 * p + 1) * 128] = biases[0][:, span]
        outs[1][:, (3 * p + 1) * 128 : (3 * p + 2) * 128] = nothing
        outs[1][:, (3 * p + 2) * 128 : (3 * p + 3) * 128] = biases[1][:, span]


def finish_up(held, outs, *, unit_width):
    _, size, part, _ = held.shape
    for f in range(size):
        rows = slice(f * part, (f + 1) * part)
        for y in range(2):
            outs[0][rows, y * unit_width : (y + 1) * unit_width] = held[y, f, :, :unit_width]
        outs[1][rows, :] = jnp.concatenate(
            [held[0, f, :, unit_width:], held[1, f, :, unit_width:]], axis=1
        )


def finish_plain(held, outs):
    _, size, part, width = held.shape
    for f in range(size):
        for y in range(2):
            outs[0][f * part : (f + 1) * part, y * width : (y + 1) * width] = held[y, f]


def pick(value, axis, index):
    return lax.dynamic_index_in_dim(value, index, axis, keepdims=False)


def add_low(a, b):
    return (a.astype(WIDE) + b.astype(WIDE)).astype(LOW)


def near_far():
    mine = lax.axis_index("fsdp")
    return mine % 2, mine // 2


def fold_cross(grads):
    low, _ = near_far()
    group = lax.axis_index("tensor") // 2
    size = lax.axis_size("fsdp")
    part, columns = grads.shape[0] // size, grads.shape[1] // 2
    grads = grads.reshape(size // 2, 2, part, 2 * columns)

    def at(y, x):
        span = (size // 2, 1, part, columns)
        return lax.dynamic_slice(grads, (0, x, 0, y * columns), span)[:, 0]

    side = swap_tensor(at(1 - group, low), 2)
    near = swap_fsdp(at(group, 1 - low), 1)
    both = swap_both(at(1 - group, 1 - low))
    return at(group, low), side, near, both


def cross_sum(own, side, near, both):
    total = own.astype(WIDE) + side.astype(WIDE)
    return (total + (near.astype(WIDE) + both.astype(WIDE))).astype(LOW)


def fold_far(grads):
    _, high = near_far()
    axis = grads.ndim - 3
    total = pick(grads, axis, high).astype(WIDE)
    for i in range(1, grads.shape[axis]):
        total = total + swap_fsdp(pick(grads, axis, high ^ i), 2 * i).astype(WIDE)
    return total


VMEM = pl.BlockSpec(memory_space=pltpu.VMEM)
SMEM = pl.BlockSpec(memory_space=pltpu.SMEM)


def small_call(kernel, place, inputs, shapes, scratch):
    return pl.pallas_call(
        kernel,
        in_specs=[SMEM] + [VMEM] * len(inputs),
        out_specs=[VMEM] * len(shapes),
        out_shape=[jax.ShapeDtypeStruct(*s) for s in shapes],
        scratch_shapes=scratch,
        cost_estimate=cost(1.5, 4 << 20),
    )(place, *inputs)


def vector_kernel(place_ref, one_ref, two_ref, up_ref, *refs, part, bias_part, head_width):
    *bias_refs, own_ref, sent_ref, held = refs
    width = one_ref.shape[1]
    rows = jnp.concatenate(
        [one_ref[0:2, :], two_ref[0:4, :], up_ref[:, :width], up_ref[:, width:]], axis=0
    )
    query = jnp.concatenate([b[0:1, :] for b in bias_refs], axis=1)
    value = jnp.concatenate([b[1:2, :] for b in bias_refs], axis=1)
    held[...] = jnp.zeros_like(held)
    for f in range(held.shape[0]):
        held[f, 0:8, 0:part] = rows[:, f * part : (f + 1) * part]
        for y in range(2):
            start = y * head_width + f * bias_part
            span = slice(start, start + bias_part)
            held[f, 8 + y : 9 + y, 0 : 2 * bias_part] = jnp.concatenate(
                [query[:, span], value[:, span]], axis=1
            )
    first = place_ref[0] % 2 == 0
    for i in range(own_ref.shape[0]):
        even, odd = held[2 * i], held[2 * i + 1]
        own_ref[i] = jnp.where(first, even, odd).astype(LOW)
        sent_ref[i] = jnp.where(first, odd, even).astype(LOW)


def tail_kernel(place_ref, *refs, count):
    owns, early_ref, late_ref, outs = refs[:count], refs[count], refs[count + 1], refs[count + 2 :]
    high = place_ref[0] // 2
    part = owns[0].shape[1]
    for i, out in enumerate(outs):
        for k in range(count):
            rows = slice(k * part, (k + 1) * part)
            got = late_ref[high ^ i] if k == count - 1 else early_ref[high ^ i, rows, :]
            out[rows, :] = (owns[k][high ^ i].astype(WIDE) + got.astype(WIDE)).astype(LOW)


def sum_of(refs):
    total = refs[0][...].astype(WIDE)
    for ref in refs[1:]:
        total = total + ref[...].astype(WIDE)
    return total


def heads_kernel(place_ref, *refs, far, part, head_width):
    tail = sum_of(refs[:far])
    vectors = sum_of(refs[far : 2 * far])
    own_ref, sent_ref = refs[2 * far :]
    first = place_ref[1] == 0
    pairs = tail.shape[0] // part - 1
    blocks = [tail[:part, :]]
    for c in range(3):
        span = slice(c * 128, (c + 1) * 128)
        blocks.append(
            jnp.concatenate(
                [tail[(1 + p) * part : (2 + p) * part, span] for p in range(pairs)], axis=1
            )
        )
    for k, block in enumerate(blocks):
        rows = slice(k * part, (k + 1) * part)
        low, high = block[:, :head_width], block[:, head_width:]
        own_ref[rows, :] = jnp.where(first, low, high).astype(LOW)
        sent_ref[rows, :] = jnp.where(first, high, low).astype(LOW)
    own_ref[4 * part :, :] = jnp.zeros((8, head_width), LOW)
    sent_ref[4 * part :, :] = jnp.zeros((8, head_width), LOW)
    low, high = [
        jnp.concatenate([vectors[:6], vectors[6 + y : 7 + y], vectors[8 + y : 9 + y]], axis=0)
        for y in range(2)
    ]
    own_ref[4 * part :, 0:128] = jnp.where(first, low, high).astype(LOW)
    sent_ref[4 * part :, 0:128] = jnp.where(first, high, low).astype(LOW)


def final_kernel(place_ref, own_ref, got_ref, *outs, part, bias_part):
    total = own_ref[...].astype(WIDE) + got_ref[...].astype(WIDE)
    out_ref, qkv_ref, one_ref, two_ref, *rows_refs, bias_ref = outs
    out_ref[...] = total[:part, :].T
    for c in range(3):
        qkv_ref[c] = total[(1 + c) * part : (2 + c) * part, :]
    vectors = total[4 * part :, :part]
    one_ref[...] = vectors[0:2]
    two_ref[...] = vectors[2:4]
    for i, ref in enumerate(rows_refs):
        ref[...] = vectors[4 + i : 5 + i]
    bias_ref[...] = jnp.concatenate(
        [vectors[7:8, :bias_part], vectors[7:8, bias_part : 2 * bias_part]], axis=0
    )


def local(
    frames_in, cotangent, ln_first, w_qkv, b_qv, w_out, b_out, ln_second, w_fc1, b_fc1, w_fc2, b_fc2
):
    _, frame_count, model_width = frames_in.shape
    size = lax.axis_size("fsdp")
    part = w_qkv.shape[0]
    head_width = w_qkv.shape[2]
    unit_width = w_fc1.shape[1]
    bias_part = b_qv.shape[1]
    group = lax.axis_index("tensor") // 2
    core = lax.axis_index("tensor") % 2
    mine = lax.axis_index("fsdp")
    far = size // 2

    vectors = jnp.concatenate(
        [
            ln_first,
            ln_second,
            b_out[None],
            b_fc2[None],
            b_fc1[None],
            jnp.pad(b_qv.reshape(1, -1), ((0, 0), (0, part - 2 * bias_part))),
        ],
        axis=0,
    )
    vectors = jnp.pad(vectors, ((0, 0), (0, 3 * head_width - part)))
    qkv_piece = jnp.concatenate([w_qkv.reshape(part, 3 * head_width), vectors], axis=0)
    qkv_far = jnp.stack(spread_far(qkv_piece))
    padded = padded_rows(frame_count)
    frames_low = take_clip(group, frames_in, padded, padded // 4)
    qkv_parts = spread_near(qkv_far)
    up_far = spread_far(jnp.concatenate([w_fc1, w_out.T], axis=1))
    down_far = spread_far(w_fc2.T)
    grad_low = take_clip(after(group, frames_low, qkv_far), cotangent, frame_count, ROWS)
    row = ((1, model_width), WIDE)
    (
        qkv_full, qkv_bias, gain_one, shift_one, gain_two, shift_two, out_bias, down_bias, up_bias
    ) = place(
        qkv_parts,
        functools.partial(finish_qkv, part=part, head_width=head_width, bias_part=bias_part),
        [((model_width, 6 * head_width), LOW), ((1, 6 * head_width), WIDE)]
        + [row] * 6
        + [((1, 2 * unit_width), WIDE)],
    )

    up_parts = spread_near(jnp.stack(after(up_far, qkv_full)))
    token_rows = after(frames_low, qkv_far).astype(WIDE)
    first_low = layer_norm(token_rows, gain_one, shift_one)[0].astype(LOW)
    qkv = (jnp.dot(first_low, qkv_full, preferred_element_type=WIDE) + qkv_bias).astype(LOW)
    down_parts = spread_near(jnp.stack(after(down_far, qkv)))
    attn_low, log_total = attend(qkv, frame_count)

    up_all, out_full = place(
        up_parts,
        functools.partial(finish_up, unit_width=unit_width),
        [((model_width, 2 * unit_width), LOW), ((model_width, 2 * head_width), LOW)],
    )
    attn_terms = lax.dot_general(attn_low, out_full, NT, preferred_element_type=WIDE).astype(LOW)
    attn_other = swap_tensor(attn_terms, 1)
    second_low, middle = norm_two(
        frames_low, attn_terms, attn_other, gain_two, shift_two, out_bias
    )

    pre_act = jnp.dot(second_low, up_all, preferred_element_type=WIDE) + up_bias
    below = 0.5 * (1.0 + lax.erf(pre_act * 0.7071067811865476))
    slope = below + pre_act * jnp.exp(-0.5 * pre_act * pre_act) * 0.3989422804014327
    act, slope = lax.optimization_barrier(((pre_act * below).astype(LOW), slope.astype(LOW)))
    grad_down = lax.dot_general(grad_low, act, TN, preferred_element_type=WIDE).astype(LOW)
    down_cross = fold_cross(grad_down)

    (stack, keys), *others = down_parts
    (down_all,) = place(
        [(after(stack, grad_down), keys)] + others,
        finish_plain,
        [((model_width, 2 * unit_width), LOW)],
    )
    grad_pre = jnp.dot(grad_low, down_all, preferred_element_type=WIDE) * slope.astype(WIDE)
    grad_up_bias = jnp.sum(grad_pre, axis=0, keepdims=True)
    grad_pre = grad_pre.astype(LOW)
    second_terms = lax.dot_general(grad_pre, up_all, NT, preferred_element_type=WIDE).astype(LOW)
    second_other = swap_tensor(second_terms, 1)
    grad_up = lax.dot_general(
        after(second_low, second_terms), grad_pre, TN, preferred_element_type=WIDE
    ).astype(LOW)
    up_cross = fold_cross(grad_up)
    down_terms = lax.dot_general(
        after(act, grad_up), down_all, NT, preferred_element_type=WIDE
    ).astype(LOW)
    down_other = swap_tensor(down_terms, 1)
    result = middle.astype(WIDE) + (down_terms.astype(WIDE) + down_other.astype(WIDE)) + down_bias
    result = result.astype(LOW)

    middle_low, sums_two = norm_back(
        core, second_terms, second_other, grad_low, gain_two, middle, False
    )
    grad_attn = jnp.dot(middle_low, out_full, preferred_element_type=WIDE).astype(LOW)
    grad_out = lax.dot_general(middle_low, attn_low, TN, preferred_element_type=WIDE)
    low, _ = near_far()
    grad_out = grad_out.astype(LOW).reshape(far, 2, part, 2 * head_width)
    owns, sents = [pick(grad_out, 1, low)], [pick(grad_out, 1, 1 - low)]

    half = model_width // 2
    out_direct = swap_tensor(lax.dynamic_slice_in_dim(result, core * half, half, axis=1), 2)
    out_across = swap_tensor(out_direct, 1)

    pairs = 2 * head_width // 128
    grads_pair, bias_sums = [], []
    grad_attn = after(grad_attn, sents[0], result)
    for p in range(pairs):
        grad_pair, sums, own, sent = attend_back(
            p, low, qkv, grad_attn, attn_low, log_total, first_low
        )
        grads_pair.append(grad_pair)
        bias_sums.append(sums)
        owns.append(own)
        sents.append(sent)
        if p == 0:
            units = jnp.stack(
                [cross_sum(*after(c, grad_pair)) for c in (down_cross, up_cross)]
            )
            grad_attn = after(grad_attn, units)
        if p == pairs - 2:
            early = jnp.concatenate(sents, axis=1)
            grad_attn = after(grad_attn, early)
    got_early = swap_fsdp(early, 1)
    got_late = swap_fsdp(sents[-1], 1)

    first_terms = merge(grads_pair, qkv_full)
    place_now = jnp.stack([mine, group])
    tail = small_call(
        functools.partial(tail_kernel, count=1 + pairs),
        place_now,
        owns + after([got_early, got_late], first_terms),
        [(((1 + pairs) * part, 384), LOW)] * far,
        [],
    )
    tail = [tail[0]] + [swap_fsdp(tail[i], 2 * i) for i in range(1, far)]
    first_other = swap_tensor(first_terms, 1)
    rows_low, *halves, sums_one = norm_back(
        core, first_terms, first_other, middle_low, gain_one, frames_low, True
    )
    direct = [swap_tensor(h, 2) for h in halves]
    across = [swap_tensor(d, 1) for d in direct]

    own, sent = small_call(
        functools.partial(
            vector_kernel, part=part, bias_part=bias_part, head_width=head_width
        ),
        place_now,
        [sums_one, sums_two, grad_up_bias, *bias_sums],
        [((far, 16, 128), LOW)] * 2,
        [pltpu.VMEM((size, 16, 128), WIDE)],
    )
    vectors = add_low(own, swap_fsdp(sent, 1))
    _, high = near_far()
    vectors = [pick(vectors, 0, high ^ i) for i in range(far)]
    vectors = vectors[:1] + [swap_fsdp(vectors[i], 2 * i) for i in range(1, far)]
    own, sent = small_call(
        functools.partial(heads_kernel, far=far, part=part, head_width=head_width),
        place_now,
        tail + vectors,
        [((4 * part + 8, head_width), LOW)] * 2,
        [],
    )
    row = ((1, part), WIDE)
    grad_out, grad_qkv, grad_one, grad_two, row_out, row_down, row_up, grad_bias = small_call(
        functools.partial(final_kernel, part=part, bias_part=bias_part),
        place_now,
        [own, swap_tensor(sent, 2)],
        [((head_width, part), WIDE), ((3, part, head_width), WIDE), ((2, part), WIDE)]
        + [((2, part), WIDE), row, row, row, ((2, bias_part), WIDE)],
        [],
    )

    blocks = pl.cdiv(frame_count, ROWS)
    frames_out = both_clips(result, out_direct, out_across, LOW, 0, blocks, None)
    grad_frames = None
    for i in range(2):
        grad_frames = both_clips(rows_low, direct[i], across[i], WIDE, 2 * i, 2, grad_frames)

    units = fold_far(units)
    grad_down, grad_up = units[0].T, units[1]

    return (
        frames_out.transpose(1, 0, 2),
        grad_frames.transpose(1, 0, 2),
        grad_one,
        grad_qkv.transpose(1, 0, 2),
        grad_bias,
        grad_out,
        row_out[0],
        grad_two,
        grad_up,
        row_up[0],
        grad_down,
        row_down[0],
    )


def solution(mesh):
    in_specs = (
        P("fsdp", None, None),
        P("fsdp", None, None),
        P(None, "fsdp"),
        P("fsdp", None, "tensor"),
        P(None, ("tensor", "fsdp")),
        P("tensor", "fsdp"),
        P("fsdp"),
        P(None, "fsdp"),
        P("fsdp", "tensor"),
        P(("tensor", "fsdp")),
        P("tensor", "fsdp"),
        P("fsdp"),
    )
    out_specs = (
        P("fsdp", None, None),
        P("fsdp", None, None),
        P(None, "fsdp"),
        P("fsdp", None, "tensor"),
        P(None, ("tensor", "fsdp")),
        P("tensor", "fsdp"),
        P("fsdp"),
        P(None, "fsdp"),
        P("fsdp", "tensor"),
        P(("tensor", "fsdp")),
        P("tensor", "fsdp"),
        P("fsdp"),
    )
    return jax.shard_map(local, mesh=mesh, in_specs=in_specs, out_specs=out_specs, check_vma=False)
```

```python
import functools

import jax
import jax.numpy as jnp
from jax import lax
from jax.experimental import pallas as pl
from jax.experimental.pallas import tpu as pltpu
from jax.sharding import PartitionSpec as P


HEAD_DIM = 64
EPSILON = 1e-05
LOW = jnp.bfloat16
WIDE = jnp.float32
NEGATIVE = -1e30
NT = (((1,), (1,)), ((), ()))
TN = (((0,), (0,)), ((), ()))


def layer_norm(values, norm_gain, norm_shift):
    centre = jnp.mean(values, axis=-1, keepdims=True)
    centred = values - centre
    inverse = lax.rsqrt(jnp.mean(centred * centred, axis=-1, keepdims=True) + EPSILON)
    normed = centred * inverse
    return (normed * norm_gain + norm_shift, normed, inverse)


def cost(microseconds, size):
    return pl.CostEstimate(
        flops=int(microseconds * 1e9), transcendentals=0, bytes_accessed=int(size)
    )


def padded_rows(count):
    return -(-count // 512) * 512


def attend_kernel(q_ref, k_ref, v_ref, o_ref, l_ref, q_all, v_all, *, rows, block):
    padded = q_all.shape[0]
    q_all[...] = q_ref[...] * LOW(HEAD_DIM**-0.5)
    v_all[:, :128] = v_ref[...]
    v_all[:, 128:] = jnp.ones((padded, 128), LOW)
    valid = lax.broadcasted_iota(jnp.int32, (block, 256), 1) < rows - (padded - 256)
    upper = lax.broadcasted_iota(jnp.int32, (block, 128), 1) >= HEAD_DIM
    for step in range(padded // block):
        start = step * block
        parts = []
        for head in range(2):
            q_head = jnp.where(upper == (head == 1), q_all[start : start + block, :], LOW(0))
            scores = lax.dot_general(q_head, k_ref[...], NT, preferred_element_type=WIDE)
            scores = jnp.concatenate(
                [
                    scores[:, : padded - 256],
                    jnp.where(valid, scores[:, padded - 256 :], NEGATIVE),
                ],
                axis=1,
            )
            highest = jnp.max(scores, axis=1, keepdims=True)
            weights = jnp.exp(scores - highest).astype(LOW)
            blended = jnp.dot(weights, v_all[...], preferred_element_type=WIDE)
            total = blended[:, 128:]
            parts.append(blended[:, :128] * (1.0 / total))
            log_total = (highest + jnp.log(total)).T
            l_ref[head, :, start : start + block] = log_total[0:8, :]
        o_ref[start : start + block, :] = jnp.where(upper, parts[1], parts[0]).astype(LOW)


def attend(qkv, rows):
    padded, width = qkv.shape
    pairs = width // 3 // 128

    def column(which):
        return pl.BlockSpec((padded, 128), lambda p: (0, 3 * p + which))

    return pl.pallas_call(
        functools.partial(attend_kernel, rows=rows, block=512),
        grid=(pairs,),
        in_specs=[column(0), column(1), column(2)],
        out_specs=[
            pl.BlockSpec((padded, 128), lambda p: (0, p)),
            pl.BlockSpec((2, 8, padded), lambda p: (p, 0, 0)),
        ],
        out_shape=[
            jax.ShapeDtypeStruct((rows, width // 3), LOW),
            jax.ShapeDtypeStruct((2 * pairs, 8, padded), WIDE),
        ],
        scratch_shapes=[pltpu.VMEM((padded, 128), LOW), pltpu.VMEM((padded, 256), LOW)],
        cost_estimate=cost(22, padded * width * 3),
        name="fa",
    )(qkv, qkv, qkv)


def attend_back_kernel(
    near_ref, q_ref, k_ref, v_ref, g_ref, o_ref, l_ref, h_ref, d_ref, db_ref, own_ref, sent_ref,
    q_all, k_all, g_all, dq_turned, centre_all, *, rows, block,
):
    padded = k_all.shape[0]
    fill = jnp.zeros((padded - rows, 128), LOW)

    def pad(value):
        return jnp.concatenate([value, fill], axis=0)

    upper = lax.broadcasted_iota(jnp.int32, (padded, 128), 1) >= HEAD_DIM
    upper8 = lax.broadcasted_iota(jnp.int32, (8, 128), 1) >= HEAD_DIM
    upper_block = lax.broadcasted_iota(jnp.int32, (block, 128), 1) >= HEAD_DIM
    row_block = lax.broadcasted_iota(jnp.int32, (block, 128), 0)
    scale = HEAD_DIM**-0.5
    keys = k_ref[...]
    k_all[...] = jnp.concatenate([keys[:rows], keys[: padded - rows]], axis=0)
    q_full = q_ref[...] * LOW(scale)
    g_full = pad(g_ref[...])
    product = g_full.astype(WIDE) * pad(o_ref[...]).astype(WIDE)
    coarse = product.astype(LOW)
    fine = (product - coarse.astype(WIDE)).astype(LOW)
    for head in range(2):
        mine = upper == (head == 1)
        q_all[head] = jnp.where(mine, q_full, LOW(0))
        g_all[head] = jnp.where(mine, g_full, LOW(0))
        ones = jnp.where(upper8 == (head == 1), 1.0, 0.0).astype(LOW)
        centre_all[head] = lax.dot_general(
            ones, coarse, NT, preferred_element_type=WIDE
        ) + lax.dot_general(ones, fine, NT, preferred_element_type=WIDE)
    dq_turned[...] = jnp.zeros_like(dq_turned)

    def step(index, value_bias):
        span = pl.ds(pl.multiple_of(index * block, block), block)
        keys, values = k_all[span, :], v_ref[span, :]
        real = row_block < rows - index * block
        grad_values = grad_keys = grad_query = None
        for head in range(2):
            scores = lax.dot_general(keys, q_all[head], NT, preferred_element_type=WIDE)
            chances = jnp.exp(scores - l_ref[head, 0:1, :])
            grad_weights = lax.dot_general(
                values, g_all[head], NT, preferred_element_type=WIDE
            )
            grad_scores = (chances * (grad_weights - centre_all[head, 0:1, :])).astype(LOW)
            from_values = jnp.dot(
                chances.astype(LOW), g_all[head], preferred_element_type=WIDE
            )
            from_keys = jnp.dot(grad_scores, q_all[head], preferred_element_type=WIDE)
            keys_head = jnp.where(real & (upper_block == (head == 1)), keys, LOW(0))
            from_query = jnp.dot(keys_head.T, grad_scores, preferred_element_type=WIDE)
            if head == 0:
                grad_values, grad_keys, grad_query = from_values, from_keys, from_query
            else:
                grad_values = grad_values + from_values
                grad_keys = grad_keys + from_keys
                grad_query = grad_query + from_query
        dq_turned[...] += grad_query
        grad_values = jnp.where(real, grad_values, 0.0)
        d_ref[span, 128:256] = jnp.where(real, grad_keys, 0.0).astype(LOW)
        d_ref[span, 256:384] = grad_values.astype(LOW)
        return value_bias + jnp.sum(grad_values, axis=0, keepdims=True)

    value_bias = lax.fori_loop(0, padded // block, step, jnp.zeros((1, 128), WIDE))
    turned = dq_turned[...] * scale
    grad_query = turned.T
    d_ref[:, 0:128] = grad_query.astype(LOW)
    db_ref[0:1, :] = jnp.sum(grad_query, axis=0, keepdims=True)
    db_ref[1:2, :] = value_bias
    turned = jnp.concatenate(
        [turned.astype(LOW), d_ref[:, 128:256].T, d_ref[:, 256:384].T], axis=0
    )
    weight = jnp.dot(turned, h_ref[...], preferred_element_type=WIDE).T
    part = own_ref.shape[1]
    first = near_ref[0] == 0
    for i in range(own_ref.shape[0]):
        even = weight[2 * i * part : (2 * i + 1) * part, :]
        odd = weight[(2 * i + 1) * part : (2 * i + 2) * part, :]
        own_ref[i] = jnp.where(first, even, odd).astype(LOW)
        sent_ref[i] = jnp.where(first, odd, even).astype(LOW)


def attend_back(near, qkv, grad_out, blended, log_total, normed):
    rows, total = grad_out.shape
    pairs = total // 128
    padded, width = normed.shape
    size = lax.axis_size("fsdp")

    def column(which):
        return pl.BlockSpec((padded, 128), lambda p, n: (0, 3 * p + which))

    single = pl.BlockSpec((rows, 128), lambda p, n: (0, p))
    half = (size // 2, width // size, 384)
    slices = pl.BlockSpec((None, *half), lambda p, n: (p, 0, 0, 0))
    return pl.pallas_call(
        functools.partial(attend_back_kernel, rows=rows, block=512),
        grid_spec=pltpu.PrefetchScalarGridSpec(
            num_scalar_prefetch=1,
            grid=(pairs,),
            in_specs=[
                column(0),
                column(1),
                column(2),
                single,
                single,
                pl.BlockSpec((2, 8, padded), lambda p, n: (p, 0, 0)),
                pl.BlockSpec((padded, width), lambda p, n: (0, 0)),
            ],
            out_specs=[
                pl.BlockSpec((padded, 384), lambda p, n: (0, p)),
                pl.BlockSpec((None, 8, 128), lambda p, n: (p, 0, 0)),
                slices,
                slices,
            ],
            scratch_shapes=[
                pltpu.VMEM((2, padded, 128), LOW),
                pltpu.VMEM((padded, 128), LOW),
                pltpu.VMEM((2, padded, 128), LOW),
                pltpu.VMEM((128, padded), WIDE),
                pltpu.VMEM((2, 8, padded), WIDE),
            ],
        ),
        out_shape=[
            jax.ShapeDtypeStruct((rows, 3 * total), LOW),
            jax.ShapeDtypeStruct((pairs, 8, 128), WIDE),
            jax.ShapeDtypeStruct((pairs, *half), LOW),
            jax.ShapeDtypeStruct((pairs, *half), LOW),
        ],
        cost_estimate=cost(45, rows * 384 * 16),
        name="b0",
    )(near.reshape(1), qkv, qkv, qkv, grad_out, blended, log_total, normed)


def merge_kernel(terms_ref, weight_ref, out_ref):
    total = lax.dot_general(terms_ref[...], weight_ref[...], NT, preferred_element_type=WIDE)
    out_ref[...] = total.astype(LOW)


def merge(terms, weight):
    rows, width = terms.shape
    size = 512
    return pl.pallas_call(
        merge_kernel,
        grid=(pl.cdiv(rows, size),),
        in_specs=[
            pl.BlockSpec((size, width), lambda i: (i, 0)),
            pl.BlockSpec(weight.shape, lambda i: (0, 0)),
        ],
        out_specs=pl.BlockSpec((size, weight.shape[0]), lambda i: (i, 0)),
        out_shape=jax.ShapeDtypeStruct((rows, weight.shape[0]), LOW),
        cost_estimate=cost(6, rows * weight.shape[1] * 4),
        name="mg",
    )(terms, weight)


def norm_two_kernel(frames_ref, own_ref, other_ref, gain_ref, shift_ref, bias_ref, out_ref, mid_ref):
    terms = own_ref[...].astype(WIDE) + other_ref[...].astype(WIDE)
    value = frames_ref[...].astype(WIDE) + terms + bias_ref[...]
    mid_ref[...] = value.astype(LOW)
    out_ref[...] = layer_norm(value, gain_ref[...], shift_ref[...])[0].astype(LOW)


def norm_two(frames, own, other, gain, shift, bias):
    rows, width = own.shape
    whole = pl.BlockSpec((ROWS, width), lambda i: (i, 0))
    row = pl.BlockSpec((1, width), lambda i: (0, 0))
    return pl.pallas_call(
        norm_two_kernel,
        grid=(pl.cdiv(rows, ROWS),),
        in_specs=[whole] * 3 + [row] * 3,
        out_specs=[whole, whole],
        out_shape=[jax.ShapeDtypeStruct((rows, width), LOW)] * 2,
        cost_estimate=cost(6, rows * width * 10),
        name="n2",
    )(frames, own, other, gain, shift, bias)


def norm_back_kernel(
    core_ref, own_ref, other_ref, base_ref, gain_ref, value_ref, out_ref, *refs, rows
):
    *half_refs, sums_ref = refs
    step = pl.program_id(0)
    grad = own_ref[...].astype(WIDE) + other_ref[...].astype(WIDE)
    value = value_ref[...].astype(WIDE)
    centred = value - jnp.mean(value, axis=-1, keepdims=True)
    inverse = lax.rsqrt(jnp.mean(centred * centred, axis=-1, keepdims=True) + EPSILON)
    normed = centred * inverse
    scaled = grad * gain_ref[...]
    change = inverse * (
        scaled
        - jnp.mean(scaled, axis=-1, keepdims=True)
        - normed * jnp.mean(scaled * normed, axis=-1, keepdims=True)
    )
    base = base_ref[...].astype(WIDE)
    total = base + change
    low = total.astype(LOW)
    out_ref[...] = low
    if half_refs:
        half = low.shape[1] // 2
        mine = jnp.where(core_ref[0] == 0, low[:, :half], low[:, half:])

        @pl.when(step < 2)
        def _():
            half_refs[0][...] = mine

        @pl.when(step >= 2)
        def _():
            half_refs[1][...] = mine

    valid = lax.broadcasted_iota(jnp.int32, grad.shape, 0) + step * grad.shape[0] < rows

    def column(summed):
        return jnp.sum(jnp.where(valid, summed, 0.0), axis=0, keepdims=True)

    sums = jnp.concatenate(
        [
            column(grad * normed),
            column(grad),
        ]
        + ([] if half_refs else [column(total), column(base)])
        + [jnp.zeros((6 if half_refs else 4, grad.shape[1]), WIDE)],
        axis=0,
    )

    @pl.when(step == 0)
    def _():
        sums_ref[...] = sums

    @pl.when(step > 0)
    def _():
        sums_ref[...] += sums


def norm_back(core, own, other, base, gain, value, halves):
    rows, width = base.shape
    whole = pl.BlockSpec((ROWS, width), lambda i, c: (i, 0))
    row = pl.BlockSpec((1, width), lambda i, c: (0, 0))
    specs, shapes = [], []
    if halves:
        specs = [
            pl.BlockSpec((ROWS, width // 2), lambda i, c: (jnp.minimum(i, 1), 0)),
            pl.BlockSpec((ROWS, width // 2), lambda i, c: (jnp.maximum(i - 2, 0), 0)),
        ]
        shapes = [jax.ShapeDtypeStruct((2 * ROWS, width // 2), LOW)] * 2
    return pl.pallas_call(
        functools.partial(norm_back_kernel, rows=rows),
        grid_spec=pltpu.PrefetchScalarGridSpec(
            num_scalar_prefetch=1,
            grid=(pl.cdiv(rows, ROWS),),
            in_specs=[whole, whole, whole, row, whole],
            out_specs=[whole] + specs + [pl.BlockSpec((8, width), lambda i, c: (0, 0))],
        ),
        out_shape=[jax.ShapeDtypeStruct((rows, width), LOW)]
        + shapes
        + [jax.ShapeDtypeStruct((8, width), WIDE)],
        cost_estimate=cost(8, rows * width * 12),
    )(core.reshape(1), own, other, base, gain, value)


ROWS = 376
SHORT = 8


def take_clip_kernel(group_ref, both_ref, own_ref, *, rows):
    size = own_ref.shape[0]
    place = lax.broadcasted_iota(jnp.int32, (SHORT, own_ref.shape[1]), 0)

    def step(index, carry):
        start = pl.multiple_of(index * SHORT, SHORT)
        both = both_ref[pl.ds(start, SHORT)]
        own = jnp.where(group_ref[0] == 0, both[:, 0, :].astype(WIDE), both[:, 1, :].astype(WIDE))
        real = place + start < rows - pl.program_id(0) * size
        own_ref[pl.ds(start, SHORT), :] = jnp.where(real, own, 0.0).astype(LOW)
        return carry

    lax.fori_loop(0, size // SHORT, step, 0, unroll=False)


def take_clip(group, both, padded, size):
    _, rows, width = both.shape
    return pl.pallas_call(
        functools.partial(take_clip_kernel, rows=rows),
        grid_spec=pltpu.PrefetchScalarGridSpec(
            num_scalar_prefetch=1,
            grid=(pl.cdiv(padded, size),),
            in_specs=[pl.BlockSpec((size, 2, width), lambda i, g: (i, 0, 0))],
            out_specs=pl.BlockSpec((size, width), lambda i, g: (i, 0)),
        ),
        out_shape=jax.ShapeDtypeStruct((padded, width), LOW),
        cost_estimate=cost(9, rows * width * 6),
    )(group.reshape(1), both.transpose(1, 0, 2))


def both_clips_kernel(place_ref, own_ref, direct_ref, across_ref, *refs):
    out_ref = refs[-1]
    group, core = place_ref[0], place_ref[1]

    def step(index, carry):
        span = pl.ds(pl.multiple_of(index * SHORT, SHORT), SHORT)
        own = own_ref[span, :].astype(WIDE)
        direct = direct_ref[span, :].astype(WIDE)
        across = across_ref[span, :].astype(WIDE)
        first = jnp.where(core == 0, direct, across)
        second = jnp.where(core == 0, across, direct)
        other = jnp.concatenate([first, second], axis=1)
        out_ref[span, 0, :] = jnp.where(group == 0, own, other).astype(out_ref.dtype)
        out_ref[span, 1, :] = jnp.where(group == 0, other, own).astype(out_ref.dtype)
        return carry

    lax.fori_loop(0, ROWS // SHORT, step, 0, unroll=False)


def both_clips(own, direct, across, dtype, first, count, previous):
    tensor_index = lax.axis_index("tensor")
    place = jnp.stack([tensor_index // 2, tensor_index % 2])
    rows, width = own.shape
    narrow = pl.BlockSpec((ROWS, width // 2), lambda i, g: (i, 0))
    more = [] if previous is None else [previous]
    return pl.pallas_call(
        both_clips_kernel,
        grid_spec=pltpu.PrefetchScalarGridSpec(
            num_scalar_prefetch=1,
            grid=(count,),
            in_specs=[pl.BlockSpec((ROWS, width), lambda i, g: (i + first, 0)), narrow, narrow]
            + [pl.BlockSpec(memory_space=pl.ANY)] * len(more),
            out_specs=pl.BlockSpec((ROWS, 2, width), lambda i, g: (i + first, 0, 0)),
        ),
        out_shape=jax.ShapeDtypeStruct((rows, 2, width), dtype),
        input_output_aliases={4: 0} if more else {},
        cost_estimate=cost(2 * count, count * ROWS * width * 12),
    )(place, own, direct, across, *more)


def swap_tensor(value, distance):
    size = lax.axis_size("tensor")
    return lax.ppermute(value, "tensor", [(i, i ^ distance) for i in range(size)])


def swap_fsdp(value, distance):
    size = lax.axis_size("fsdp")
    return lax.ppermute(value, "fsdp", [(i, i ^ distance) for i in range(size)])


def swap_both(value):
    width = lax.axis_size("tensor")
    count = lax.axis_size("fsdp") * width
    pairs = [(i, ((i // width) ^ 1) * width + ((i % width) ^ 2)) for i in range(count)]
    return lax.ppermute(value, ("fsdp", "tensor"), pairs)


def after(value, *others):
    return lax.optimization_barrier((value, others))[0]


def spread_far(piece):
    far = lax.axis_size("fsdp") // 2
    return [piece] + [swap_fsdp(piece, 2 * i) for i in range(1, far)]


def spread_near(stack, first=0):
    far = stack.shape[0]
    return [
        (value, tuple((y, 2 * (i + first) + x) for i in range(far)))
        for y, x, value in (
            (0, 0, stack),
            (0, 1, swap_fsdp(stack, 1)),
            (1, 0, swap_tensor(stack, 2)),
            (1, 1, swap_both(stack)),
        )
    ]


def place_kernel(*refs, keys, finish):
    count = len(keys)
    stacks = refs[:count]
    outs, held, sem = refs[count:-2], refs[-2], refs[-1]
    mine = lax.axis_index("fsdp")
    group = lax.axis_index("tensor") // 2
    copies = []
    for stack, names in zip(stacks, keys):
        for i, (y, f) in enumerate(names):
            copy = pltpu.make_async_copy(
                stack.at[i], held.at[group ^ y, mine ^ f], sem.at[len(copies)]
            )
            copy.start()
            copies.append(copy)
    for copy in copies:
        copy.wait()
    finish(held, outs)


def place(parts, finish, out_shapes):
    size = lax.axis_size("fsdp")
    _, rows, columns = parts[0][0].shape
    total = sum(len(ks) for _, ks in parts)
    return pl.pallas_call(
        functools.partial(place_kernel, keys=tuple(ks for _, ks in parts), finish=finish),
        in_specs=[pl.BlockSpec(memory_space=pl.ANY)] * len(parts),
        out_specs=[pl.BlockSpec(memory_space=pltpu.VMEM)] * len(out_shapes),
        out_shape=[jax.ShapeDtypeStruct(*s) for s in out_shapes],
        scratch_shapes=[
            pltpu.VMEM((2, size, rows, columns), LOW),
            pltpu.SemaphoreType.DMA((total,)),
        ],
        cost_estimate=cost(3.5, 4 * size * rows * columns * 2),
    )(*[p for p, _ in parts])


def finish_qkv(held, outs, *, part, head_width, bias_part):
    _, size, _, _ = held.shape
    pairs = 2 * head_width // 128
    for f in range(size):
        a, b = held[0, f, :part], held[1, f, :part]
        wide = []
        for c in range(3):
            span = slice(c * head_width, (c + 1) * head_width)
            wide.append(jnp.concatenate([a[:, span], b[:, span]], axis=1))
        for p in range(pairs):
            for c in range(3):
                outs[0][f * part : (f + 1) * part, (3 * p + c) * 128 : (3 * p + c + 1) * 128] = (
                    wide[c][:, p * 128 : (p + 1) * 128]
                )
    rows = [[held[y, f, part:].astype(WIDE) for f in range(size)] for y in range(2)]
    full = [jnp.concatenate([r[:, :part] for r in rows[y]], axis=1) for y in range(2)]
    for i in range(6):
        outs[2 + i][...] = full[0][i : i + 1]
    outs[8][...] = jnp.concatenate([full[0][6:7], full[1][6:7]], axis=1)
    biases = []
    for c in range(2):
        span = slice(c * bias_part, (c + 1) * bias_part)
        biases.append(jnp.concatenate([r[7:8, span] for y in range(2) for r in rows[y]], axis=1))
    nothing = jnp.zeros((1, 128), WIDE)
    for p in range(pairs):
        span = slice(p * 128, (p + 1) * 128)
        outs[1][:, 3 * p * 128 : (3 * p + 1) * 128] = biases[0][:, span]
        outs[1][:, (3 * p + 1) * 128 : (3 * p + 2) * 128] = nothing
        outs[1][:, (3 * p + 2) * 128 : (3 * p + 3) * 128] = biases[1][:, span]


def finish_up(held, outs, *, unit_width):
    _, size, part, _ = held.shape
    for f in range(size):
        rows = slice(f * part, (f + 1) * part)
        for y in range(2):
            outs[0][rows, y * unit_width : (y + 1) * unit_width] = held[y, f, :, :unit_width]
        outs[1][rows, :] = jnp.concatenate(
            [held[0, f, :, unit_width:], held[1, f, :, unit_width:]], axis=1
        )


def finish_plain(held, outs):
    _, size, part, width = held.shape
    for f in range(size):
        for y in range(2):
            outs[0][f * part : (f + 1) * part, y * width : (y + 1) * width] = held[y, f]


def pick(value, axis, index):
    return lax.dynamic_index_in_dim(value, index, axis, keepdims=False)


def add_low(a, b):
    return (a.astype(WIDE) + b.astype(WIDE)).astype(LOW)


def near_far():
    mine = lax.axis_index("fsdp")
    return mine % 2, mine // 2


def fold_cross(grads):
    low, _ = near_far()
    group = lax.axis_index("tensor") // 2
    size = lax.axis_size("fsdp")
    part, columns = grads.shape[0] // size, grads.shape[1] // 2
    grads = grads.reshape(size // 2, 2, part, 2 * columns)

    def at(y, x):
        span = (size // 2, 1, part, columns)
        return lax.dynamic_slice(grads, (0, x, 0, y * columns), span)[:, 0]

    side = swap_tensor(at(1 - group, low), 2)
    near = swap_fsdp(at(group, 1 - low), 1)
    both = swap_both(at(1 - group, 1 - low))
    return at(group, low), side, near, both


def cross_sum(own, side, near, both):
    total = own.astype(WIDE) + side.astype(WIDE)
    return (total + (near.astype(WIDE) + both.astype(WIDE))).astype(LOW)


def fold_far(grads):
    _, high = near_far()
    axis = grads.ndim - 3
    total = pick(grads, axis, high).astype(WIDE)
    for i in range(1, grads.shape[axis]):
        total = total + swap_fsdp(pick(grads, axis, high ^ i), 2 * i).astype(WIDE)
    return total


VMEM = pl.BlockSpec(memory_space=pltpu.VMEM)
SMEM = pl.BlockSpec(memory_space=pltpu.SMEM)


def small_call(kernel, place, inputs, shapes, scratch):
    return pl.pallas_call(
        kernel,
        in_specs=[SMEM] + [VMEM] * len(inputs),
        out_specs=[VMEM] * len(shapes),
        out_shape=[jax.ShapeDtypeStruct(*s) for s in shapes],
        scratch_shapes=scratch,
        cost_estimate=cost(1.5, 4 << 20),
    )(place, *inputs)


def vector_kernel(place_ref, one_ref, two_ref, up_ref, *refs, part, bias_part, head_width):
    bias_ref, own_ref, sent_ref, held = refs
    pairs = bias_ref.shape[0]
    width = one_ref.shape[1]
    rows = jnp.concatenate(
        [one_ref[0:2, :], two_ref[0:4, :], up_ref[:, :width], up_ref[:, width:]], axis=0
    )
    query = jnp.concatenate([bias_ref[p, 0:1, :] for p in range(pairs)], axis=1)
    value = jnp.concatenate([bias_ref[p, 1:2, :] for p in range(pairs)], axis=1)
    held[...] = jnp.zeros_like(held)
    for f in range(held.shape[0]):
        held[f, 0:8, 0:part] = rows[:, f * part : (f + 1) * part]
        for y in range(2):
            start = y * head_width + f * bias_part
            span = slice(start, start + bias_part)
            held[f, 8 + y : 9 + y, 0 : 2 * bias_part] = jnp.concatenate(
                [query[:, span], value[:, span]], axis=1
            )
    first = place_ref[0] % 2 == 0
    for i in range(own_ref.shape[0]):
        even, odd = held[2 * i], held[2 * i + 1]
        own_ref[i] = jnp.where(first, even, odd).astype(LOW)
        sent_ref[i] = jnp.where(first, odd, even).astype(LOW)


def tail_kernel(place_ref, out_own_ref, out_got_ref, own_ref, got_ref, *outs):
    high = place_ref[0] // 2
    part = out_own_ref.shape[1]
    for i, out in enumerate(outs):
        row = high ^ i
        total = out_own_ref[row].astype(WIDE) + out_got_ref[row].astype(WIDE)
        out[:part, :] = total.astype(LOW)
        for p in range(own_ref.shape[0]):
            total = own_ref[p, row].astype(WIDE) + got_ref[p, row].astype(WIDE)
            out[(1 + p) * part : (2 + p) * part, :] = total.astype(LOW)


def sum_of(refs):
    total = refs[0][...].astype(WIDE)
    for ref in refs[1:]:
        total = total + ref[...].astype(WIDE)
    return total


def heads_kernel(place_ref, *refs, far, part, head_width):
    tail = sum_of(refs[:far])
    vectors = sum_of(refs[far : 2 * far])
    own_ref, sent_ref = refs[2 * far :]
    first = place_ref[1] == 0
    pairs = tail.shape[0] // part - 1
    blocks = [tail[:part, :]]
    for c in range(3):
        span = slice(c * 128, (c + 1) * 128)
        blocks.append(
            jnp.concatenate(
                [tail[(1 + p) * part : (2 + p) * part, span] for p in range(pairs)], axis=1
            )
        )
    for k, block in enumerate(blocks):
        rows = slice(k * part, (k + 1) * part)
        low, high = block[:, :head_width], block[:, head_width:]
        own_ref[rows, :] = jnp.where(first, low, high).astype(LOW)
        sent_ref[rows, :] = jnp.where(first, high, low).astype(LOW)
    own_ref[4 * part :, :] = jnp.zeros((8, head_width), LOW)
    sent_ref[4 * part :, :] = jnp.zeros((8, head_width), LOW)
    low, high = [
        jnp.concatenate([vectors[:6], vectors[6 + y : 7 + y], vectors[8 + y : 9 + y]], axis=0)
        for y in range(2)
    ]
    own_ref[4 * part :, 0:128] = jnp.where(first, low, high).astype(LOW)
    sent_ref[4 * part :, 0:128] = jnp.where(first, high, low).astype(LOW)


def final_kernel(place_ref, own_ref, got_ref, *outs, part, bias_part):
    total = own_ref[...].astype(WIDE) + got_ref[...].astype(WIDE)
    out_ref, qkv_ref, one_ref, two_ref, *rows_refs, bias_ref = outs
    out_ref[...] = total[:part, :].T
    for c in range(3):
        qkv_ref[c] = total[(1 + c) * part : (2 + c) * part, :]
    vectors = total[4 * part :, :part]
    one_ref[...] = vectors[0:2]
    two_ref[...] = vectors[2:4]
    for i, ref in enumerate(rows_refs):
        ref[...] = vectors[4 + i : 5 + i]
    bias_ref[...] = jnp.concatenate(
        [vectors[7:8, :bias_part], vectors[7:8, bias_part : 2 * bias_part]], axis=0
    )


def local(
    frames_in, cotangent, ln_first, w_qkv, b_qv, w_out, b_out, ln_second, w_fc1, b_fc1, w_fc2, b_fc2
):
    _, frame_count, model_width = frames_in.shape
    size = lax.axis_size("fsdp")
    part = w_qkv.shape[0]
    head_width = w_qkv.shape[2]
    unit_width = w_fc1.shape[1]
    bias_part = b_qv.shape[1]
    group = lax.axis_index("tensor") // 2
    core = lax.axis_index("tensor") % 2
    mine = lax.axis_index("fsdp")
    far = size // 2

    vectors = jnp.concatenate(
        [
            ln_first,
            ln_second,
            b_out[None],
            b_fc2[None],
            b_fc1[None],
            jnp.pad(b_qv.reshape(1, -1), ((0, 0), (0, part - 2 * bias_part))),
        ],
        axis=0,
    )
    vectors = jnp.pad(vectors, ((0, 0), (0, 3 * head_width - part)))
    qkv_piece = jnp.concatenate([w_qkv.reshape(part, 3 * head_width), vectors], axis=0)
    qkv_own = spread_near(qkv_piece[None])
    qkv_far = jnp.stack(spread_far(qkv_piece)[1:])
    padded = padded_rows(frame_count)
    frames_low = take_clip(group, frames_in, padded, padded // 4)
    qkv_parts = qkv_own + spread_near(qkv_far, 1)
    up_far = spread_far(jnp.concatenate([w_fc1, w_out.T], axis=1))
    down_far = spread_far(w_fc2.T)
    grad_low = take_clip(after(group, frames_low, qkv_far), cotangent, frame_count, ROWS)
    row = ((1, model_width), WIDE)
    (
        qkv_full, qkv_bias, gain_one, shift_one, gain_two, shift_two, out_bias, down_bias, up_bias
    ) = place(
        qkv_parts,
        functools.partial(finish_qkv, part=part, head_width=head_width, bias_part=bias_part),
        [((model_width, 6 * head_width), LOW), ((1, 6 * head_width), WIDE)]
        + [row] * 6
        + [((1, 2 * unit_width), WIDE)],
    )

    up_parts = spread_near(jnp.stack(after(up_far, qkv_full)))
    token_rows = after(frames_low, qkv_far).astype(WIDE)
    first_low = layer_norm(token_rows, gain_one, shift_one)[0].astype(LOW)
    qkv = (jnp.dot(first_low, qkv_full, preferred_element_type=WIDE) + qkv_bias).astype(LOW)
    down_parts = spread_near(jnp.stack(after(down_far, qkv)))
    attn_low, log_total = attend(qkv, frame_count)

    up_all, out_full = place(
        up_parts,
        functools.partial(finish_up, unit_width=unit_width),
        [((model_width, 2 * unit_width), LOW), ((model_width, 2 * head_width), LOW)],
    )
    attn_terms = lax.dot_general(attn_low, out_full, NT, preferred_element_type=WIDE).astype(LOW)
    attn_other = swap_tensor(attn_terms, 1)
    second_low, middle = norm_two(
        frames_low, attn_terms, attn_other, gain_two, shift_two, out_bias
    )

    pre_act = jnp.dot(second_low, up_all, preferred_element_type=WIDE) + up_bias
    below = 0.5 * (1.0 + lax.erf(pre_act * 0.7071067811865476))
    slope = below + pre_act * jnp.exp(-0.5 * pre_act * pre_act) * 0.3989422804014327
    act, slope = lax.optimization_barrier(((pre_act * below).astype(LOW), slope.astype(LOW)))
    grad_down = lax.dot_general(grad_low, act, TN, preferred_element_type=WIDE).astype(LOW)
    down_cross = fold_cross(grad_down)

    (stack, keys), *others = down_parts
    (down_all,) = place(
        [(after(stack, grad_down), keys)] + others,
        finish_plain,
        [((model_width, 2 * unit_width), LOW)],
    )
    grad_pre = jnp.dot(grad_low, down_all, preferred_element_type=WIDE) * slope.astype(WIDE)
    grad_up_bias = jnp.sum(grad_pre, axis=0, keepdims=True)
    grad_pre = grad_pre.astype(LOW)
    second_terms = lax.dot_general(grad_pre, up_all, NT, preferred_element_type=WIDE).astype(LOW)
    second_other = swap_tensor(second_terms, 1)
    grad_up = lax.dot_general(
        after(second_low, second_terms), grad_pre, TN, preferred_element_type=WIDE
    ).astype(LOW)
    up_cross = fold_cross(grad_up)
    down_terms = lax.dot_general(
        after(act, grad_up), down_all, NT, preferred_element_type=WIDE
    ).astype(LOW)
    down_other = swap_tensor(down_terms, 1)
    result = middle.astype(WIDE) + (down_terms.astype(WIDE) + down_other.astype(WIDE)) + down_bias
    result = result.astype(LOW)

    middle_low, sums_two = norm_back(
        core, second_terms, second_other, grad_low, gain_two, middle, False
    )
    grad_attn = jnp.dot(middle_low, out_full, preferred_element_type=WIDE).astype(LOW)
    grad_out = lax.dot_general(middle_low, attn_low, TN, preferred_element_type=WIDE)
    low, _ = near_far()
    grad_out = grad_out.astype(LOW).reshape(far, 2, part, 2 * head_width)
    out_own, out_sent = pick(grad_out, 1, low), pick(grad_out, 1, 1 - low)
    out_got = swap_fsdp(out_sent, 1)

    half = model_width // 2
    out_direct = swap_tensor(lax.dynamic_slice_in_dim(result, core * half, half, axis=1), 2)
    out_across = swap_tensor(out_direct, 1)

    pairs = 2 * head_width // 128
    grads, bias_sums, own, sent = attend_back(
        low, qkv, after(grad_attn, out_sent, result), attn_low, log_total, first_low
    )
    got = swap_fsdp(sent, 1)
    units = jnp.stack(
        [cross_sum(*after(c, grads)) for c in (down_cross, up_cross)]
    )
    place_now = jnp.stack([mine, group])

    first_terms = merge(after(grads, units), qkv_full)
    tail = small_call(
        tail_kernel,
        place_now,
        [out_own, out_got, own, after(got, first_terms)],
        [(((1 + pairs) * part, 384), LOW)] * far,
        [],
    )
    tail = [tail[0]] + [swap_fsdp(tail[i], 2 * i) for i in range(1, far)]
    first_other = swap_tensor(first_terms, 1)
    rows_low, *halves, sums_one = norm_back(
        core, first_terms, first_other, middle_low, gain_one, frames_low, True
    )
    direct = [swap_tensor(h, 2) for h in halves]
    across = [swap_tensor(d, 1) for d in direct]

    own, sent = small_call(
        functools.partial(
            vector_kernel, part=part, bias_part=bias_part, head_width=head_width
        ),
        place_now,
        [sums_one, sums_two, grad_up_bias, bias_sums],
        [((far, 16, 128), LOW)] * 2,
        [pltpu.VMEM((size, 16, 128), WIDE)],
    )
    vectors = add_low(own, swap_fsdp(sent, 1))
    _, high = near_far()
    vectors = [pick(vectors, 0, high ^ i) for i in range(far)]
    vectors = vectors[:1] + [swap_fsdp(vectors[i], 2 * i) for i in range(1, far)]
    own, sent = small_call(
        functools.partial(heads_kernel, far=far, part=part, head_width=head_width),
        place_now,
        tail + vectors,
        [((4 * part + 8, head_width), LOW)] * 2,
        [],
    )
    row = ((1, part), WIDE)
    grad_out, grad_qkv, grad_one, grad_two, row_out, row_down, row_up, grad_bias = small_call(
        functools.partial(final_kernel, part=part, bias_part=bias_part),
        place_now,
        [own, swap_tensor(sent, 2)],
        [((head_width, part), WIDE), ((3, part, head_width), WIDE), ((2, part), WIDE)]
        + [((2, part), WIDE), row, row, row, ((2, bias_part), WIDE)],
        [],
    )

    blocks = pl.cdiv(frame_count, ROWS)
    frames_out = both_clips(result, out_direct, out_across, LOW, 0, blocks, None)
    grad_frames = None
    for i in range(2):
        grad_frames = both_clips(rows_low, direct[i], across[i], WIDE, 2 * i, 2, grad_frames)

    units = fold_far(units)
    grad_down, grad_up = units[0].T, units[1]

    return (
        frames_out.transpose(1, 0, 2),
        grad_frames.transpose(1, 0, 2),
        grad_one,
        grad_qkv.transpose(1, 0, 2),
        grad_bias,
        grad_out,
        row_out[0],
        grad_two,
        grad_up,
        row_up[0],
        grad_down,
        row_down[0],
    )


def solution(mesh):
    in_specs = (
        P("fsdp", None, None),
        P("fsdp", None, None),
        P(None, "fsdp"),
        P("fsdp", None, "tensor"),
        P(None, ("tensor", "fsdp")),
        P("tensor", "fsdp"),
        P("fsdp"),
        P(None, "fsdp"),
        P("fsdp", "tensor"),
        P(("tensor", "fsdp")),
        P("tensor", "fsdp"),
        P("fsdp"),
    )
    out_specs = (
        P("fsdp", None, None),
        P("fsdp", None, None),
        P(None, "fsdp"),
        P("fsdp", None, "tensor"),
        P(None, ("tensor", "fsdp")),
        P("tensor", "fsdp"),
        P("fsdp"),
        P(None, "fsdp"),
        P("fsdp", "tensor"),
        P(("tensor", "fsdp")),
        P("tensor", "fsdp"),
        P("fsdp"),
    )
    return jax.shard_map(local, mesh=mesh, in_specs=in_specs, out_specs=out_specs, check_vma=False)
```

```python
import functools

import jax
import jax.numpy as jnp
from jax import lax
from jax.experimental import pallas as pl
from jax.experimental.pallas import tpu as pltpu
from jax.sharding import PartitionSpec as P


HEAD_DIM = 64
EPSILON = 1e-05
LOW = jnp.bfloat16
WIDE = jnp.float32
NEGATIVE = -1e30
NT = (((1,), (1,)), ((), ()))
TN = (((0,), (0,)), ((), ()))


def layer_norm(values, norm_gain, norm_shift):
    centre = jnp.mean(values, axis=-1, keepdims=True)
    centred = values - centre
    inverse = lax.rsqrt(jnp.mean(centred * centred, axis=-1, keepdims=True) + EPSILON)
    normed = centred * inverse
    return (normed * norm_gain + norm_shift, normed, inverse)


def cost(microseconds, size):
    return pl.CostEstimate(
        flops=int(microseconds * 1e9), transcendentals=0, bytes_accessed=int(size)
    )


def padded_rows(count):
    return -(-count // 512) * 512


def attend_kernel(q_ref, k_ref, v_ref, o_ref, l_ref, q_all, v_all, *, rows, block):
    padded = q_all.shape[0]
    q_all[...] = q_ref[...] * LOW(HEAD_DIM**-0.5)
    v_all[:, :128] = v_ref[...]
    v_all[:, 128:] = jnp.ones((padded, 128), LOW)
    valid = lax.broadcasted_iota(jnp.int32, (block, 256), 1) < rows - (padded - 256)
    upper = lax.broadcasted_iota(jnp.int32, (block, 128), 1) >= HEAD_DIM
    for step in range(padded // block):
        start = step * block
        parts = []
        for head in range(2):
            q_head = jnp.where(upper == (head == 1), q_all[start : start + block, :], LOW(0))
            scores = lax.dot_general(q_head, k_ref[...], NT, preferred_element_type=WIDE)
            scores = jnp.concatenate(
                [
                    scores[:, : padded - 256],
                    jnp.where(valid, scores[:, padded - 256 :], NEGATIVE),
                ],
                axis=1,
            )
            highest = jnp.max(scores, axis=1, keepdims=True)
            weights = jnp.exp(scores - highest).astype(LOW)
            blended = jnp.dot(weights, v_all[...], preferred_element_type=WIDE)
            total = blended[:, 128:]
            parts.append(blended[:, :128] * (1.0 / total))
            log_total = (highest + jnp.log(total)).T
            l_ref[head, :, start : start + block] = log_total[0:8, :]
        o_ref[start : start + block, :] = jnp.where(upper, parts[1], parts[0]).astype(LOW)


def attend(qkv, rows):
    padded, width = qkv.shape
    pairs = width // 3 // 128

    def column(which):
        return pl.BlockSpec((padded, 128), lambda p: (0, 3 * p + which))

    return pl.pallas_call(
        functools.partial(attend_kernel, rows=rows, block=512),
        grid=(pairs,),
        in_specs=[column(0), column(1), column(2)],
        out_specs=[
            pl.BlockSpec((padded, 128), lambda p: (0, p)),
            pl.BlockSpec((2, 8, padded), lambda p: (p, 0, 0)),
        ],
        out_shape=[
            jax.ShapeDtypeStruct((rows, width // 3), LOW),
            jax.ShapeDtypeStruct((2 * pairs, 8, padded), WIDE),
        ],
        scratch_shapes=[pltpu.VMEM((padded, 128), LOW), pltpu.VMEM((padded, 256), LOW)],
        cost_estimate=cost(22, padded * width * 3),
        name="fa",
    )(qkv, qkv, qkv)


def attend_back_kernel(
    near_ref, q_ref, k_ref, v_ref, g_ref, o_ref, l_ref, h_ref, d_ref, db_ref, own_ref, sent_ref,
    q_all, k_all, g_all, dq_turned, centre_all, *, rows, block,
):
    padded = k_all.shape[0]
    fill = jnp.zeros((padded - rows, 128), LOW)

    def pad(value):
        return jnp.concatenate([value, fill], axis=0)

    upper = lax.broadcasted_iota(jnp.int32, (padded, 128), 1) >= HEAD_DIM
    upper8 = lax.broadcasted_iota(jnp.int32, (8, 128), 1) >= HEAD_DIM
    upper_block = lax.broadcasted_iota(jnp.int32, (block, 128), 1) >= HEAD_DIM
    row_block = lax.broadcasted_iota(jnp.int32, (block, 128), 0)
    scale = HEAD_DIM**-0.5
    keys = k_ref[...]
    k_all[...] = jnp.concatenate([keys[:rows], keys[: padded - rows]], axis=0)
    q_full = q_ref[...] * LOW(scale)
    g_full = pad(g_ref[...])
    product = g_full.astype(WIDE) * pad(o_ref[...]).astype(WIDE)
    coarse = product.astype(LOW)
    fine = (product - coarse.astype(WIDE)).astype(LOW)
    for head in range(2):
        mine = upper == (head == 1)
        q_all[head] = jnp.where(mine, q_full, LOW(0))
        g_all[head] = jnp.where(mine, g_full, LOW(0))
        ones = jnp.where(upper8 == (head == 1), 1.0, 0.0).astype(LOW)
        centre_all[head] = lax.dot_general(
            ones, coarse, NT, preferred_element_type=WIDE
        ) + lax.dot_general(ones, fine, NT, preferred_element_type=WIDE)
    dq_turned[...] = jnp.zeros_like(dq_turned)

    def step(index, value_bias):
        span = pl.ds(pl.multiple_of(index * block, block), block)
        keys, values = k_all[span, :], v_ref[span, :]
        real = row_block < rows - index * block
        grad_values = grad_keys = grad_query = None
        for head in range(2):
            scores = lax.dot_general(keys, q_all[head], NT, preferred_element_type=WIDE)
            chances = jnp.exp(scores - l_ref[head, 0:1, :])
            grad_weights = lax.dot_general(
                values, g_all[head], NT, preferred_element_type=WIDE
            )
            grad_scores = (chances * (grad_weights - centre_all[head, 0:1, :])).astype(LOW)
            from_values = jnp.dot(
                chances.astype(LOW), g_all[head], preferred_element_type=WIDE
            )
            from_keys = jnp.dot(grad_scores, q_all[head], preferred_element_type=WIDE)
            keys_head = jnp.where(real & (upper_block == (head == 1)), keys, LOW(0))
            from_query = jnp.dot(keys_head.T, grad_scores, preferred_element_type=WIDE)
            if head == 0:
                grad_values, grad_keys, grad_query = from_values, from_keys, from_query
            else:
                grad_values = grad_values + from_values
                grad_keys = grad_keys + from_keys
                grad_query = grad_query + from_query
        dq_turned[...] += grad_query
        grad_values = jnp.where(real, grad_values, 0.0)
        d_ref[span, 128:256] = jnp.where(real, grad_keys, 0.0).astype(LOW)
        d_ref[span, 256:384] = grad_values.astype(LOW)
        return value_bias + jnp.sum(grad_values, axis=0, keepdims=True)

    value_bias = lax.fori_loop(
        0, padded // block, step, jnp.zeros((1, 128), WIDE)
    )
    turned = dq_turned[...] * scale
    grad_query = turned.T
    d_ref[:, 0:128] = grad_query.astype(LOW)
    db_ref[0:1, :] = jnp.sum(grad_query, axis=0, keepdims=True)
    db_ref[1:2, :] = value_bias
    turned = jnp.concatenate(
        [turned.astype(LOW), d_ref[:, 128:256].T, d_ref[:, 256:384].T], axis=0
    )
    weight = jnp.dot(turned, h_ref[...], preferred_element_type=WIDE).T
    part = own_ref.shape[1]
    first = near_ref[0] == 0
    for i in range(own_ref.shape[0]):
        even = weight[2 * i * part : (2 * i + 1) * part, :]
        odd = weight[(2 * i + 1) * part : (2 * i + 2) * part, :]
        own_ref[i] = jnp.where(first, even, odd).astype(LOW)
        sent_ref[i] = jnp.where(first, odd, even).astype(LOW)


def attend_back(near, qkv, grad_out, blended, log_total, normed):
    rows, total = grad_out.shape
    pairs = total // 128
    padded, width = normed.shape
    size = lax.axis_size("fsdp")

    def column(which):
        return pl.BlockSpec((padded, 128), lambda p, n: (0, 3 * p + which))

    single = pl.BlockSpec((rows, 128), lambda p, n: (0, p))
    half = (size // 2, width // size, 384)
    slices = pl.BlockSpec((None, *half), lambda p, n: (p, 0, 0, 0))
    return pl.pallas_call(
        functools.partial(attend_back_kernel, rows=rows, block=512),
        grid_spec=pltpu.PrefetchScalarGridSpec(
            num_scalar_prefetch=1,
            grid=(pairs,),
            in_specs=[
                column(0),
                column(1),
                column(2),
                single,
                single,
                pl.BlockSpec((2, 8, padded), lambda p, n: (p, 0, 0)),
                pl.BlockSpec((padded, width), lambda p, n: (0, 0)),
            ],
            out_specs=[
                pl.BlockSpec((padded, 384), lambda p, n: (0, p)),
                pl.BlockSpec((None, 8, 128), lambda p, n: (p, 0, 0)),
                slices,
                slices,
            ],
            scratch_shapes=[
                pltpu.VMEM((2, padded, 128), LOW),
                pltpu.VMEM((padded, 128), LOW),
                pltpu.VMEM((2, padded, 128), LOW),
                pltpu.VMEM((128, padded), WIDE),
                pltpu.VMEM((2, 8, padded), WIDE),
            ],
        ),
        out_shape=[
            jax.ShapeDtypeStruct((rows, 3 * total), LOW),
            jax.ShapeDtypeStruct((pairs, 8, 128), WIDE),
            jax.ShapeDtypeStruct((pairs, *half), LOW),
            jax.ShapeDtypeStruct((pairs, *half), LOW),
        ],
        cost_estimate=cost(45, rows * 384 * 16),
        name="b0",
    )(near.reshape(1), qkv, qkv, qkv, grad_out, blended, log_total, normed)


def norm_two_kernel(frames_ref, own_ref, other_ref, gain_ref, shift_ref, bias_ref, out_ref, mid_ref):
    terms = own_ref[...].astype(WIDE) + other_ref[...].astype(WIDE)
    value = frames_ref[...].astype(WIDE) + terms + bias_ref[...]
    mid_ref[...] = value.astype(LOW)
    out_ref[...] = layer_norm(value, gain_ref[...], shift_ref[...])[0].astype(LOW)


def norm_two(frames, own, other, gain, shift, bias):
    rows, width = own.shape
    whole = pl.BlockSpec((ROWS, width), lambda i: (i, 0))
    row = pl.BlockSpec((1, width), lambda i: (0, 0))
    return pl.pallas_call(
        norm_two_kernel,
        grid=(pl.cdiv(rows, ROWS),),
        in_specs=[whole] * 3 + [row] * 3,
        out_specs=[whole, whole],
        out_shape=[jax.ShapeDtypeStruct((rows, width), LOW)] * 2,
        cost_estimate=cost(6, rows * width * 10),
        name="n2",
    )(frames, own, other, gain, shift, bias)


def norm_back_kernel(
    core_ref, own_ref, other_ref, base_ref, gain_ref, value_ref, out_ref, *refs, rows
):
    *half_refs, sums_ref = refs
    step = pl.program_id(0)
    grad = own_ref[...].astype(WIDE) + other_ref[...].astype(WIDE)
    value = value_ref[...].astype(WIDE)
    centred = value - jnp.mean(value, axis=-1, keepdims=True)
    inverse = lax.rsqrt(jnp.mean(centred * centred, axis=-1, keepdims=True) + EPSILON)
    normed = centred * inverse
    scaled = grad * gain_ref[...]
    change = inverse * (
        scaled
        - jnp.mean(scaled, axis=-1, keepdims=True)
        - normed * jnp.mean(scaled * normed, axis=-1, keepdims=True)
    )
    base = base_ref[...].astype(WIDE)
    total = base + change
    low = total.astype(LOW)
    out_ref[...] = low
    if half_refs:
        half = low.shape[1] // 2
        mine = jnp.where(core_ref[0] == 0, low[:, :half], low[:, half:])

        @pl.when(step < 2)
        def _():
            half_refs[0][...] = mine

        @pl.when(step >= 2)
        def _():
            half_refs[1][...] = mine

    valid = lax.broadcasted_iota(jnp.int32, grad.shape, 0) + step * grad.shape[0] < rows

    def column(summed):
        return jnp.sum(jnp.where(valid, summed, 0.0), axis=0, keepdims=True)

    sums = jnp.concatenate(
        [
            column(grad * normed),
            column(grad),
        ]
        + ([] if half_refs else [column(total), column(base)])
        + [jnp.zeros((6 if half_refs else 4, grad.shape[1]), WIDE)],
        axis=0,
    )

    @pl.when(step == 0)
    def _():
        sums_ref[...] = sums

    @pl.when(step > 0)
    def _():
        sums_ref[...] += sums


def norm_back(core, own, other, base, gain, value, halves):
    rows, width = base.shape
    whole = pl.BlockSpec((ROWS, width), lambda i, c: (i, 0))
    row = pl.BlockSpec((1, width), lambda i, c: (0, 0))
    specs, shapes = [], []
    if halves:
        specs = [
            pl.BlockSpec((ROWS, width // 2), lambda i, c: (jnp.minimum(i, 1), 0)),
            pl.BlockSpec((ROWS, width // 2), lambda i, c: (jnp.maximum(i - 2, 0), 0)),
        ]
        shapes = [jax.ShapeDtypeStruct((2 * ROWS, width // 2), LOW)] * 2
    return pl.pallas_call(
        functools.partial(norm_back_kernel, rows=rows),
        grid_spec=pltpu.PrefetchScalarGridSpec(
            num_scalar_prefetch=1,
            grid=(pl.cdiv(rows, ROWS),),
            in_specs=[whole, whole, whole, row, whole],
            out_specs=[whole] + specs + [pl.BlockSpec((8, width), lambda i, c: (0, 0))],
        ),
        out_shape=[jax.ShapeDtypeStruct((rows, width), LOW)]
        + shapes
        + [jax.ShapeDtypeStruct((8, width), WIDE)],
        cost_estimate=cost(8, rows * width * 12),
    )(core.reshape(1), own, other, base, gain, value)


ROWS = 376
SHORT = 8


def take_clip_kernel(group_ref, both_ref, own_ref, *, rows):
    size = own_ref.shape[0]
    place = lax.broadcasted_iota(jnp.int32, (SHORT, own_ref.shape[1]), 0)

    def step(index, carry):
        start = pl.multiple_of(index * SHORT, SHORT)
        both = both_ref[pl.ds(start, SHORT)]
        own = jnp.where(group_ref[0] == 0, both[:, 0, :].astype(WIDE), both[:, 1, :].astype(WIDE))
        real = place + start < rows - pl.program_id(0) * size
        own_ref[pl.ds(start, SHORT), :] = jnp.where(real, own, 0.0).astype(LOW)
        return carry

    lax.fori_loop(0, size // SHORT, step, 0, unroll=False)


def take_clip(group, both, padded, size):
    _, rows, width = both.shape
    return pl.pallas_call(
        functools.partial(take_clip_kernel, rows=rows),
        grid_spec=pltpu.PrefetchScalarGridSpec(
            num_scalar_prefetch=1,
            grid=(pl.cdiv(padded, size),),
            in_specs=[pl.BlockSpec((size, 2, width), lambda i, g: (i, 0, 0))],
            out_specs=pl.BlockSpec((size, width), lambda i, g: (i, 0)),
        ),
        out_shape=jax.ShapeDtypeStruct((padded, width), LOW),
        cost_estimate=cost(9, rows * width * 6),
    )(group.reshape(1), both.transpose(1, 0, 2))


def both_clips_kernel(place_ref, own_ref, direct_ref, across_ref, *refs):
    out_ref = refs[-1]
    group, core = place_ref[0], place_ref[1]

    def step(index, carry):
        span = pl.ds(pl.multiple_of(index * SHORT, SHORT), SHORT)
        own = own_ref[span, :].astype(WIDE)
        direct = direct_ref[span, :].astype(WIDE)
        across = across_ref[span, :].astype(WIDE)
        first = jnp.where(core == 0, direct, across)
        second = jnp.where(core == 0, across, direct)
        other = jnp.concatenate([first, second], axis=1)
        out_ref[span, 0, :] = jnp.where(group == 0, own, other).astype(out_ref.dtype)
        out_ref[span, 1, :] = jnp.where(group == 0, other, own).astype(out_ref.dtype)
        return carry

    lax.fori_loop(0, ROWS // SHORT, step, 0, unroll=False)


def both_clips(own, direct, across, dtype, first, count, previous):
    tensor_index = lax.axis_index("tensor")
    place = jnp.stack([tensor_index // 2, tensor_index % 2])
    rows, width = own.shape
    narrow = pl.BlockSpec((ROWS, width // 2), lambda i, g: (i, 0))
    more = [] if previous is None else [previous]
    return pl.pallas_call(
        both_clips_kernel,
        grid_spec=pltpu.PrefetchScalarGridSpec(
            num_scalar_prefetch=1,
            grid=(count,),
            in_specs=[pl.BlockSpec((ROWS, width), lambda i, g: (i + first, 0)), narrow, narrow]
            + [pl.BlockSpec(memory_space=pl.ANY)] * len(more),
            out_specs=pl.BlockSpec((ROWS, 2, width), lambda i, g: (i + first, 0, 0)),
        ),
        out_shape=jax.ShapeDtypeStruct((rows, 2, width), dtype),
        input_output_aliases={4: 0} if more else {},
        cost_estimate=cost(2 * count, count * ROWS * width * 12),
    )(place, own, direct, across, *more)


def swap_tensor(value, distance):
    size = lax.axis_size("tensor")
    return lax.ppermute(value, "tensor", [(i, i ^ distance) for i in range(size)])


def swap_fsdp(value, distance):
    size = lax.axis_size("fsdp")
    return lax.ppermute(value, "fsdp", [(i, i ^ distance) for i in range(size)])


def swap_both(value):
    width = lax.axis_size("tensor")
    count = lax.axis_size("fsdp") * width
    pairs = [(i, ((i // width) ^ 1) * width + ((i % width) ^ 2)) for i in range(count)]
    return lax.ppermute(value, ("fsdp", "tensor"), pairs)


def after(value, *others):
    return lax.optimization_barrier((value, others))[0]


def spread_far(piece):
    far = lax.axis_size("fsdp") // 2
    return [piece] + [swap_fsdp(piece, 2 * i) for i in range(1, far)]


def spread_near(stack, first=0):
    far = stack.shape[0]
    return [
        (value, tuple((y, 2 * (i + first) + x) for i in range(far)))
        for y, x, value in (
            (0, 0, stack),
            (0, 1, swap_fsdp(stack, 1)),
            (1, 0, swap_tensor(stack, 2)),
            (1, 1, swap_both(stack)),
        )
    ]


def place_kernel(*refs, keys, finish):
    count = len(keys)
    stacks = refs[:count]
    outs, held, sem = refs[count:-2], refs[-2], refs[-1]
    mine = lax.axis_index("fsdp")
    group = lax.axis_index("tensor") // 2
    copies = []
    for stack, names in zip(stacks, keys):
        for i, (y, f) in enumerate(names):
            copy = pltpu.make_async_copy(
                stack.at[i], held.at[group ^ y, mine ^ f], sem.at[len(copies)]
            )
            copy.start()
            copies.append(copy)
    for copy in copies:
        copy.wait()
    finish(held, outs)


def place(parts, finish, out_shapes):
    size = lax.axis_size("fsdp")
    _, rows, columns = parts[0][0].shape
    total = sum(len(ks) for _, ks in parts)
    return pl.pallas_call(
        functools.partial(place_kernel, keys=tuple(ks for _, ks in parts), finish=finish),
        in_specs=[pl.BlockSpec(memory_space=pl.ANY)] * len(parts),
        out_specs=[pl.BlockSpec(memory_space=pltpu.VMEM)] * len(out_shapes),
        out_shape=[jax.ShapeDtypeStruct(*s) for s in out_shapes],
        scratch_shapes=[
            pltpu.VMEM((2, size, rows, columns), LOW),
            pltpu.SemaphoreType.DMA((total,)),
        ],
        cost_estimate=cost(3.5, 4 * size * rows * columns * 2),
    )(*[p for p, _ in parts])


def finish_qkv(held, outs, *, part, head_width, bias_part):
    _, size, _, _ = held.shape
    pairs = 2 * head_width // 128
    for f in range(size):
        a, b = held[0, f, :part], held[1, f, :part]
        wide = []
        for c in range(3):
            span = slice(c * head_width, (c + 1) * head_width)
            wide.append(jnp.concatenate([a[:, span], b[:, span]], axis=1))
        for p in range(pairs):
            for c in range(3):
                outs[0][f * part : (f + 1) * part, (3 * p + c) * 128 : (3 * p + c + 1) * 128] = (
                    wide[c][:, p * 128 : (p + 1) * 128]
                )
    rows = [[held[y, f, part:].astype(WIDE) for f in range(size)] for y in range(2)]
    full = [jnp.concatenate([r[:, :part] for r in rows[y]], axis=1) for y in range(2)]
    for i in range(6):
        outs[2 + i][...] = full[0][i : i + 1]
    outs[8][...] = jnp.concatenate([full[0][6:7], full[1][6:7]], axis=1)
    biases = []
    for c in range(2):
        span = slice(c * bias_part, (c + 1) * bias_part)
        biases.append(jnp.concatenate([r[7:8, span] for y in range(2) for r in rows[y]], axis=1))
    nothing = jnp.zeros((1, 128), WIDE)
    for p in range(pairs):
        span = slice(p * 128, (p + 1) * 128)
        outs[1][:, 3 * p * 128 : (3 * p + 1) * 128] = biases[0][:, span]
        outs[1][:, (3 * p + 1) * 128 : (3 * p + 2) * 128] = nothing
        outs[1][:, (3 * p + 2) * 128 : (3 * p + 3) * 128] = biases[1][:, span]


def finish_up(held, outs, *, unit_width):
    _, size, part, _ = held.shape
    for f in range(size):
        for y in range(2):
            outs[0][f * part : (f + 1) * part, y * unit_width : (y + 1) * unit_width] = held[
                y, f, :, :unit_width
            ]


def finish_out(held, outs, *, unit_width):
    _, size, part, _ = held.shape
    for f in range(size):
        outs[0][f * part : (f + 1) * part, :] = jnp.concatenate(
            [held[0, f, :, unit_width:], held[1, f, :, unit_width:]], axis=1
        )


def finish_plain(held, outs):
    _, size, part, width = held.shape
    for f in range(size):
        for y in range(2):
            outs[0][f * part : (f + 1) * part, y * width : (y + 1) * width] = held[y, f]


def pick(value, axis, index):
    return lax.dynamic_index_in_dim(value, index, axis, keepdims=False)


def add_low(a, b):
    return (a.astype(WIDE) + b.astype(WIDE)).astype(LOW)


def near_far():
    mine = lax.axis_index("fsdp")
    return mine % 2, mine // 2


def fold_cross(grads):
    low, _ = near_far()
    group = lax.axis_index("tensor") // 2
    size = lax.axis_size("fsdp")
    part, columns = grads.shape[0] // size, grads.shape[1] // 2
    grads = grads.reshape(size // 2, 2, part, 2 * columns)

    def at(y, x):
        span = (size // 2, 1, part, columns)
        return lax.dynamic_slice(grads, (0, x, 0, y * columns), span)[:, 0]

    side = swap_tensor(at(1 - group, low), 2)
    near = swap_fsdp(at(group, 1 - low), 1)
    both = swap_both(at(1 - group, 1 - low))
    return at(group, low), side, near, both


def cross_sum(own, side, near, both):
    total = own.astype(WIDE) + side.astype(WIDE)
    return (total + (near.astype(WIDE) + both.astype(WIDE))).astype(LOW)


def fold_far(grads):
    _, high = near_far()
    axis = grads.ndim - 3
    total = pick(grads, axis, high).astype(WIDE)
    for i in range(1, grads.shape[axis]):
        total = total + swap_fsdp(pick(grads, axis, high ^ i), 2 * i).astype(WIDE)
    return total


VMEM = pl.BlockSpec(memory_space=pltpu.VMEM)
SMEM = pl.BlockSpec(memory_space=pltpu.SMEM)


def small_call(kernel, place, inputs, shapes, scratch):
    return pl.pallas_call(
        kernel,
        in_specs=[SMEM] + [VMEM] * len(inputs),
        out_specs=[VMEM] * len(shapes),
        out_shape=[jax.ShapeDtypeStruct(*s) for s in shapes],
        scratch_shapes=scratch,
        cost_estimate=cost(1.5, 4 << 20),
    )(place, *inputs)


def vector_kernel(place_ref, one_ref, two_ref, up_ref, *refs, part, bias_part, head_width):
    bias_ref, own_ref, sent_ref, held = refs
    pairs = bias_ref.shape[0]
    width = one_ref.shape[1]
    rows = jnp.concatenate(
        [one_ref[0:2, :], two_ref[0:4, :], up_ref[:, :width], up_ref[:, width:]], axis=0
    )
    query = jnp.concatenate([bias_ref[p, 0:1, :] for p in range(pairs)], axis=1)
    value = jnp.concatenate([bias_ref[p, 1:2, :] for p in range(pairs)], axis=1)
    held[...] = jnp.zeros_like(held)
    for f in range(held.shape[0]):
        held[f, 0:8, 0:part] = rows[:, f * part : (f + 1) * part]
        for y in range(2):
            start = y * head_width + f * bias_part
            span = slice(start, start + bias_part)
            held[f, 8 + y : 9 + y, 0 : 2 * bias_part] = jnp.concatenate(
                [query[:, span], value[:, span]], axis=1
            )
    first = place_ref[0] % 2 == 0
    for i in range(own_ref.shape[0]):
        even, odd = held[2 * i], held[2 * i + 1]
        own_ref[i] = jnp.where(first, even, odd).astype(LOW)
        sent_ref[i] = jnp.where(first, odd, even).astype(LOW)


def tail_kernel(place_ref, out_own_ref, out_got_ref, own_ref, got_ref, *outs):
    high = place_ref[0] // 2
    part = out_own_ref.shape[1]
    for i, out in enumerate(outs):
        row = high ^ i
        total = out_own_ref[row].astype(WIDE) + out_got_ref[row].astype(WIDE)
        out[:part, :] = total.astype(LOW)
        for p in range(own_ref.shape[0]):
            total = own_ref[p, row].astype(WIDE) + got_ref[p, row].astype(WIDE)
            out[(1 + p) * part : (2 + p) * part, :] = total.astype(LOW)


def sum_of(refs):
    total = refs[0][...].astype(WIDE)
    for ref in refs[1:]:
        total = total + ref[...].astype(WIDE)
    return total


def heads_kernel(place_ref, *refs, far, part, head_width):
    tail = sum_of(refs[:far])
    vectors = sum_of(refs[far : 2 * far])
    own_ref, sent_ref = refs[2 * far :]
    first = place_ref[1] == 0
    pairs = tail.shape[0] // part - 1
    blocks = [tail[:part, :]]
    for c in range(3):
        span = slice(c * 128, (c + 1) * 128)
        blocks.append(
            jnp.concatenate(
                [tail[(1 + p) * part : (2 + p) * part, span] for p in range(pairs)], axis=1
            )
        )
    for k, block in enumerate(blocks):
        rows = slice(k * part, (k + 1) * part)
        low, high = block[:, :head_width], block[:, head_width:]
        own_ref[rows, :] = jnp.where(first, low, high).astype(LOW)
        sent_ref[rows, :] = jnp.where(first, high, low).astype(LOW)
    own_ref[4 * part :, :] = jnp.zeros((8, head_width), LOW)
    sent_ref[4 * part :, :] = jnp.zeros((8, head_width), LOW)
    low, high = [
        jnp.concatenate([vectors[:6], vectors[6 + y : 7 + y], vectors[8 + y : 9 + y]], axis=0)
        for y in range(2)
    ]
    own_ref[4 * part :, 0:128] = jnp.where(first, low, high).astype(LOW)
    sent_ref[4 * part :, 0:128] = jnp.where(first, high, low).astype(LOW)


def final_kernel(place_ref, own_ref, got_ref, *outs, part, bias_part):
    total = own_ref[...].astype(WIDE) + got_ref[...].astype(WIDE)
    out_ref, qkv_ref, one_ref, two_ref, *rows_refs, bias_ref = outs
    out_ref[...] = total[:part, :].T
    for c in range(3):
        qkv_ref[c] = total[(1 + c) * part : (2 + c) * part, :]
    vectors = total[4 * part :, :part]
    one_ref[...] = vectors[0:2]
    two_ref[...] = vectors[2:4]
    for i, ref in enumerate(rows_refs):
        ref[...] = vectors[4 + i : 5 + i]
    bias_ref[...] = jnp.concatenate(
        [vectors[7:8, :bias_part], vectors[7:8, bias_part : 2 * bias_part]], axis=0
    )


def local(
    frames_in, cotangent, ln_first, w_qkv, b_qv, w_out, b_out, ln_second, w_fc1, b_fc1, w_fc2, b_fc2
):
    _, frame_count, model_width = frames_in.shape
    size = lax.axis_size("fsdp")
    part = w_qkv.shape[0]
    head_width = w_qkv.shape[2]
    unit_width = w_fc1.shape[1]
    bias_part = b_qv.shape[1]
    group = lax.axis_index("tensor") // 2
    core = lax.axis_index("tensor") % 2
    mine = lax.axis_index("fsdp")
    far = size // 2

    vectors = jnp.concatenate(
        [
            ln_first,
            ln_second,
            b_out[None],
            b_fc2[None],
            b_fc1[None],
            jnp.pad(b_qv.reshape(1, -1), ((0, 0), (0, part - 2 * bias_part))),
        ],
        axis=0,
    )
    vectors = jnp.pad(vectors, ((0, 0), (0, 3 * head_width - part)))
    qkv_piece = jnp.concatenate([w_qkv.reshape(part, 3 * head_width), vectors], axis=0)
    qkv_own = spread_near(qkv_piece[None])
    qkv_far = jnp.stack(spread_far(qkv_piece)[1:])
    padded = padded_rows(frame_count)
    frames_low = take_clip(group, frames_in, padded, padded // 4)
    qkv_parts = qkv_own + spread_near(qkv_far, 1)
    up_far = spread_far(jnp.concatenate([w_fc1, w_out.T], axis=1))
    down_far = spread_far(w_fc2.T)
    grad_low = take_clip(after(group, frames_low, qkv_far), cotangent, frame_count, ROWS)
    row = ((1, model_width), WIDE)
    (
        qkv_full, qkv_bias, gain_one, shift_one, gain_two, shift_two, out_bias, down_bias, up_bias
    ) = place(
        qkv_parts,
        functools.partial(finish_qkv, part=part, head_width=head_width, bias_part=bias_part),
        [((model_width, 6 * head_width), LOW), ((1, 6 * head_width), WIDE)]
        + [row] * 6
        + [((1, 2 * unit_width), WIDE)],
    )

    up_parts = spread_near(jnp.stack(after(up_far, qkv_full)))
    token_rows = after(frames_low, qkv_far).astype(WIDE)
    first_low = layer_norm(token_rows, gain_one, shift_one)[0].astype(LOW)
    qkv = (jnp.dot(first_low, qkv_full, preferred_element_type=WIDE) + qkv_bias).astype(LOW)
    down_parts = spread_near(jnp.stack(after(down_far, qkv)))
    attn_low, log_total = attend(qkv, frame_count)

    (out_full,) = place(
        up_parts,
        functools.partial(finish_out, unit_width=unit_width),
        [((model_width, 2 * head_width), LOW)],
    )
    attn_terms = lax.dot_general(attn_low, out_full, NT, preferred_element_type=WIDE).astype(LOW)
    (stack, keys), *others = up_parts
    (up_all,) = place(
        [(after(stack, attn_terms), keys)] + others,
        functools.partial(finish_up, unit_width=unit_width),
        [((model_width, 2 * unit_width), LOW)],
    )
    attn_other = swap_tensor(attn_terms, 1)
    second_low, middle = norm_two(
        frames_low, attn_terms, attn_other, gain_two, shift_two, out_bias
    )

    pre_act = jnp.dot(second_low, up_all, preferred_element_type=WIDE) + up_bias
    below = 0.5 * (1.0 + lax.erf(pre_act * 0.7071067811865476))
    slope = below + pre_act * jnp.exp(-0.5 * pre_act * pre_act) * 0.3989422804014327
    act, slope = lax.optimization_barrier(((pre_act * below).astype(LOW), slope.astype(LOW)))
    grad_down = lax.dot_general(grad_low, act, TN, preferred_element_type=WIDE).astype(LOW)
    down_cross = fold_cross(grad_down)

    (stack, keys), *others = down_parts
    (down_all,) = place(
        [(after(stack, grad_down), keys)] + others,
        finish_plain,
        [((model_width, 2 * unit_width), LOW)],
    )
    grad_pre = jnp.dot(grad_low, down_all, preferred_element_type=WIDE) * slope.astype(WIDE)
    grad_up_bias = jnp.sum(grad_pre, axis=0, keepdims=True)
    grad_pre = grad_pre.astype(LOW)
    second_terms = lax.dot_general(grad_pre, up_all, NT, preferred_element_type=WIDE).astype(LOW)
    second_other = swap_tensor(second_terms, 1)
    grad_up = lax.dot_general(
        after(second_low, second_terms), grad_pre, TN, preferred_element_type=WIDE
    ).astype(LOW)
    up_cross = fold_cross(grad_up)
    down_terms = lax.dot_general(
        after(act, grad_up), down_all, NT, preferred_element_type=WIDE
    ).astype(LOW)
    down_other = swap_tensor(down_terms, 1)
    result = middle.astype(WIDE) + (down_terms.astype(WIDE) + down_other.astype(WIDE)) + down_bias
    result = result.astype(LOW)

    middle_low, sums_two = norm_back(
        core, second_terms, second_other, grad_low, gain_two, middle, False
    )
    grad_attn = jnp.dot(middle_low, out_full, preferred_element_type=WIDE).astype(LOW)
    grad_out = lax.dot_general(middle_low, attn_low, TN, preferred_element_type=WIDE)
    low, _ = near_far()
    grad_out = grad_out.astype(LOW).reshape(far, 2, part, 2 * head_width)
    out_own, out_sent = pick(grad_out, 1, low), pick(grad_out, 1, 1 - low)
    out_got = swap_fsdp(out_sent, 1)

    half = model_width // 2
    out_direct = swap_tensor(lax.dynamic_slice_in_dim(result, core * half, half, axis=1), 2)
    out_across = swap_tensor(out_direct, 1)

    grad_down = fold_far(cross_sum(*after(down_cross, middle_low))).T

    pairs = 2 * head_width // 128
    grads, bias_sums, own, sent = attend_back(
        low, qkv, after(grad_attn, out_sent, result), attn_low, log_total, first_low
    )
    got = swap_fsdp(sent, 1)
    place_now = jnp.stack([mine, group])

    first_terms = lax.dot_general(
        grads, qkv_full, NT, preferred_element_type=WIDE
    ).astype(LOW)
    first_other = swap_tensor(first_terms, 1)
    grad_up = fold_far(cross_sum(*after(up_cross, first_terms)))
    rows_low, *halves, sums_one = norm_back(
        core, first_terms, first_other, middle_low, gain_one, frames_low, True
    )
    direct = [swap_tensor(h, 2) for h in halves]
    across = [swap_tensor(d, 1) for d in direct]

    tail = small_call(
        tail_kernel,
        place_now,
        [out_own, out_got, own, after(got, rows_low)],
        [(((1 + pairs) * part, 384), LOW)] * far,
        [],
    )
    tail = [tail[0]] + [swap_fsdp(tail[i], 2 * i) for i in range(1, far)]

    own, sent = small_call(
        functools.partial(
            vector_kernel, part=part, bias_part=bias_part, head_width=head_width
        ),
        place_now,
        [sums_one, sums_two, grad_up_bias, bias_sums],
        [((far, 16, 128), LOW)] * 2,
        [pltpu.VMEM((size, 16, 128), WIDE)],
    )
    vectors = add_low(own, swap_fsdp(sent, 1))
    _, high = near_far()
    vectors = [pick(vectors, 0, high ^ i) for i in range(far)]
    vectors = vectors[:1] + [swap_fsdp(vectors[i], 2 * i) for i in range(1, far)]
    own, sent = small_call(
        functools.partial(heads_kernel, far=far, part=part, head_width=head_width),
        place_now,
        tail + vectors,
        [((4 * part + 8, head_width), LOW)] * 2,
        [],
    )
    row = ((1, part), WIDE)
    grad_out, grad_qkv, grad_one, grad_two, row_out, row_down, row_up, grad_bias = small_call(
        functools.partial(final_kernel, part=part, bias_part=bias_part),
        place_now,
        [own, swap_tensor(sent, 2)],
        [((head_width, part), WIDE), ((3, part, head_width), WIDE), ((2, part), WIDE)]
        + [((2, part), WIDE), row, row, row, ((2, bias_part), WIDE)],
        [],
    )

    blocks = pl.cdiv(frame_count, ROWS)
    frames_out = both_clips(result, out_direct, out_across, LOW, 0, blocks, None)
    grad_frames = None
    for i in range(2):
        grad_frames = both_clips(rows_low, direct[i], across[i], WIDE, 2 * i, 2, grad_frames)


    return (
        frames_out.transpose(1, 0, 2),
        grad_frames.transpose(1, 0, 2),
        grad_one,
        grad_qkv.transpose(1, 0, 2),
        grad_bias,
        grad_out,
        row_out[0],
        grad_two,
        grad_up,
        row_up[0],
        grad_down,
        row_down[0],
    )


def solution(mesh):
    in_specs = (
        P("fsdp", None, None),
        P("fsdp", None, None),
        P(None, "fsdp"),
        P("fsdp", None, "tensor"),
        P(None, ("tensor", "fsdp")),
        P("tensor", "fsdp"),
        P("fsdp"),
        P(None, "fsdp"),
        P("fsdp", "tensor"),
        P(("tensor", "fsdp")),
        P("tensor", "fsdp"),
        P("fsdp"),
    )
    out_specs = (
        P("fsdp", None, None),
        P("fsdp", None, None),
        P(None, "fsdp"),
        P("fsdp", None, "tensor"),
        P(None, ("tensor", "fsdp")),
        P("tensor", "fsdp"),
        P("fsdp"),
        P(None, "fsdp"),
        P("fsdp", "tensor"),
        P(("tensor", "fsdp")),
        P("tensor", "fsdp"),
        P("fsdp"),
    )
    return jax.shard_map(local, mesh=mesh, in_specs=in_specs, out_specs=out_specs, check_vma=False)
```
